32 devices in a mesh: seq: 4 (over y, x), fsdp: 8 (over z, core).
Axes of the slice: x: 2, y: 2, z: 4, core: 2. Of those that a mesh axis runs over, the one named last changes fastest.
Arguments:
- tokens: bfloat16 [8, 1024, 1536], P('fsdp', 'seq'), may hold values from -6 to 6
- mixing_weight: bfloat16 [1536, 2560], P(('seq', 'fsdp')), may hold values from -0.21875 to 0.21875
- output_weight: bfloat16 [1536, 1536], P(('seq', 'fsdp')), may hold values from -0.625 to 0.625
- norm_gains: bfloat16 [1536, 2], P(('seq', 'fsdp')), may hold values from 0.099609375 to 1.8984375
- expert_gate: bfloat16 [1536, 40, 512], P('fsdp', 'seq'), may hold values from -0.15625 to 0.15625
- expert_up: bfloat16 [1536, 40, 512], P('fsdp', 'seq'), may hold values from -0.15625 to 0.15625
- expert_down: bfloat16 [1536, 40, 512], P('fsdp', 'seq'), may hold values from -1.25 to 1.25
- gate_logits: float32 [8, 1024, 8], P('fsdp'), may hold values from -3 to 3
- routes: int32 [8, 1024, 8], P('fsdp'), may hold values from 0 to 39, all different within a row
- fill_order: int32 [8, 1024], P('fsdp'), may hold values from 0 to 1023, each once within a row
- cotangent: bfloat16 [8, 1024, 1536], P('fsdp', 'seq'), may hold values from -6 to 6
Outputs:
- layer_output: bfloat16 [8, 1024, 1536], P('fsdp', 'seq')
- tokens_gradient: float32 [8, 1024, 1536], P('fsdp', 'seq')
- mixing_gradient: float32 [1536, 2560], P(('seq', 'fsdp'))
- output_gradient: float32 [1536, 1536], P(('seq', 'fsdp'))
- gains_gradient: float32 [1536, 2], P(('seq', 'fsdp'))
- gate_gradient: float32 [1536, 40, 512], P('fsdp', 'seq')
- up_gradient: float32 [1536, 40, 512], P('fsdp', 'seq')
- down_gradient: float32 [1536, 40, 512], P('fsdp', 'seq')
- logits_gradient: float32 [8, 1024, 8], P('fsdp', 'seq')
The draws below stay inside these ranges and needn't reach their ends.
Inputs may be any that keep to these rules, and one draw needn't show every extreme that they name: `routes`: each token names 8 different experts. `fill_order`: each sequence's row holds each token index of that sequence once.
All inputs are finite; a program needn't handle non-finite values.
Results may differ from the reference program's by a relative error of at most 0.017.
The reference program's roundings to bfloat16 on the way count: a program that leaves them out, or rounds other values in their place, can miss the bound.
Values may be sent and summed in bfloat16 or wider, within the bound.
A program may use at most 256 MiB of HBM per device.

```python
import math
import jax
import jax.numpy as jnp
from jax import lax

D = 1536
HEADS = 24
KV_HEADS = 8
HEAD_DIM = 64
FF = 512
EXPERTS = 40
TOP = 8
QBLK = 512
SEQS = 8
LEN = 1024
CAP = 205
QKV_WIDTH = 2560


def shard_levels(rng, dims, split, least, largest):
    def one(position, shards_of):
        heights = jax.random.uniform(jax.random.fold_in(jax.random.fold_in(rng, 6), position), (shards_of,), jnp.float32, least / len(split), largest / len(split))
        return jnp.repeat(jnp.exp(heights), dims[position] // shards_of).reshape((-1,) + (1,) * (len(dims) - position - 1))

    factor_of = one(*split[0])
    for cut in split[1:]:
        factor_of = factor_of * one(*cut)
    return factor_of


def choose_distinct(stream_key, rows, number_of, top, lift):
    sequence = jax.random.permutation(jax.random.fold_in(stream_key, 1), number_of)
    boost = sequence
    for power in range(3):
        boost = boost * boost // number_of
    boost = boost * lift // number_of
    chance = jax.random.randint(jax.random.fold_in(stream_key, 2), (rows, number_of), 0, 4096) + boost
    sure = jax.random.permutation(jax.random.fold_in(stream_key, 3), rows)[jnp.arange(number_of) % rows]
    chance = jnp.where(jnp.arange(rows)[:, None] == sure[None, :], 1 << 14, chance)
    merit = chance * number_of + jnp.arange(number_of)
    return lax.top_k(merit.astype(jnp.int32), top)[1].astype(jnp.int32)


def scatter_about(rng, extent, width, most, pieces=(), kind=jnp.bfloat16):
    gain = shard_levels(rng, extent, pieces, -0.22, 0.18) if pieces else 1.0
    values = jax.random.normal(rng, extent, jnp.float32) * width * gain
    return jnp.minimum(jnp.maximum(values, -most), most).astype(kind)


def setup_inputs(seed: int = 0) -> dict:
    arg_keys = jax.random.split(jax.random.key(seed), 12)
    tokens = scatter_about(arg_keys[0], (SEQS, LEN, D), 1.0, 6.0, ((0, 8), (1, 4)))
    mixing_weight = scatter_about(arg_keys[1], (D, QKV_WIDTH), (D // 2) ** -0.5, 0.21875, ((0, 32),))
    output_weight = scatter_about(arg_keys[2], (D, HEADS * HEAD_DIM), (D // 16) ** -0.5, 0.625, ((0, 32),))
    norm_gains = jnp.clip(1.0 + 0.18 * jax.random.normal(arg_keys[3], (D, 2), jnp.float32), 0.099609375, 1.8984375).astype(jnp.bfloat16)
    expert_gate = scatter_about(arg_keys[4], (D, EXPERTS, FF), D ** -0.5, 0.15625, ((0, 8), (1, 4)))
    expert_up = scatter_about(arg_keys[5], (D, EXPERTS, FF), D ** -0.5, 0.15625, ((0, 8), (1, 4)))
    expert_down = scatter_about(arg_keys[6], (D, EXPERTS, FF), (FF // 25) ** -0.5, 1.25, ((0, 8), (1, 4)))
    gate_logits = scatter_about(arg_keys[7], (SEQS, LEN, TOP), 0.5, 3.0, ((0, 8),), jnp.float32)
    routes = choose_distinct(arg_keys[8], SEQS * LEN, EXPERTS, TOP, 1638).reshape((SEQS, LEN, TOP))
    fill_order = jax.vmap(lambda own: jax.random.permutation(own, LEN))(jax.random.split(arg_keys[9], SEQS)).reshape((SEQS, LEN)).astype(jnp.int32)
    cotangent = scatter_about(arg_keys[10], (SEQS, LEN, D), 1.0, 6.0, ((0, 8), (1, 4)))
    return {"tokens": tokens, "mixing_weight": mixing_weight, "output_weight": output_weight, "norm_gains": norm_gains, "expert_gate": expert_gate, "expert_up": expert_up, "expert_down": expert_down, "gate_logits": gate_logits, "routes": routes, "fill_order": fill_order, "cotangent": cotangent}


epsilon = 1e-05
rope_base = 10000.0
highest = lax.Precision.HIGHEST

@jax.custom_vjp
def low(v):
    return lax.optimization_barrier(v.astype(jnp.bfloat16)).astype(jnp.float32)

@jax.custom_vjp
def low_back(v):
    return v

def low_keep(v):
    return (low(v), None)

def low_pass(kept, grad):
    return (grad,)

def back_keep(v):
    return (v, None)

def back_low(kept, grad):
    return (low(grad),)
low.defvjp(low_keep, low_pass)
low_back.defvjp(back_keep, back_low)

def norm_apply(values, gain_row):
    return values * lax.rsqrt(lax.optimization_barrier(jnp.mean(values * values, axis=-1, keepdims=True)) + epsilon) * gain_row

def rotary_tables(positions):
    half_width = HEAD_DIM // 2
    frequency = rope_base ** (-2.0 * jnp.arange(half_width, dtype=jnp.float32) / HEAD_DIM)
    angles = positions.astype(jnp.float32)[:, None] * frequency[None, :]
    cos_table = jnp.cos(angles)
    sin_table = jnp.sin(angles)
    return (jnp.concatenate([cos_table, cos_table], 1), jnp.concatenate([sin_table, sin_table], 1))

def rotate(values, cos_table, sin_table):
    half_width = values.shape[-1] // 2
    turned = jnp.concatenate([-values[..., half_width:], values[..., :half_width]], -1)
    return values * cos_table[:, None, :] + turned * sin_table[:, None, :]

def softmax_last(logit_rows):
    row_max = lax.optimization_barrier(jnp.max(logit_rows, axis=-1, keepdims=True))
    exponent = jnp.exp(logit_rows - row_max)
    return exponent / lax.optimization_barrier(jnp.sum(exponent, axis=-1, keepdims=True))

def build_slots(route_rows, order_rows, expert_ids, capacity):
    length = route_rows.shape[0]
    chosen = route_rows[:, :, None] == expert_ids[None, None, :]
    hit_count = lax.optimization_barrier(jnp.sum(chosen.astype(jnp.int32), axis=1)).astype(jnp.int32)
    ordered = hit_count[order_rows]
    before = (jnp.cumsum(ordered, axis=0) - ordered).astype(jnp.int32)
    slot_rank = jnp.zeros_like(before).at[order_rows].set(before)
    kept_mask = (hit_count > 0) & (slot_rank < capacity)
    slot_place = jnp.where(kept_mask, slot_rank, capacity).astype(jnp.int32)
    expert_cols = jnp.broadcast_to(jnp.arange(expert_ids.shape[0], dtype=jnp.int32)[None, :], slot_place.shape)
    token_ids = jnp.broadcast_to(jnp.arange(length, dtype=jnp.int32)[:, None], slot_place.shape)
    table_full = jnp.full((expert_ids.shape[0], capacity + 1), length, jnp.int32)
    table_full = table_full.at[expert_cols, slot_place].set(token_ids)
    return (chosen, table_full[:, :capacity])

def attention(queries, keys, values):
    length = queries.shape[0]
    group_size = HEADS // KV_HEADS
    grouped = queries.reshape(length // QBLK, QBLK, KV_HEADS, group_size, HEAD_DIM)
    starts = jnp.arange(length // QBLK, dtype=jnp.int32) * QBLK
    score_scale = 1.0 / math.sqrt(HEAD_DIM)
    key_pos = jnp.arange(length, dtype=jnp.int32)

    def block(block_items):
        row_block, first_row = block_items
        scores = jnp.einsum('bkgd,tkd->kgbt', row_block, keys, precision=highest) * score_scale
        scores = low_back(scores)
        allowed = (first_row + jnp.arange(QBLK, dtype=jnp.int32))[:, None] >= key_pos[None, :]
        scores = jnp.where(allowed, scores, -jnp.inf)
        soft_weights = low(softmax_last(scores))
        return jnp.einsum('kgbt,tkd->bkgd', soft_weights, values, precision=highest)
    outputs = lax.map(jax.checkpoint(block), (grouped, starts))
    return outputs.reshape(length, HEADS * HEAD_DIM)

def sequence_layer(seq_tokens, seq_logits, seq_routes, seq_order, mixing, exit_weight, gain_pair, gate_matrix, up_matrix, down_matrix):
    length = seq_tokens.shape[0]
    query_width = HEADS * HEAD_DIM
    key_width = KV_HEADS * HEAD_DIM
    normed = low(norm_apply(seq_tokens, gain_pair[:, 0]))
    projected = jnp.dot(normed, mixing, precision=highest)
    cos_table, sin_table = rotary_tables(jnp.arange(length, dtype=jnp.int32))
    queries = low_back(projected[:, :query_width]).reshape(length, HEADS, HEAD_DIM)
    queries = low(low_back(rotate(queries, cos_table, sin_table)))
    keys = low_back(projected[:, query_width:query_width + key_width]).reshape(length, KV_HEADS, HEAD_DIM)
    keys = low(low_back(rotate(keys, cos_table, sin_table)))
    values = low(low_back(projected[:, query_width + key_width:])).reshape(length, KV_HEADS, HEAD_DIM)
    attended = low(low_back(attention(queries, keys, values)))
    attn_out = low_back(jnp.dot(attended, exit_weight.T, precision=highest))
    hidden = seq_tokens + attn_out
    normed_two = low(norm_apply(hidden, gain_pair[:, 1]))
    gating = softmax_last(seq_logits)
    expert_ids = jnp.arange(EXPERTS, dtype=jnp.int32)
    chosen, slot_table = build_slots(seq_routes, seq_order, expert_ids, CAP)
    token_weight = lax.optimization_barrier(jnp.sum(gating[:, :, None] * chosen.astype(jnp.float32), axis=1))
    padded_weight = jnp.concatenate([token_weight, jnp.zeros((1, EXPERTS), jnp.float32)], 0)
    slot_weight = padded_weight[slot_table, expert_ids[:, None]]
    padded_rows = jnp.concatenate([normed_two, jnp.zeros((1, D), jnp.float32)], 0)
    slot_rows = padded_rows[slot_table]
    gate_pre = low_back(jnp.einsum('ecd,def->ecf', slot_rows, gate_matrix, precision=highest))
    up_pre = low_back(jnp.einsum('ecd,def->ecf', slot_rows, up_matrix, precision=highest))
    mid = low(gate_pre * jax.nn.sigmoid(gate_pre) * up_pre)
    expert_out = low_back(jnp.einsum('ecf,def->ecd', mid, down_matrix, precision=highest))
    moe = jnp.zeros((length + 1, D), jnp.float32).at[slot_table].add(expert_out * slot_weight[:, :, None])[:length]
    return hidden + moe

def reference(tokens, mixing_weight, output_weight, norm_gains, expert_gate, expert_up, expert_down, gate_logits, routes, fill_order, cotangent):

    def forward(token_f, mixing_f, output_f, gains_f, gate_f, up_f, down_f, logits_f):

        def one_sequence(carried, block_items):
            seq_tokens, seq_logits, seq_routes, seq_order = block_items
            result = sequence_layer(seq_tokens, seq_logits, seq_routes, seq_order, mixing_f, output_f, gains_f, gate_f, up_f, down_f)
            return (carried, result)
        unused, outputs = lax.scan(one_sequence, jnp.zeros((), jnp.float32), (token_f, logits_f, routes, fill_order))
        return outputs
    floats = (tokens.astype(jnp.float32), mixing_weight.astype(jnp.float32), output_weight.astype(jnp.float32), norm_gains.astype(jnp.float32), expert_gate.astype(jnp.float32), expert_up.astype(jnp.float32), expert_down.astype(jnp.float32), gate_logits.astype(jnp.float32))
    result, pullback = jax.vjp(forward, *floats)
    gradients = pullback(cotangent.astype(jnp.float32))
    return (result.astype(jnp.bfloat16), gradients[0], gradients[1], gradients[2], gradients[3], gradients[4], gradients[5], gradients[6], gradients[7])
```

```python
import functools
import math

import jax
import jax.numpy as jnp
import numpy as np
from jax import lax
from jax.experimental import pallas as pl
from jax.experimental.pallas import tpu as pltpu
from jax.sharding import Mesh
from jax.sharding import PartitionSpec as P

D = 1536
HEADS = 24
KV_HEADS = 8
HEAD_DIM = 64
FF = 512
EXPERTS = 40
TOP = 8
QROWS = 256
PAD = 128

epsilon = 1e-05
rope_base = 10000.0
single = jnp.float32
narrow = jnp.bfloat16


def rotary_tables(positions):
    half_width = HEAD_DIM // 2
    frequency = rope_base ** (-2.0 * jnp.arange(half_width, dtype=single) / HEAD_DIM)
    angles = positions.astype(single)[:, None] * frequency[None, :]
    cos_table = jnp.cos(angles)
    sin_table = jnp.sin(angles)
    return (jnp.concatenate([cos_table, cos_table], 1), jnp.concatenate([sin_table, sin_table], 1))


def softmax_last(logit_rows):
    row_max = jnp.max(logit_rows, axis=-1, keepdims=True)
    exponent = jnp.exp(logit_rows - row_max)
    return exponent / jnp.sum(exponent, axis=-1, keepdims=True)


def swap(value, axis, step, size):
    return lax.ppermute(value, axis, [(i, i ^ step) for i in range(size)])


def dot(left, right, left_dim, right_dim):
    return lax.dot_general(
        left, right, (((left_dim,), (right_dim,)), ((), ())), preferred_element_type=single
    )


def rope(values, cos_row, sin_row):
    width = values.shape[-1]
    lane = lax.broadcasted_iota(jnp.int32, values.shape, 1) % HEAD_DIM
    turned = jnp.where(
        lane < HEAD_DIM // 2,
        -pltpu.roll(values, width - HEAD_DIM // 2, 1),
        pltpu.roll(values, HEAD_DIM // 2, 1),
    )
    return values * cos_row + turned * sin_row


def rope_back(values, cos_row, sin_row):
    width = values.shape[-1]
    lane = lax.broadcasted_iota(jnp.int32, values.shape, 1) % HEAD_DIM
    scaled = values * sin_row
    turned = jnp.where(
        lane < HEAD_DIM // 2,
        pltpu.roll(scaled, width - HEAD_DIM // 2, 1),
        -pltpu.roll(scaled, HEAD_DIM // 2, 1),
    )
    return values * cos_row + turned


def wide(table, width):
    return jnp.concatenate([table] * (width // table.shape[1]), axis=1)


def stacked(ref, at, kv, size):
    group_size = HEADS // KV_HEADS
    return jnp.concatenate(
        [
            ref[at : at + size, (kv * group_size + g) * HEAD_DIM : (kv * group_size + g + 1) * HEAD_DIM]
            for g in range(group_size)
        ],
        axis=0,
    )


def key_scores(keys, queries, at, size):
    scores = dot(keys, queries, 1, 1) * (1.0 / math.sqrt(HEAD_DIM))
    shape = scores.shape
    key_at = lax.broadcasted_iota(jnp.int32, shape, 0)
    query_at = lax.broadcasted_iota(jnp.int32, shape, 1) % size + at
    return jnp.where(key_at <= query_at, scores, -jnp.inf)


def attention_body(
    tok_ref, mix_ref, exit_ref, gain_ref, cos_ref, sin_ref,
    normed_ref, q_ref, k_ref, v_ref, att_ref, log_ref, part_ref,
):
    seq_len = tok_ref.shape[0]
    size = QROWS
    for at in range(0, seq_len, size):
        project_rows(
            at, size, tok_ref[at : at + size], mix_ref[...], gain_ref[0:1],
            cos_ref, sin_ref, normed_ref, q_ref, k_ref, v_ref,
        )
    attend_rows(q_ref, k_ref, v_ref, att_ref, log_ref)
    for at in range(0, seq_len, size):
        part_ref[at : at + size] = dot(att_ref[at : at + size], exit_ref[...], 1, 1).astype(narrow)


def attention_call(tokens_all, mixing_own, exit_own, gains, cos_table, sin_table):
    seq_len = tokens_all.shape[0]
    q_width = exit_own.shape[1]
    k_width = (mixing_own.shape[1] - q_width) // 2
    group_size = HEADS // KV_HEADS
    blocks = k_width // HEAD_DIM * (seq_len // QROWS)
    shape = jax.ShapeDtypeStruct
    return pl.pallas_call(
        attention_body,
        out_shape=[
            shape((seq_len, D), narrow),
            shape((seq_len, q_width), narrow),
            shape((seq_len, k_width), narrow),
            shape((seq_len, k_width), narrow),
            shape((seq_len, q_width), narrow),
            shape((blocks, 1, group_size * QROWS), single),
            shape((seq_len, D), narrow),
        ],
        cost_estimate=pl.CostEstimate(
            flops=2 * seq_len * D * (mixing_own.shape[1] + q_width) + 4 * seq_len**2 * q_width * 4,
            bytes_accessed=seq_len * D * 6, transcendentals=0,
        ),
        name="attention_forward",
    )(tokens_all, mixing_own, exit_own, gains, cos_table, sin_table)


def attention_back_body(
    grad_ref, exit_ref, mix_ref, q_ref, k_ref, v_ref, log_ref, tok_ref, cos_ref, sin_ref,
    pg_ref, part_ref, gain_ref,
    out_grad, keys_sum, values_sum,
):
    seq_len = tok_ref.shape[0]
    size = QROWS
    q_width, k_width = q_ref.shape[1], k_ref.shape[1]
    group_size = HEADS // KV_HEADS
    scale = 1.0 / math.sqrt(HEAD_DIM)
    for at in range(0, seq_len, size):
        out_grad[at : at + size] = dot(grad_ref[at : at + size], exit_ref[...], 1, 0).astype(narrow)
    for kv in range(k_width // HEAD_DIM):
        lanes = slice(kv * HEAD_DIM, (kv + 1) * HEAD_DIM)
        keys_sum[...] = jnp.zeros_like(keys_sum)
        values_sum[...] = jnp.zeros_like(values_sum)
        for block in range(seq_len // size):
            at = block * size
            end = at + size
            queries = stacked(q_ref, at, kv, size)
            grads = stacked(out_grad, at, kv, size)
            keys, values = k_ref[:end, lanes], v_ref[:end, lanes]
            scores = key_scores(keys, queries, at, size)
            soft = jnp.exp(scores - log_ref[kv * (seq_len // size) + block])
            values_sum[:end] += dot(soft.astype(narrow), grads, 1, 0)
            soft_grad = dot(values, grads, 1, 1)
            delta = jnp.sum(soft * soft_grad, axis=0, keepdims=True)
            scores_grad = (soft * (soft_grad - delta)).astype(narrow)
            keys_sum[:end] += dot(scores_grad, queries, 1, 0) * scale
            query_grad = dot(keys, scores_grad, 0, 0) * scale
            for g in range(group_size):
                head = kv * group_size + g
                pg_ref[at:end, head * HEAD_DIM : (head + 1) * HEAD_DIM] = (
                    query_grad[:, g * size : (g + 1) * size].T.astype(narrow)
                )
        first = q_width + kv * HEAD_DIM
        pg_ref[:, first : first + HEAD_DIM] = keys_sum[...].astype(narrow)
        first += k_width
        pg_ref[:, first : first + HEAD_DIM] = values_sum[...].astype(narrow)
    gain = jnp.zeros((1, D), single)
    turned = q_width + k_width
    for at in range(0, seq_len, size):
        rows = slice(at, at + size)
        cos_row, sin_row = cos_ref[rows], sin_ref[rows]
        pg_ref[rows, :turned] = rope_back(
            pg_ref[rows, :turned].astype(single), wide(cos_row, turned), wide(sin_row, turned)
        ).astype(narrow)
        normed_part = dot(pg_ref[rows], mix_ref[...], 1, 1)
        part_ref[rows] = normed_part.astype(narrow)
        values = tok_ref[rows].astype(single)
        inverse = lax.rsqrt(jnp.mean(values * values, axis=-1, keepdims=True) + epsilon)
        gain = gain + jnp.sum(normed_part * (values * inverse), axis=0, keepdims=True)
    gain_ref[...] = gain


def attention_back_call(grads, exit_own, mixing_own, q, k, v, logs, tokens_all, cos_table, sin_table):
    seq_len = tokens_all.shape[0]
    shape = jax.ShapeDtypeStruct
    return pl.pallas_call(
        attention_back_body,
        out_shape=[
            shape((seq_len, mixing_own.shape[1]), narrow),
            shape((seq_len, D), narrow),
            shape((1, D), single),
        ],
        scratch_shapes=[
            pltpu.VMEM(q.shape, narrow),
            pltpu.VMEM((seq_len, HEAD_DIM), single),
            pltpu.VMEM((seq_len, HEAD_DIM), single),
        ],
        cost_estimate=pl.CostEstimate(
            flops=2 * seq_len * D * (mixing_own.shape[1] + q.shape[1])
            + 10 * seq_len**2 * q.shape[1] * 4,
            bytes_accessed=seq_len * D * 8, transcendentals=0,
        ),
        name="attention_backward",
    )(grads, exit_own, mixing_own, q, k, v, logs, tokens_all, cos_table, sin_table)


def after(*values):
    return lax.optimization_barrier(values)


MESH = pl.DeviceIdType.MESH


def project_rows(at, size, tok_rows, mix, gain_row, cos_ref, sin_ref, normed_ref, q_ref, k_ref, v_ref):
    rows = slice(at, at + size)
    q_width, k_width = q_ref.shape[1], k_ref.shape[1]
    values = tok_rows.astype(single)
    inverse = lax.rsqrt(jnp.mean(values * values, axis=-1, keepdims=True) + epsilon)
    normed = (values * inverse * gain_row).astype(narrow)
    normed_ref[rows] = normed
    projected = dot(normed, mix, 1, 0)
    width = q_width + k_width
    turned = rope(
        projected[:, :width], wide(cos_ref[rows], width), wide(sin_ref[rows], width)
    ).astype(narrow)
    q_ref[rows] = turned[:, :q_width]
    k_ref[rows] = turned[:, q_width:]
    v_ref[rows] = projected[:, width:].astype(narrow)


def attend_rows(q_ref, k_ref, v_ref, att_ref, log_ref):
    seq_len, k_width = k_ref.shape
    size = QROWS
    group_size = HEADS // KV_HEADS
    for kv in range(k_width // HEAD_DIM):
        lanes = slice(kv * HEAD_DIM, (kv + 1) * HEAD_DIM)
        for block in range(seq_len // size):
            at = block * size
            end = at + size
            queries = stacked(q_ref, at, kv, size)
            scores = key_scores(k_ref[:end, lanes], queries, at, size)
            top = jnp.max(scores, axis=0, keepdims=True)
            exponent = jnp.exp(scores - top)
            total = jnp.sum(exponent, axis=0, keepdims=True)
            soft = (exponent * (1.0 / total)).astype(narrow)
            log_ref[kv * (seq_len // size) + block] = top + jnp.log(total)
            out = dot(v_ref[:end, lanes], soft, 0, 0)
            for g in range(group_size):
                head = kv * group_size + g
                att_ref[at:end, head * HEAD_DIM : (head + 1) * HEAD_DIM] = (
                    out[:, g * size : (g + 1) * size].T.astype(narrow)
                )


def forward_body(
    tok_ref, pack_ref, cot_ref, wg_ref, wu_ref, wd_ref, cos_ref, sin_ref,
    normed_ref, q_ref, k_ref, v_ref, att_ref, log_ref, hid_ref, gain_ref,
    tokall_ref, wall_ref, xa_ref, xo_ref, ya_ref, yo_ref, wout_ref,
    tokv, wv, part, landed, xv, send, recv, local_sem,
):
    groups, fsdp, few, width = wv.shape
    q_width, k_width = q_ref.shape[1], k_ref.shape[1]
    mix_width = q_width + 2 * k_width
    size = tok_ref.shape[0]
    s, h, r = lax.axis_index("seq"), lax.axis_index("half"), lax.axis_index("ring")
    f = h * 4 + r
    counter = [0]
    to_half, to_z, to_core = {"half": h ^ 1}, {"ring": r ^ 2}, {"ring": r ^ 1}
    to_seq = [{"seq": s ^ j} for j in range(groups)]

    def remote(source, target, peer):
        k = counter[0]
        counter[0] += 1
        return pltpu.make_async_remote_copy(
            src_ref=source, dst_ref=target, send_sem=send.at[k], recv_sem=recv.at[k],
            device_id=peer, device_id_type=MESH,
        )

    started = []

    def start(*copies):
        for copy in copies:
            copy.start()
            started.append(copy)

    def spread(source, target):
        return [remote(source, target, to_seq[j]) for j in range(1, groups)]

    barrier = pltpu.get_barrier_semaphore()
    peers = to_seq[1:] + [to_half, to_z, to_core]
    for peer in peers:
        pl.semaphore_signal(barrier, inc=1, device_id=peer, device_id_type=MESH)
    pl.semaphore_wait(barrier, len(peers))

    pack_go = [remote(pack_ref.at[s ^ j], wv.at[s, f], to_seq[j]) for j in range(1, groups)]
    tok_go = spread(tok_ref, tokv.at[s])
    start(*pack_go)
    start(*tok_go)
    own_cot = pltpu.make_async_copy(cot_ref, ya_ref.at[s], local_sem.at[0])
    own_cot.start()
    wv[s, f] = pack_ref[s]
    tokv[s] = tok_ref[...]

    for copy in pack_go:
        copy.wait_recv()
    mine = wv.at[:, f]
    a_half, a_z, a_core = (
        remote(mine, mine, to_half), remote(mine, mine, to_z), remote(mine, mine, to_core)
    )
    start(a_half, a_z, a_core)
    cot_go = spread(cot_ref, ya_ref.at[s])
    start(*cot_go)
    a_half.wait_recv()
    block = wv.at[:, f ^ 4]
    b_z, b_core = remote(block, block, to_z), remote(block, block, to_core)
    start(b_z, b_core)
    a_z.wait_recv()
    block = wv.at[:, f ^ 2]
    c_core = remote(block, block, to_core)
    start(c_core)
    cot_half = remote(cot_ref, yo_ref.at[s], to_half)
    start(cot_half)

    sources = (wg_ref, wu_ref, wd_ref)

    def weights_first(t):
        own, other = sources[t].at[h], sources[t].at[1 - h]
        target = wout_ref.at[t, h, r]
        copies = (
            remote(other, target, to_half), remote(own, target, to_z), remote(own, target, to_core)
        )
        start(*copies)
        return copies

    def weights_next(t, first):
        first[0].wait_recv()
        came = wout_ref.at[t, 1 - h, r]
        on_z, on_core = remote(came, came, to_z), remote(came, came, to_core)
        start(on_z, on_core)
        first[1].wait_recv()
        beside = wout_ref.at[t, h, r ^ 2]
        last = remote(beside, beside, to_core)
        start(last)
        return on_z, on_core, last

    def weights_last(t, second):
        second[0].wait_recv()
        beyond = wout_ref.at[t, 1 - h, r ^ 2]
        copy = remote(beyond, beyond, to_core)
        start(copy)
        return copy

    gate_first = weights_first(0)
    b_z.wait_recv()
    block = wv.at[:, f ^ 6]
    d_core = remote(block, block, to_core)
    start(d_core)
    up_first = weights_first(1)

    for copy in tok_go + [a_core, b_core, c_core, d_core]:
        copy.wait_recv()
    keep_tok = pltpu.make_async_copy(tokv, tokall_ref, local_sem.at[1])
    keep_tok.start()
    keep_wall = pltpu.make_async_copy(wv, wall_ref, local_sem.at[2])
    keep_wall.start()
    depth = groups * fsdp * few
    gains = wv[:, :, :, mix_width + q_width :].reshape(depth, width - mix_width - q_width)
    gains = gains.astype(single).T[0:8]
    gain_ref[...] = gains
    for j in range(groups):
        project_rows(
            j * size, size, tokv[j], wv[:, :, :, :mix_width].reshape(depth, mix_width),
            gains[0:1], cos_ref, sin_ref, normed_ref, q_ref, k_ref, v_ref,
        )
    attend_rows(q_ref, k_ref, v_ref, att_ref, log_ref)
    exit_own = wv[:, :, :, mix_width : mix_width + q_width].reshape(depth, q_width)
    part_go = []
    for j in list(range(1, groups)) + [0]:
        rows = pl.ds(pl.multiple_of((s ^ j) * size, size), size)
        partial = dot(att_ref[rows], exit_own, 1, 1)
        if j:
            part[j - 1] = partial.astype(narrow)
            copy = remote(part.at[j - 1], landed.at[j - 1], to_seq[j])
            start(copy)
            part_go.append(copy)
        else:
            hid_ref[...] = tok_ref[...].astype(single) + partial
    cot_half.wait_recv()
    gate_next = weights_next(0, gate_first)
    for j, copy in enumerate(part_go):
        copy.wait_recv()
        hid_ref[...] += landed[j].astype(single)
    hidden = hid_ref[...]
    inverse = lax.rsqrt(jnp.mean(hidden * hidden, axis=-1, keepdims=True) + epsilon)
    xv[...] = (hidden * inverse * gains[1:2]).astype(narrow)
    row_half = remote(xv, xo_ref.at[s], to_half)
    start(row_half)
    row_go = spread(xv, xa_ref.at[s])
    start(*row_go)
    own_row = pltpu.make_async_copy(xv, xa_ref.at[s], local_sem.at[3])
    own_row.start()
    down_first = weights_first(2)
    up_next = weights_next(1, up_first)
    row_half.wait_recv()
    other_go = spread(xo_ref.at[s], xo_ref.at[s])
    start(*other_go)
    cot_other = spread(yo_ref.at[s], yo_ref.at[s])
    start(*cot_other)
    weights_last(0, gate_next)
    down_next = weights_next(2, down_first)
    weights_last(1, up_next)
    weights_last(2, down_next)
    waited = set(
        id(copy)
        for copy in pack_go + tok_go + part_go
        + [a_half, a_z, a_core, b_z, b_core, c_core, d_core, cot_half, row_half]
        + [item for first in (gate_first, up_first, down_first) for item in first[:2]]
        + [second[0] for second in (gate_next, up_next, down_next)]
    )
    for copy in started:
        copy.wait_send()
        if id(copy) not in waited:
            copy.wait_recv()
    for copy in (own_cot, keep_tok, keep_wall, own_row):
        copy.wait()


def forward_call(tokens, packed, cotangent, weights, cos_table, sin_table, q_width, k_width):
    groups, few, width = packed.shape
    _, own, part, hidden_units = weights[0].shape
    size = tokens.shape[0]
    seq_len = size * groups
    blocks = k_width // HEAD_DIM * (seq_len // QROWS)
    shape = jax.ShapeDtypeStruct
    vmem = pl.BlockSpec(memory_space=pltpu.VMEM)
    hbm = pl.BlockSpec(memory_space=pl.ANY)
    rows = shape((groups, size, D), narrow)
    count = 80
    return pl.pallas_call(
        forward_body,
        in_specs=[vmem] * 3 + [hbm] * 3 + [vmem] * 2,
        out_specs=[vmem] * 8 + [hbm] * 7,
        out_shape=[
            shape((seq_len, D), narrow),
            shape((seq_len, q_width), narrow),
            shape((seq_len, k_width), narrow),
            shape((seq_len, k_width), narrow),
            shape((seq_len, q_width), narrow),
            shape((blocks, 1, HEADS // KV_HEADS * QROWS), single),
            shape((size, D), single),
            shape((8, D), single),
            rows,
            shape((groups, 8, few, width), narrow),
            rows, rows, rows, rows,
            shape((3, 2, 4, own, part, hidden_units), narrow),
        ],
        scratch_shapes=[
            pltpu.VMEM((groups, size, D), narrow),
            pltpu.VMEM((groups, 8, few, width), narrow),
            pltpu.VMEM((groups - 1, size, D), narrow),
            pltpu.VMEM((groups - 1, size, D), narrow),
            pltpu.VMEM((size, D), narrow),
            pltpu.SemaphoreType.DMA((count,)),
            pltpu.SemaphoreType.DMA((count,)),
            pltpu.SemaphoreType.DMA((4,)),
        ],
        compiler_params=pltpu.CompilerParams(collective_id=0, has_side_effects=True),
        cost_estimate=pl.CostEstimate(
            flops=200_000_000_000, bytes_accessed=100_000_000, transcendentals=0
        ),
        name="forward_exchange",
    )(tokens, packed, cotangent, *weights, cos_table, sin_table)


def expert_body(
    batch, own_apart, where_ref, all_ref, g_ref, u_ref, d_ref, *refs,
):
    _, halves, rings, _, part, width = all_ref.shape
    pieces = halves * rings
    x_refs, y_refs, w_ref = refs[:batch], refs[batch : 2 * batch], refs[2 * batch]
    refs = refs[2 * batch + 1 :]
    out_refs, row_refs, slot_ref = refs[:batch], refs[batch : 2 * batch], refs[2 * batch]
    gg_ref, gu_ref, gd_ref, held, sems = refs[2 * batch + 1 :]
    half, ring = where_ref[0], where_ref[1]
    e = pl.program_id(0)
    slot = lax.rem(e, 2)

    def each(expert, slot, act):
        for t, own_ref in enumerate((g_ref, u_ref, d_ref)):
            for g in range(halves):
                for r in range(rings):
                    at = g * rings + r
                    target, sem = held.at[slot, t, at], sems.at[slot, t, at]
                    if not own_apart:
                        act(pltpu.make_async_copy(all_ref.at[t, g, r, expert], target, sem))
                        continue
                    own = (half == g) & (ring == r)

                    @pl.when(own)
                    def _():
                        act(pltpu.make_async_copy(own_ref.at[g, expert], target, sem))

                    @pl.when(jnp.logical_not(own))
                    def _():
                        act(pltpu.make_async_copy(all_ref.at[t, g, r, expert], target, sem))

    @pl.when(e == 0)
    def _():
        each(e, slot, lambda copy: copy.start())

    @pl.when(e + 1 < pl.num_programs(0))
    def _():
        each(e + 1, 1 - slot, lambda copy: copy.start())

    for t in range(3):
        for at in range(pieces):
            pltpu.make_async_copy(
                all_ref.at[t, at // rings, at % rings, e], held.at[slot, t, at], sems.at[slot, t, at]
            ).wait()

    def weight(t):
        return held[slot, t].reshape(pieces * part, width)

    def write(ref, value):
        for g in range(halves):
            for r in range(rings):
                at = (g * rings + r) * part
                ref[r, g ^ half, 0] = value[at : at + part].astype(ref.dtype)

    slots = x_refs[0].shape[1]

    def split(outs, value):
        for b, ref in enumerate(outs):
            ref[0] = value[b * slots : (b + 1) * slots].astype(ref.dtype)

    rows = jnp.concatenate([ref[0] for ref in x_refs], axis=0)
    cots = jnp.concatenate([ref[0] for ref in y_refs], axis=0)
    share = w_ref[0]
    gate, up, down = weight(0), weight(1), weight(2)
    gate_pre = dot(rows, gate, 1, 0)
    up_pre = dot(rows, up, 1, 0)
    sig = jax.nn.sigmoid(gate_pre)
    mid = (gate_pre * sig * up_pre).astype(narrow)
    expert_out = dot(mid, down, 1, 1)
    cot_float = cots.astype(single)
    slot_ref[0] = jnp.sum(cot_float * expert_out, axis=-1, keepdims=True)
    split(out_refs, expert_out * share)
    out_low = (cot_float * share).astype(narrow)
    mid_grad = dot(out_low, down, 1, 0)
    write(gd_ref, dot(out_low, mid, 0, 0))
    gate_grad = (mid_grad * up_pre * sig * (1.0 + gate_pre * (1.0 - sig))).astype(narrow)
    up_grad = (mid_grad * gate_pre * sig).astype(narrow)
    split(row_refs, dot(gate_grad, gate, 1, 1) + dot(up_grad, up, 1, 1))
    write(gg_ref, dot(rows, gate_grad, 0, 0))
    write(gu_ref, dot(rows, up_grad, 0, 0))


def expert_call(where, gathered, weights, own_apart, rows, cots, share):
    _, halves, rings, own, part, width = gathered.shape
    batch = len(rows)
    _, slots, depth = rows[0].shape
    pieces = halves * rings
    weight_spec = pl.BlockSpec((rings, halves, 1, part, width), lambda e, h: (0, 0, e, 0, 0))
    row_spec = pl.BlockSpec((1, slots, depth), lambda e, h: (e, 0, 0))
    share_spec = pl.BlockSpec((1, batch * slots, 1), lambda e, h: (e, 0, 0))
    shape = jax.ShapeDtypeStruct
    row_shape = shape((own, slots, depth), narrow)
    outs = pl.pallas_call(
        functools.partial(expert_body, batch, own_apart),
        grid_spec=pltpu.PrefetchScalarGridSpec(
            num_scalar_prefetch=1,
            grid=(own,),
            in_specs=[pl.BlockSpec(memory_space=pl.ANY)] * 4
            + [row_spec] * (2 * batch)
            + [share_spec],
            out_specs=[row_spec] * (2 * batch) + [share_spec] + [weight_spec] * 3,
            scratch_shapes=[
                pltpu.VMEM((2, 3, pieces, part, width), narrow),
                pltpu.SemaphoreType.DMA((2, 3, pieces)),
            ],
        ),
        out_shape=[row_shape] * (2 * batch)
        + [shape((own, batch * slots, 1), single)]
        + [shape((rings, halves, own, part, width), narrow)] * 3,
        cost_estimate=pl.CostEstimate(
            flops=9 * 2 * own * batch * slots * depth * width,
            bytes_accessed=12 * own * depth * width + 8 * batch * own * slots * depth,
            transcendentals=0,
        ),
        name="expert_ffn",
    )(where, gathered, *weights, *rows, *cots, share)
    return outs[:batch], outs[batch : 2 * batch], outs[2 * batch], outs[2 * batch + 1 :]


def local(
    halves, rings,
    tokens, mixing_weight, output_weight, norm_gains, expert_gate, expert_up, expert_down,
    gate_logits, routes, fill_order, cotangent,
):
    groups = lax.axis_size("seq")
    column = lax.axis_index("seq")
    half = lax.axis_index("half")
    ring = lax.axis_index("ring")
    paired = halves == 2
    tok_rows = tokens.shape[1]
    seq_len = tok_rows * groups
    capacity = (seq_len * TOP + EXPERTS - 1) // EXPERTS
    local_count = expert_gate.shape[1]
    own_count = local_count // halves
    part = expert_gate.shape[0]
    fsdp_rows = mixing_weight.shape[0]
    q_width = HEADS * HEAD_DIM // groups
    k_width = KV_HEADS * HEAD_DIM // groups
    mix_width = q_width + 2 * k_width
    own_kv = KV_HEADS // groups
    own_heads = HEADS // groups
    group_size = HEADS // KV_HEADS
    score_scale = 1.0 / math.sqrt(HEAD_DIM)
    query_all = HEADS * HEAD_DIM
    key_all = KV_HEADS * HEAD_DIM

    def gather_seq(value):
        parts = [value] + [swap(value, "seq", j, groups) for j in range(1, groups)]
        whole = jnp.zeros((groups,) + value.shape, value.dtype)
        for j, item in enumerate(parts):
            whole = lax.dynamic_update_index_in_dim(whole, item, column ^ j, 0)
        return whole.reshape((seq_len,) + value.shape[1:])

    def scatter_seq(value):
        blocks = value.reshape((groups, tok_rows) + value.shape[1:])
        total = lax.dynamic_index_in_dim(blocks, column, 0, False).astype(single)
        for j in range(1, groups):
            sent = lax.dynamic_index_in_dim(blocks, column ^ j, 0, False).astype(narrow)
            total = total + swap(sent, "seq", j, groups).astype(single)
        return total

    def exchange_seq(blocks):
        whole = lax.dynamic_update_index_in_dim(
            jnp.zeros_like(blocks), lax.dynamic_index_in_dim(blocks, column, 0, False), column, 0
        )
        for j in range(1, groups):
            sent = lax.dynamic_index_in_dim(blocks, column ^ j, 0, False)
            whole = lax.dynamic_update_index_in_dim(
                whole, swap(sent, "seq", j, groups), column ^ j, 0
            )
        return whole

    packed = jnp.concatenate(
        [
            mixing_weight[:, :query_all].reshape(fsdp_rows, groups, q_width),
            mixing_weight[:, query_all : query_all + key_all].reshape(fsdp_rows, groups, k_width),
            mixing_weight[:, query_all + key_all :].reshape(fsdp_rows, groups, k_width),
            output_weight.reshape(fsdp_rows, groups, q_width),
            jnp.broadcast_to(
                jnp.pad(norm_gains, ((0, 0), (0, PAD - 2)))[:, None], (fsdp_rows, groups, PAD)
            ),
        ],
        2,
    ).transpose(1, 0, 2)
    cos_table, sin_table = rotary_tables(jnp.arange(seq_len, dtype=jnp.int32))
    cos_table, sin_table = jnp.tile(cos_table, (1, 2)), jnp.tile(sin_table, (1, 2))
    own_weights = [
        item.transpose(1, 0, 2).reshape(halves, own_count, part, FF)
        for item in (expert_gate, expert_up, expert_down)
    ]
    inputs = tokens[0].astype(single)
    if paired:
        (
            normed_low, queries, keys, values, attended, logs, hidden, gains_float,
            tokens_all, packed, own_x, other_x, own_y, other_y, gathered,
        ) = forward_call(
            tokens[0], packed, cotangent[0], own_weights, cos_table, sin_table, q_width, k_width
        )
        tokens_all = tokens_all.reshape(seq_len, D)
        packed = packed.reshape(D, -1)
        mixing_own = packed[:, :mix_width]
        exit_own = packed[:, mix_width : mix_width + q_width]
        seq_rows = [item.reshape(seq_len, D) for item in (own_x, other_x)]
        cot_rows = [item.reshape(seq_len, D) for item in (own_y, other_y)]
    else:
        packed = exchange_seq(packed)
        packed = lax.all_gather(packed, ("half", "ring"), axis=0, tiled=False)
        packed = packed.transpose(1, 0, 2, 3).reshape(D, -1)
        mixing_own = packed[:, :mix_width]
        exit_own = packed[:, mix_width : mix_width + q_width]
        gains_float = packed[:, mix_width + q_width : mix_width + q_width + 2].astype(single).T
        tokens_all = gather_seq(tokens[0])
        gathered = jnp.stack(
            [lax.all_gather(item[0], "ring", axis=0, tiled=False)[None] for item in own_weights]
        )
        normed_low, queries, keys, values, attended, logs, attn_part = attention_call(
            tokens_all, mixing_own, exit_own, gains_float, cos_table, sin_table
        )
        hidden = inputs + scatter_seq(attn_part)
        scale_two = lax.rsqrt(jnp.mean(hidden * hidden, axis=-1, keepdims=True) + epsilon)
        seq_rows = [gather_seq((hidden * scale_two * gains_float[1]).astype(narrow))]
        cot_rows = [gather_seq(cotangent[0])]
    inverse_two = lax.rsqrt(jnp.mean(hidden * hidden, axis=-1, keepdims=True) + epsilon)

    def pair(value):
        if halves == 1:
            return value[None]
        return jnp.stack([value, swap(value, "half", 1, halves)])

    def scatter_rows(values):
        if halves == 1:
            return scatter_seq(combine(0, values[0]))
        first, own = after(combine(1, values[1]), values[0])
        other = scatter_seq(first).astype(narrow)
        return scatter_seq(combine(0, own)) + swap(other, "half", 1, halves).astype(single)

    pair_routes = pair(routes[0])
    pair_order = pair(fill_order[0])
    pair_gating = softmax_last(pair(gate_logits[0]))
    expert_ids = column * local_count + half * own_count + jnp.arange(own_count, dtype=jnp.int32)
    slots = (capacity + 15) // 16 * 16
    places = jnp.arange(seq_len, dtype=jnp.int32)
    chosen = (pair_routes[..., None] == expert_ids).astype(single)
    hits = jnp.sum(chosen, axis=2)
    token_weight = jnp.sum(pair_gating[..., None] * chosen, axis=2)
    place_of = jnp.sum(
        jnp.where(pair_order[:, :, None] == places, places[None, :, None], 0), axis=1
    )
    earlier = (place_of[:, None, :] < place_of[:, :, None]).astype(narrow)
    rank = jnp.einsum(
        "btu,bue->bte", earlier, hits.astype(narrow), preferred_element_type=single
    ).astype(jnp.int32)
    kept = (hits > 0) & (rank < capacity)
    flat_place = jnp.where(kept, rank + jnp.arange(own_count, dtype=jnp.int32) * slots, -1)
    flat_ids = jnp.arange(own_count * slots, dtype=jnp.int32)
    filled = flat_place[:, :, 0:1] == flat_ids
    for e in range(1, own_count):
        filled = filled | (flat_place[:, :, e : e + 1] == flat_ids)
    select = filled.astype(narrow)
    batch = select.shape[0]
    match = flat_place[:, :, :, None] == (
        jnp.arange(own_count, dtype=jnp.int32)[:, None] * slots
        + jnp.arange(slots, dtype=jnp.int32)[None, :]
    )
    slot_weight = jnp.sum(jnp.where(match, token_weight[..., None], 0.0), axis=1)
    share = slot_weight.transpose(1, 0, 2).reshape(own_count, batch * slots, 1)

    def dispatch(rows):
        return [
            lax.dot_general(
                select[b], item, (((0,), (0,)), ((), ())), preferred_element_type=narrow
            ).reshape(own_count, slots, D)
            for b, item in enumerate(rows)
        ]

    def combine(b, values):
        return lax.dot_general(
            select[b],
            values.reshape(own_count * slots, D),
            (((1,), (0,)), ((), ())),
            preferred_element_type=narrow,
        )

    slot_out, slot_back, slot_grad, (gate_term, up_term, down_term) = expert_call(
        jnp.stack([half, ring]), gathered, own_weights, paired,
        dispatch(seq_rows), dispatch(cot_rows), share,
    )
    normed_two_grad = scatter_rows(slot_back)
    slot_grad = slot_grad.reshape(own_count, batch, slots).transpose(1, 0, 2)
    weight_grad_tok = jnp.sum(jnp.where(match, slot_grad[:, None], 0.0), axis=3)
    route_part = jnp.sum(weight_grad_tok[:, :, None, :] * chosen, axis=-1)

    def send_routes(value):
        blocks = value.reshape(groups, tok_rows, TOP)
        total = lax.dynamic_index_in_dim(blocks, column, 0, False)
        for j in range(1, groups):
            sent = lax.dynamic_index_in_dim(blocks, column ^ j, 0, False)
            total = total + swap(sent, "seq", j, groups)
        return total

    if halves > 1:
        route_part = route_part[0] + swap(route_part[1], "half", 1, halves)
    else:
        route_part = route_part[0]
    route_grad = send_routes(route_part)
    gating = softmax_last(
        lax.dynamic_slice_in_dim(gate_logits[0], column * tok_rows, tok_rows, 0)
    )
    logits_rows = gating * (route_grad - jnp.sum(gating * route_grad, axis=-1, keepdims=True))

    def expert_gradient(term):
        if halves > 1:
            own, other = term[0], swap(term[1], "half", 1, halves)
            term = jnp.stack([jnp.where(half == 0, own, other), jnp.where(half == 0, other, own)])
        return term.reshape(local_count, part, FF).transpose(1, 0, 2).astype(single)

    def ring_sum(term):
        return lax.psum_scatter(term, "ring", scatter_dimension=0, tiled=False)

    down_sum, gate_sum = ring_sum(down_term), ring_sum(gate_term)
    *slot_out, normed_two_grad = after(*slot_out, normed_two_grad)
    moe_rows = scatter_rows(slot_out)
    layer_output = (hidden + moe_rows).astype(narrow)[None]

    normal_two = hidden * inverse_two
    scaled_two = normed_two_grad * gains_float[1]
    hidden_grad = cotangent[0].astype(single) + inverse_two * (
        scaled_two - normal_two * jnp.mean(scaled_two * normal_two, axis=-1, keepdims=True)
    )
    gain_two_grad = jnp.sum(normed_two_grad * normal_two, axis=0)
    attn_grad, down_sum = after(hidden_grad.astype(narrow), down_sum)
    attn_grad_all = gather_seq(attn_grad)
    projected_grad, normed_part, gain_one_grad = attention_back_call(
        attn_grad_all, exit_own, mixing_own, queries, keys, values, logs, tokens_all,
        cos_table, sin_table,
    )
    mixing_term = dot(normed_low, projected_grad, 0, 0)
    output_term = dot(attn_grad_all, attended, 0, 0)
    gains_term = jnp.pad(jnp.stack([gain_one_grad[0], gain_two_grad], 1), ((0, 0), (0, PAD - 2)))
    attn_term = jnp.concatenate([mixing_term, output_term, gains_term], 1).astype(narrow)
    attn_term = attn_term.reshape(groups, halves * rings, fsdp_rows, -1).transpose(1, 0, 2, 3)
    attn_total = lax.psum_scatter(attn_term, ("half", "ring"), scatter_dimension=0, tiled=False)
    attn_total = exchange_seq(attn_total).astype(single)

    def columns(first, width):
        return attn_total[:, :, first : first + width].transpose(1, 0, 2).reshape(fsdp_rows, -1)

    mixing_gradient = jnp.concatenate(
        [
            columns(0, q_width),
            columns(q_width, k_width),
            columns(q_width + k_width, k_width),
        ],
        1,
    )
    output_gradient = columns(mix_width, q_width)
    gains_gradient = jnp.sum(attn_total[:, :, mix_width + q_width :][:, :, :2], axis=0)

    normed_grad, gate_sum = after(scatter_seq(normed_part), gate_sum)
    down_gradient = expert_gradient(down_sum)
    gate_gradient = expert_gradient(gate_sum)
    up_gradient = expert_gradient(ring_sum(up_term))
    inverse_one = lax.rsqrt(jnp.mean(inputs * inputs, axis=-1, keepdims=True) + epsilon)
    normal_one = inputs * inverse_one
    scaled_one = normed_grad * gains_float[0]
    tokens_gradient = (
        hidden_grad
        + inverse_one
        * (scaled_one - normal_one * jnp.mean(scaled_one * normal_one, axis=-1, keepdims=True))
    )[None]
    return (
        layer_output,
        tokens_gradient,
        mixing_gradient,
        output_gradient,
        gains_gradient,
        gate_gradient,
        up_gradient,
        down_gradient,
        logits_rows[None],
    )


def solution(mesh):
    groups, shards = mesh.shape["seq"], mesh.shape["fsdp"]
    halves = 2 if (EXPERTS // groups) % 2 == 0 and shards == 8 else 1
    rings = shards // halves
    grid = Mesh(mesh.devices.reshape(groups, halves, rings), ("seq", "half", "ring"))
    fsdp = ("half", "ring")
    every = ("seq", "half", "ring")
    in_specs = (
        P(fsdp, "seq", None),
        P(every, None),
        P(every, None),
        P(every, None),
        P(fsdp, "seq", None),
        P(fsdp, "seq", None),
        P(fsdp, "seq", None),
        P(fsdp, None, None),
        P(fsdp, None, None),
        P(fsdp, None),
        P(fsdp, "seq", None),
    )
    out_specs = (
        P(fsdp, "seq", None),
        P(fsdp, "seq", None),
        P(every, None),
        P(every, None),
        P(every, None),
        P(fsdp, "seq", None),
        P(fsdp, "seq", None),
        P(fsdp, "seq", None),
        P(fsdp, "seq", None),
    )
    return jax.shard_map(
        functools.partial(local, halves, rings),
        mesh=grid,
        in_specs=in_specs,
        out_specs=out_specs,
        check_vma=False,
    )
```

```python
import functools
import math

import jax
import jax.numpy as jnp
import numpy as np
from jax import lax
from jax.experimental import pallas as pl
from jax.experimental.pallas import tpu as pltpu
from jax.sharding import Mesh
from jax.sharding import PartitionSpec as P

D = 1536
HEADS = 24
KV_HEADS = 8
HEAD_DIM = 64
FF = 512
EXPERTS = 40
TOP = 8
QROWS = 256
PAD = 128

epsilon = 1e-05
rope_base = 10000.0
single = jnp.float32
narrow = jnp.bfloat16
MESH = pl.DeviceIdType.MESH


def rotary_tables(positions):
    half_width = HEAD_DIM // 2
    frequency = rope_base ** (-2.0 * jnp.arange(half_width, dtype=single) / HEAD_DIM)
    angles = positions.astype(single)[:, None] * frequency[None, :]
    cos_table = jnp.cos(angles)
    sin_table = jnp.sin(angles)
    return (jnp.concatenate([cos_table, cos_table], 1), jnp.concatenate([sin_table, sin_table], 1))


def softmax_last(logit_rows):
    row_max = jnp.max(logit_rows, axis=-1, keepdims=True)
    exponent = jnp.exp(logit_rows - row_max)
    return exponent / jnp.sum(exponent, axis=-1, keepdims=True)


def swap(value, axis, step, size):
    return lax.ppermute(value, axis, [(i, i ^ step) for i in range(size)])


def dot(left, right, left_dim, right_dim):
    return lax.dot_general(
        left, right, (((left_dim,), (right_dim,)), ((), ())), preferred_element_type=single
    )


def rope(values, cos_row, sin_row):
    width = values.shape[-1]
    lane = lax.broadcasted_iota(jnp.int32, values.shape, 1) % HEAD_DIM
    turned = jnp.where(
        lane < HEAD_DIM // 2,
        -pltpu.roll(values, width - HEAD_DIM // 2, 1),
        pltpu.roll(values, HEAD_DIM // 2, 1),
    )
    return values * cos_row + turned * sin_row


def rope_back(values, cos_row, sin_row):
    width = values.shape[-1]
    lane = lax.broadcasted_iota(jnp.int32, values.shape, 1) % HEAD_DIM
    scaled = values * sin_row
    turned = jnp.where(
        lane < HEAD_DIM // 2,
        pltpu.roll(scaled, width - HEAD_DIM // 2, 1),
        -pltpu.roll(scaled, HEAD_DIM // 2, 1),
    )
    return values * cos_row + turned


def wide(table, width):
    return jnp.concatenate([table] * (width // table.shape[1]), axis=1)


def stacked(ref, at, kv, size):
    group_size = HEADS // KV_HEADS
    return jnp.concatenate(
        [
            ref[at : at + size, (kv * group_size + g) * HEAD_DIM : (kv * group_size + g + 1) * HEAD_DIM]
            for g in range(group_size)
        ],
        axis=0,
    )


def key_scores(keys, queries, at, size):
    scores = dot(keys, queries, 1, 1) * (1.0 / math.sqrt(HEAD_DIM))
    shape = scores.shape
    key_at = lax.broadcasted_iota(jnp.int32, shape, 0)
    query_at = lax.broadcasted_iota(jnp.int32, shape, 1) % size + at
    return jnp.where(key_at <= query_at, scores, -jnp.inf)


def attention_body(
    tok_ref, mix_ref, exit_ref, gain_ref, cos_ref, sin_ref,
    normed_ref, q_ref, k_ref, v_ref, att_ref, log_ref, part_ref,
):
    seq_len = tok_ref.shape[0]
    size = QROWS
    for at in range(0, seq_len, size):
        project_rows(
            at, size, tok_ref[at : at + size], mix_ref[...], gain_ref[0:1],
            cos_ref, sin_ref, normed_ref, q_ref, k_ref, v_ref,
        )
    attend_rows(q_ref, k_ref, v_ref, att_ref, log_ref)
    for at in range(0, seq_len, size):
        part_ref[at : at + size] = dot(att_ref[at : at + size], exit_ref[...], 1, 1).astype(narrow)


def attention_call(tokens_all, mixing_own, exit_own, gains, cos_table, sin_table):
    seq_len = tokens_all.shape[0]
    q_width = exit_own.shape[1]
    k_width = (mixing_own.shape[1] - q_width) // 2
    group_size = HEADS // KV_HEADS
    blocks = k_width // HEAD_DIM * (seq_len // QROWS)
    shape = jax.ShapeDtypeStruct
    return pl.pallas_call(
        attention_body,
        out_shape=[
            shape((seq_len, D), narrow),
            shape((seq_len, q_width), narrow),
            shape((seq_len, k_width), narrow),
            shape((seq_len, k_width), narrow),
            shape((seq_len, q_width), narrow),
            shape((blocks, 1, group_size * QROWS), single),
            shape((seq_len, D), narrow),
        ],
        cost_estimate=pl.CostEstimate(
            flops=2 * seq_len * D * (mixing_own.shape[1] + q_width) + 4 * seq_len**2 * q_width * 4,
            bytes_accessed=seq_len * D * 6, transcendentals=0,
        ),
        name="attention_forward",
    )(tokens_all, mixing_own, exit_own, gains, cos_table, sin_table)


def norm_back(grads, values, gain_row):
    inverse = lax.rsqrt(jnp.mean(values * values, axis=-1, keepdims=True) + epsilon)
    normal = values * inverse
    scaled = grads * gain_row
    back = inverse * (scaled - normal * jnp.mean(scaled * normal, axis=-1, keepdims=True))
    return back, jnp.sum(grads * normal, axis=0, keepdims=True)


def attend_back_rows(out_grad, q_ref, k_ref, v_ref, log_ref, pg_ref, keys_sum, values_sum):
    seq_len, k_width = k_ref.shape
    q_width = q_ref.shape[1]
    size = QROWS
    group_size = HEADS // KV_HEADS
    scale = 1.0 / math.sqrt(HEAD_DIM)
    for kv in range(k_width // HEAD_DIM):
        lanes = slice(kv * HEAD_DIM, (kv + 1) * HEAD_DIM)
        keys_sum[...] = jnp.zeros_like(keys_sum)
        values_sum[...] = jnp.zeros_like(values_sum)
        for block in range(seq_len // size):
            at = block * size
            end = at + size
            queries = stacked(q_ref, at, kv, size)
            grads = stacked(out_grad, at, kv, size)
            keys, values = k_ref[:end, lanes], v_ref[:end, lanes]
            scores = key_scores(keys, queries, at, size)
            soft = jnp.exp(scores - log_ref[kv * (seq_len // size) + block])
            values_sum[:end] += dot(soft.astype(narrow), grads, 1, 0)
            soft_grad = dot(values, grads, 1, 1)
            delta = jnp.sum(soft * soft_grad, axis=0, keepdims=True)
            scores_grad = (soft * (soft_grad - delta)).astype(narrow)
            keys_sum[:end] += dot(scores_grad, queries, 1, 0) * scale
            query_grad = dot(keys, scores_grad, 0, 0) * scale
            for g in range(group_size):
                head = kv * group_size + g
                pg_ref[at:end, head * HEAD_DIM : (head + 1) * HEAD_DIM] = (
                    query_grad[:, g * size : (g + 1) * size].T.astype(narrow)
                )
        first = q_width + kv * HEAD_DIM
        pg_ref[:, first : first + HEAD_DIM] = keys_sum[...].astype(narrow)
        first += k_width
        pg_ref[:, first : first + HEAD_DIM] = values_sum[...].astype(narrow)


def project_back_rows(pg_ref, mix_ref, tok_ref, cos_ref, sin_ref, part_ref, turned, size):
    gain = jnp.zeros((1, D), single)
    for at in range(0, tok_ref.shape[0], size):
        rows = slice(at, at + size)
        pg_ref[rows, :turned] = rope_back(
            pg_ref[rows, :turned].astype(single), wide(cos_ref[rows], turned),
            wide(sin_ref[rows], turned),
        ).astype(narrow)
        normed_part = dot(pg_ref[rows], mix_ref, 1, 1)
        part_ref[rows] = normed_part.astype(narrow)
        values = tok_ref[rows].astype(single)
        inverse = lax.rsqrt(jnp.mean(values * values, axis=-1, keepdims=True) + epsilon)
        gain = gain + jnp.sum(normed_part * (values * inverse), axis=0, keepdims=True)
    return gain


def attention_back_body(
    grad_ref, exit_ref, mix_ref, q_ref, k_ref, v_ref, log_ref, tok_ref, cos_ref, sin_ref,
    pg_ref, part_ref, gain_ref,
    out_grad, keys_sum, values_sum,
):
    size = QROWS
    for at in range(0, tok_ref.shape[0], size):
        out_grad[at : at + size] = dot(grad_ref[at : at + size], exit_ref[...], 1, 0).astype(narrow)
    attend_back_rows(out_grad, q_ref, k_ref, v_ref, log_ref, pg_ref, keys_sum, values_sum)
    turned = q_ref.shape[1] + k_ref.shape[1]
    gain_ref[...] = project_back_rows(
        pg_ref, mix_ref[...], tok_ref, cos_ref, sin_ref, part_ref, turned, size
    )


def totals(wire, t, first, third, zed, buffers, out_send, own_out, half_out):
    sources = (first, third, zed)
    for g in (1, 0):
        loads = [wire.near(ref.at[g], buffers.at[i]) for i, ref in enumerate(sources)]
        for load in loads:
            load.wait()
        total = buffers[0].astype(single) + buffers[1].astype(single) + buffers[2].astype(single)
        if g:
            out_send[...] = total.astype(narrow)
            wire.go(out_send, half_out, wire.to_half)
        else:
            buffers[0] = total.astype(narrow)
            wire.near(buffers.at[0], own_out).wait()


def backward_body(
    ba_ref, bo_ref, oa_ref, oo_ref, pickall_ref, tokall_ref, gg_ref, gu_ref, gd_ref,
    hid_ref, gain_ref, cot_ref, wall_ref, q_ref, k_ref, v_ref, log_ref, cos_ref, sin_ref,
    slot_ref, table_ref, otab_ref,
    pg_ref, part_ref, gsum_ref, hgrad_ref, layer_ref, lgrad_ref,
    ra_ref, mo_ref, ma_ref, grad_out, c1_ref, c3_ref, zb_ref, own_ref, hx_ref,
    ag, out_grad, keys_sum, values_sum, land_a, land_b, land_h, land_m, sums, own_rows, buffers, far,
    leave, passed, passing, values, pick, stage, route_own, route_send, land_r, quarters, land_q, logits,
    send, recv, local,
):
    wire = Wire(send, recv, local)
    s, groups = wire.s, wire.groups
    size = hid_ref.shape[0]
    q_width, k_width = q_ref.shape[1], k_ref.shape[1]
    mix_width = q_width + 2 * k_width
    terms = (gg_ref, gu_ref, gd_ref)
    wire.meet()

    middle = size // 2

    def scatter(source, landing):
        return wire.scatter(lambda j: source.at[s ^ j], landing)

    def scatter_on(keys, source, landing, which):
        loads = [
            wire.near(source.at[s ^ 2, pl.ds(0, middle)], passed.at[0]),
            wire.near(source.at[s ^ 1, pl.ds(middle, middle)], passed.at[1]),
        ]
        for load in loads:
            load.wait()
        wire.scatter_on(
            keys, landing, lambda j: passed[0 if j == 2 else 1].astype(single), passing.at[which]
        )

    def quarter_sends(source, landing):
        return [
            wire.go(source.at[s ^ j], landing.at[j - 1], wire.to_seq[j]) for j in range(1, groups)
        ]

    def fetch(source, b):
        loads = [wire.near(source, values)]
        if b is not None:
            loads.append(wire.near(pickall_ref.at[b], pick))
        for load in loads:
            load.wait()

    def combine(j):
        return dot(pick[:, j * size : (j + 1) * size], values[...], 0, 0).astype(narrow)

    def combine_out(target):
        for j in range(groups):
            stage[j] = combine(j)
        wire.near(stage, target).wait()

    core_go = []
    for t in range(3):
        core_go.append(
            (
                wire.go(terms[t].at[3], c3_ref.at[t], wire.to_core),
                wire.go(terms[t].at[1], c1_ref.at[t], wire.to_core),
            )
        )
    fetch(bo_ref, 1)
    combine_out(mo_ref)
    other_go = scatter(mo_ref, land_a)
    own_rows[0] = stage[s]
    z_go = []

    def send_far(t):
        wire.come(core_go[t][0])
        if t >= 2:
            wire.leave(z_go[t - 2])
        for g in (1, 0):
            loads = [
                wire.near(terms[t].at[2, g], buffers.at[0]),
                wire.near(c3_ref.at[t, g], buffers.at[1]),
            ]
            for load in loads:
                load.wait()
            far[t % 2, g] = (buffers[0].astype(single) + buffers[1].astype(single)).astype(narrow)
        z_go.append(wire.go(far.at[t % 2], zb_ref.at[t], wire.to_z))

    send_far(0)
    fetch(ba_ref, 0)
    combine_out(ra_ref)
    own_go = scatter(ra_ref, land_b)
    own_rows[1] = stage[s]
    scatter_on(other_go, mo_ref, land_a, 0)

    own_count = slot_ref.shape[0]
    slots = slot_ref.shape[1] // 2
    ids = own_ids(own_count, 2 * own_count)

    def route_rows(b, table):
        total = jnp.zeros((TOP, groups * size), single)
        for e in range(own_count):
            mine = pick[e * slots : (e + 1) * slots].astype(single)
            row = jnp.sum(mine * slot_ref[e, b * slots : (b + 1) * slots], axis=0, keepdims=True)
            total = total + jnp.where(table[0:TOP] == ids[e], row, 0.0)
        return total

    route_own[...] = route_rows(0, table_ref)
    fetch(oa_ref, None)
    combine_out(ma_ref)
    own_rows[3] = stage[s]
    total = wire.scatter_end(other_go, land_a, own_rows[0].astype(single))
    sums[...] = total.astype(narrow)
    half_go = wire.go(sums, land_h, wire.to_half)
    scatter_on(own_go, ra_ref, land_b, 1)
    send_far(1)
    for k in other_go:
        wire.leave(k)
    fetch(oo_ref, 1)
    combine_out(mo_ref)
    own_rows[2] = stage[s]
    route_send[...] = route_rows(1, otab_ref)
    route_go = wire.go(route_send, land_r, wire.to_half)
    total = wire.scatter_end(own_go, land_b, own_rows[1].astype(single))
    wire.come(half_go)
    total = total + land_h[...].astype(single)
    back, gain_two = norm_back(total, hid_ref[...], gain_ref[1:2])
    hidden_grad = cot_ref[...].astype(single) + back
    hgrad_ref[...] = hidden_grad
    ag[s] = hidden_grad.astype(narrow)
    grad_go = wire.gather(ag.at[s], ag)
    wire.come(route_go)
    total = route_own[...] + land_r[...]
    for j in range(groups):
        quarters[j] = total[:, j * size : (j + 1) * size]
        logits[j] = table_ref[TOP : 2 * TOP, j * size : (j + 1) * size]
    quarter_go = quarter_sends(quarters, land_q)

    def finish_term(t):
        wire.come(core_go[t][1], z_go[t])
        totals(
            wire, t, terms[t].at[0], c1_ref.at[t], zb_ref.at[t], buffers, leave.at[t],
            own_ref.at[t], hx_ref.at[t],
        )

    finish_term(0)
    wire.gather_on(grad_go, ag)
    send_far(2)
    tok_rows = values.at[pl.ds(0, groups * size)]
    load_tok = wire.near(tokall_ref, tok_rows)
    wire.gather_end(grad_go)
    moe_go = scatter(mo_ref, land_a)
    moe_own_go = scatter(ma_ref, land_b)
    keep_grad = wire.near(ag, grad_out)
    exit_own = wall_ref[:, mix_width : mix_width + q_width]
    for j in range(groups):
        out_grad[j * size : (j + 1) * size] = dot(ag[j], exit_own, 1, 0).astype(narrow)
    attend_back_rows(out_grad, q_ref, k_ref, v_ref, log_ref, pg_ref, keys_sum, values_sum)
    for k in other_go[4:] + own_go[4:]:
        wire.leave(k)
    scatter_on(moe_go, mo_ref, land_a, 0)
    scatter_on(moe_own_go, ma_ref, land_b, 1)
    finish_term(1)
    load_tok.wait()
    gain_one = project_back_rows(
        pg_ref, wall_ref[:, :mix_width], tok_rows, cos_ref, sin_ref, part_ref, q_width + k_width, size
    )
    gsum_ref[...] = jnp.concatenate([gain_one, gain_two, jnp.zeros((6, D), single)], axis=0)
    total = wire.scatter_end(moe_go, land_a, own_rows[2].astype(single))
    wire.leave(half_go)
    sums[...] = total.astype(narrow)
    moe_half_go = wire.go(sums, land_m, wire.to_half)
    wire.come(*quarter_go)
    route_grad = quarters[s]
    for j in range(groups - 1):
        route_grad = route_grad + land_q[j]
    top = logits[s]
    exponent = jnp.exp(top - jnp.max(top, axis=0, keepdims=True))
    gating = exponent / jnp.sum(exponent, axis=0, keepdims=True)
    lgrad_ref[...] = gating * (route_grad - jnp.sum(gating * route_grad, axis=0, keepdims=True))
    total = wire.scatter_end(moe_own_go, land_b, hid_ref[...] + own_rows[3].astype(single))
    wire.come(moe_half_go)
    layer_ref[...] = (total + land_m[...].astype(single)).astype(narrow)
    keep_grad.wait()
    wire.finish()


def backward_call(
    backs, outs, pick, terms, hidden, gains, cot, wall, q, k, v, logs, tokens_all,
    cos_table, sin_table, slot_grad, table, other_table,
):
    size = hidden.shape[0]
    seq_len = tokens_all.shape[0]
    groups = seq_len // size
    rings, halves, own, part, width = terms[0].shape
    slot_rows = pick.shape[1]
    shape = jax.ShapeDtypeStruct
    vmem = pl.BlockSpec(memory_space=pltpu.VMEM)
    hbm = pl.BlockSpec(memory_space=pl.ANY)
    block = (groups, size, D)
    mix_width = q.shape[1] + 2 * k.shape[1]
    landing = pltpu.VMEM((6, size // 2, D), narrow)
    route = pltpu.VMEM((TOP, seq_len), single)
    count = 72
    return pl.pallas_call(
        backward_body,
        in_specs=[hbm] * 9 + [vmem] * 13,
        out_specs=[vmem] * 6 + [hbm] * 9,
        out_shape=[
            shape((seq_len, mix_width), narrow),
            shape((seq_len, D), narrow),
            shape((8, D), single),
            shape((size, D), single),
            shape((size, D), narrow),
            shape((TOP, size), single),
            shape(block, narrow),
            shape(block, narrow),
            shape(block, narrow),
            shape(block, narrow),
            shape((3, halves, own, part, width), narrow),
            shape((3, halves, own, part, width), narrow),
            shape((3, halves, own, part, width), narrow),
            shape((2, own, part, width), narrow),
            shape((2, own, part, width), narrow),
        ],
        scratch_shapes=[
            pltpu.VMEM(block, narrow),
            pltpu.VMEM(q.shape, narrow),
            pltpu.VMEM((seq_len, HEAD_DIM), single),
            pltpu.VMEM((seq_len, HEAD_DIM), single),
            landing,
            landing,
            pltpu.VMEM((size, D), narrow),
            pltpu.VMEM((size, D), narrow),
            pltpu.VMEM((size, D), narrow),
            pltpu.VMEM((4, size, D), narrow),
            pltpu.VMEM((3, own, part, width), narrow),
            pltpu.VMEM((2, halves, own, part, width), narrow),
            pltpu.VMEM((2, own, part, width), narrow),
            pltpu.VMEM((2, size // 2, D), narrow),
            pltpu.VMEM((2, 2, size // 2, D), narrow),
            pltpu.VMEM((slot_rows, D), narrow),
            pltpu.VMEM((slot_rows, seq_len), narrow),
            pltpu.VMEM(block, narrow),
            route,
            route,
            route,
            pltpu.VMEM((groups, TOP, size), single),
            pltpu.VMEM((groups - 1, TOP, size), single),
            pltpu.VMEM((groups, TOP, size), single),
            pltpu.SemaphoreType.DMA((count,)),
            pltpu.SemaphoreType.DMA((count,)),
            pltpu.SemaphoreType.DMA((count,)),
        ],
        compiler_params=pltpu.CompilerParams(
            collective_id=1, has_side_effects=True, vmem_limit_bytes=67_000_000
        ),
        cost_estimate=pl.CostEstimate(
            flops=150_000_000_000, bytes_accessed=100_000_000, transcendentals=0
        ),
        name="backward_exchange",
    )(
        *backs, *outs, pick, tokens_all, *terms, hidden, gains, cot, wall, q, k, v, logs,
        cos_table, sin_table, slot_grad, table, other_table,
    )


def final_body(
    part_ref, gd_ref, c1_ref, zb_ref, grad_ref,
    normed_ref, pg_ref, att_ref, gsum_ref, gain_ref, hgrad_ref, tok_ref,
    tgrad_ref, attn_ref, own_ref, hx_ref,
    gw, r1, r2, r3, a2, a6, c4, fin, land_a, passed, passing, own_rows, agv, buffers, leave,
    send, recv, local,
):
    wire = Wire(send, recv, local)
    s, f, groups = wire.s, wire.f, wire.groups
    _, shards, few, width = gw.shape
    depth = groups * shards * few
    wire.meet()

    norm_go = wire.scatter(lambda j: part_ref.at[s ^ j], land_a)
    load_grad = wire.near(grad_ref, agv)
    middle = land_a.shape[1]
    loads = [
        wire.near(part_ref.at[s], own_rows),
        wire.near(part_ref.at[s ^ 2, pl.ds(0, middle)], passed.at[0]),
        wire.near(part_ref.at[s ^ 1, pl.ds(middle, middle)], passed.at[1]),
    ]
    totals(
        wire, 2, gd_ref.at[0], c1_ref.at[2], zb_ref.at[2], buffers, leave, own_ref, hx_ref
    )
    mix_width, q_width = pg_ref.shape[1], att_ref.shape[1]
    last = mix_width + q_width
    load_grad.wait()
    shape = (groups, shards, few)
    gw[:, :, :, :mix_width] = (
        dot(normed_ref[...], pg_ref[...], 0, 0).astype(narrow).reshape(shape + (mix_width,))
    )
    grads = agv[...].reshape(groups * agv.shape[1], D)
    gw[:, :, :, mix_width:last] = (
        dot(grads, att_ref[...], 0, 0).astype(narrow).reshape(shape + (q_width,))
    )
    gains = jnp.concatenate([gsum_ref[...], jnp.zeros((width - last - 8, D), single)], axis=0)
    gw[:, :, :, last:] = gains.T.astype(narrow).reshape(shape + (width - last,))
    core_go = [wire.go(gw.at[:, f ^ (m + 1)], r1.at[m // 2], wire.to_core) for m in (2, 6, 0, 4)]
    for load in loads:
        load.wait()
    wire.scatter_on(
        norm_go, land_a, lambda j: passed[0 if j == 2 else 1].astype(single), passing
    )
    wire.come(*core_go)

    def pair_sum(m):
        return gw[:, f ^ m].astype(single) + r1[m // 2].astype(single)

    a2[...] = pair_sum(2).astype(narrow)
    go_2 = wire.go(a2, r2.at[0], wire.to_z)
    a6[...] = pair_sum(6).astype(narrow)
    go_6 = wire.go(a6, r2.at[1], wire.to_z)
    wire.come(go_6)
    c4[...] = (pair_sum(4) + r2[1].astype(single)).astype(narrow)
    go_4 = wire.go(c4, r3, wire.to_half)
    total = wire.scatter_end(norm_go, land_a, own_rows[...].astype(single))
    back, _ = norm_back(total, tok_ref[...].astype(single), gain_ref[0:1])
    tgrad_ref[...] = hgrad_ref[...] + back
    wire.come(go_2, go_4)
    fin[...] = pair_sum(0) + r2[0].astype(single) + r3[...].astype(single)
    attn_ref[s] = fin[s]
    last_go = [wire.go(fin.at[s ^ j], attn_ref.at[s], wire.to_seq[j]) for j in range(1, groups)]
    wire.finish()


def final_call(part, term, c1, zb, grad_all, normed, pg, att, gsum, gains, hgrad, tok, few, width):
    size = tok.shape[0]
    seq_len = normed.shape[0]
    groups = seq_len // size
    _, halves, own, rows, units = term.shape
    shape = jax.ShapeDtypeStruct
    vmem = pl.BlockSpec(memory_space=pltpu.VMEM)
    hbm = pl.BlockSpec(memory_space=pl.ANY)
    block = (groups, size, D)
    slab = (groups, few, width)
    landing = pltpu.VMEM((6, size // 2, D), narrow)
    count = 32
    return pl.pallas_call(
        final_body,
        in_specs=[hbm] * 5 + [vmem] * 7,
        out_specs=[vmem] * 2 + [hbm] * 2,
        out_shape=[
            shape((size, D), single),
            shape(slab, single),
            shape((own, rows, units), narrow),
            shape((own, rows, units), narrow),
        ],
        scratch_shapes=[
            pltpu.VMEM((groups, 8, few, width), narrow),
            pltpu.VMEM((4,) + slab, narrow),
            pltpu.VMEM((2,) + slab, narrow),
            pltpu.VMEM(slab, narrow),
            pltpu.VMEM(slab, narrow),
            pltpu.VMEM(slab, narrow),
            pltpu.VMEM(slab, narrow),
            pltpu.VMEM(slab, single),
            landing,
            pltpu.VMEM((2, size // 2, D), narrow),
            pltpu.VMEM((2, size // 2, D), narrow),
            pltpu.VMEM((size, D), narrow),
            pltpu.VMEM(block, narrow),
            pltpu.VMEM((3, own, rows, units), narrow),
            pltpu.VMEM((own, rows, units), narrow),
            pltpu.SemaphoreType.DMA((count,)),
            pltpu.SemaphoreType.DMA((count,)),
            pltpu.SemaphoreType.DMA((count,)),
        ],
        compiler_params=pltpu.CompilerParams(collective_id=2, has_side_effects=True),
        cost_estimate=pl.CostEstimate(
            flops=50_000_000_000, bytes_accessed=100_000_000, transcendentals=0
        ),
        name="final_exchange",
    )(
        part.reshape(block), term, c1, zb, grad_all, normed, pg, att, gsum, gains, hgrad, tok,
    )


def attention_back_call(grads, exit_own, mixing_own, q, k, v, logs, tokens_all, cos_table, sin_table):
    seq_len = tokens_all.shape[0]
    shape = jax.ShapeDtypeStruct
    return pl.pallas_call(
        attention_back_body,
        out_shape=[
            shape((seq_len, mixing_own.shape[1]), narrow),
            shape((seq_len, D), narrow),
            shape((1, D), single),
        ],
        scratch_shapes=[
            pltpu.VMEM(q.shape, narrow),
            pltpu.VMEM((seq_len, HEAD_DIM), single),
            pltpu.VMEM((seq_len, HEAD_DIM), single),
        ],
        cost_estimate=pl.CostEstimate(
            flops=2 * seq_len * D * (mixing_own.shape[1] + q.shape[1])
            + 10 * seq_len**2 * q.shape[1] * 4,
            bytes_accessed=seq_len * D * 8, transcendentals=0,
        ),
        name="attention_backward",
    )(grads, exit_own, mixing_own, q, k, v, logs, tokens_all, cos_table, sin_table)


def project_rows(at, size, tok_rows, mix, gain_row, cos_ref, sin_ref, normed_ref, q_ref, k_ref, v_ref):
    rows = slice(at, at + size)
    q_width, k_width = q_ref.shape[1], k_ref.shape[1]
    values = tok_rows.astype(single)
    inverse = lax.rsqrt(jnp.mean(values * values, axis=-1, keepdims=True) + epsilon)
    normed = (values * inverse * gain_row).astype(narrow)
    normed_ref[rows] = normed
    projected = dot(normed, mix, 1, 0)
    width = q_width + k_width
    turned = rope(
        projected[:, :width], wide(cos_ref[rows], width), wide(sin_ref[rows], width)
    ).astype(narrow)
    q_ref[rows] = turned[:, :q_width]
    k_ref[rows] = turned[:, q_width:]
    v_ref[rows] = projected[:, width:].astype(narrow)


def attend_rows(q_ref, k_ref, v_ref, att_ref, log_ref):
    seq_len, k_width = k_ref.shape
    size = QROWS
    group_size = HEADS // KV_HEADS
    for kv in range(k_width // HEAD_DIM):
        lanes = slice(kv * HEAD_DIM, (kv + 1) * HEAD_DIM)
        for block in range(seq_len // size):
            at = block * size
            end = at + size
            queries = stacked(q_ref, at, kv, size)
            scores = key_scores(k_ref[:end, lanes], queries, at, size)
            top = jnp.max(scores, axis=0, keepdims=True)
            exponent = jnp.exp(scores - top)
            total = jnp.sum(exponent, axis=0, keepdims=True)
            soft = (exponent * (1.0 / total)).astype(narrow)
            log_ref[kv * (seq_len // size) + block] = top + jnp.log(total)
            out = dot(v_ref[:end, lanes], soft, 0, 0)
            for g in range(group_size):
                head = kv * group_size + g
                att_ref[at:end, head * HEAD_DIM : (head + 1) * HEAD_DIM] = (
                    out[:, g * size : (g + 1) * size].T.astype(narrow)
                )


class Wire:
    def __init__(self, send, recv, local):
        self.send, self.recv, self.local = send, recv, local
        self.remotes, self.landed, self.left, self.locals = [], [], [], 0
        s, h, r = lax.axis_index("seq"), lax.axis_index("half"), lax.axis_index("ring")
        groups = lax.axis_size("seq")
        self.s, self.h, self.r, self.f, self.groups = s, h, r, h * 4 + r, groups
        self.to_half, self.to_z, self.to_core = {"half": h ^ 1}, {"ring": r ^ 2}, {"ring": r ^ 1}
        self.to_seq = [{"seq": s ^ j} for j in range(groups)]

    def meet(self):
        barrier = pltpu.get_barrier_semaphore()
        peers = self.to_seq[1:] + [self.to_half, self.to_z, self.to_core]
        for peer in peers:
            pl.semaphore_signal(barrier, inc=1, device_id=peer, device_id_type=MESH)
        pl.semaphore_wait(barrier, len(peers))

    def go(self, source, target, peer):
        k = len(self.remotes)
        copy = pltpu.make_async_remote_copy(
            src_ref=source, dst_ref=target, send_sem=self.send.at[k], recv_sem=self.recv.at[k],
            device_id=peer, device_id_type=MESH,
        )
        copy.start()
        self.remotes.append(copy)
        self.landed.append(False)
        self.left.append(False)
        return k

    def by_core(self, *sends):
        keys = []
        made = []
        for source, target, peer in sends:
            k = len(self.remotes)
            copy = pltpu.make_async_remote_copy(
                src_ref=source, dst_ref=target, send_sem=self.send.at[k],
                recv_sem=self.recv.at[k], device_id=peer, device_id_type=MESH,
            )
            self.remotes.append(copy)
            self.landed.append(False)
            self.left.append(False)
            keys.append(k)
            made.append(copy)

        @pl.when(self.r % 2 == 0)
        def _():
            for copy in made:
                copy.start()

        @pl.when(self.r % 2 == 1)
        def _():
            for copy in reversed(made):
                copy.start()

        return keys

    def come(self, *which):
        for k in which:
            self.remotes[k].wait_recv()
            self.landed[k] = True

    def leave(self, k):
        if not self.left[k]:
            self.remotes[k].wait_send()
        self.left[k] = True

    def near(self, source, target):
        copy = pltpu.make_async_copy(source, target, self.local.at[self.locals])
        self.locals += 1
        copy.start()
        return copy

    def gather(self, source, target):
        s = self.s
        return [self.go(source, target.at[s], self.to_seq[j]) for j in (1, 2)]

    def gather_on(self, keys, target):
        s, middle = self.s, target.shape[1] // 2
        first, second = pl.ds(0, middle), pl.ds(middle, middle)
        self.come(keys[0])
        block = target.at[s ^ 1, first]
        keys.append(self.go(block, block, self.to_seq[2]))
        self.come(keys[1])
        block = target.at[s ^ 2, second]
        keys.append(self.go(block, block, self.to_seq[1]))

    def gather_end(self, keys):
        self.come(*keys[2:])

    def scatter(self, source, landing):
        middle = landing.shape[1]
        first, second = pl.ds(0, middle), pl.ds(middle, middle)
        return [
            self.go(source(3).at[first], landing.at[1], self.to_seq[1]),
            self.go(source(3).at[second], landing.at[3], self.to_seq[2]),
            self.go(source(1).at[first], landing.at[0], self.to_seq[1]),
            self.go(source(2).at[second], landing.at[2], self.to_seq[2]),
        ]

    def scatter_on(self, keys, landing, kept, passing):
        self.come(keys[0])
        passing[0] = (kept(2) + landing[1].astype(single)).astype(narrow)
        keys.append(self.go(passing.at[0], landing.at[4], self.to_seq[2]))
        self.come(keys[1])
        passing[1] = (kept(1) + landing[3].astype(single)).astype(narrow)
        keys.append(self.go(passing.at[1], landing.at[5], self.to_seq[1]))

    def scatter_end(self, keys, landing, own):
        self.come(*keys[2:])
        first = landing[0].astype(single) + landing[4].astype(single)
        second = landing[2].astype(single) + landing[5].astype(single)
        return own + jnp.concatenate([first, second], axis=0)

    def finish(self):
        for k, copy in enumerate(self.remotes):
            if not self.left[k]:
                copy.wait_send()
            if not self.landed[k]:
                copy.wait_recv()


def place_rows(table, ids, capacity, slots, pick_ref, share_ref, b):
    length = table.shape[1]
    picked, logits, order = table[0:TOP], table[TOP : 2 * TOP], table[2 * TOP : 2 * TOP + 1]
    exponent = jnp.exp(logits - jnp.max(logits, axis=0, keepdims=True))
    gating = exponent / jnp.sum(exponent, axis=0, keepdims=True)
    down = lax.broadcasted_iota(jnp.int32, (length, length), 0).astype(single)
    along = lax.broadcasted_iota(jnp.int32, (length, length), 1).astype(single)
    place_col = jnp.sum(jnp.where(order == down, along, 0.0), axis=1, keepdims=True)
    place_row = jnp.broadcast_to(place_col, (length, 128)).T[0:1]
    earlier = (place_col < place_row).astype(single).astype(narrow)
    hits = [jnp.sum((picked == i).astype(single), axis=0, keepdims=True) for i in ids]
    share = [
        jnp.sum(jnp.where(picked == i, gating, 0.0), axis=0, keepdims=True) for i in ids
    ]
    spare = jnp.zeros((8 - len(ids), length), single)
    rank = dot(jnp.concatenate(hits + [spare], axis=0).astype(narrow), earlier, 1, 0)
    slot_at = lax.broadcasted_iota(jnp.int32, (slots, length), 0).astype(single)
    for e in range(len(ids)):
        kept = (hits[e] > 0.0) & (rank[e : e + 1] < capacity)
        filled = jnp.where(kept, rank[e : e + 1], -1.0) == slot_at
        pick_ref[b, e * slots : (e + 1) * slots] = filled.astype(single).astype(narrow)
        share_ref[e, b * slots : (b + 1) * slots] = jnp.sum(
            jnp.where(filled, share[e], 0.0), axis=1, keepdims=True
        )


def own_ids(own, local_count):
    first = lax.axis_index("seq") * local_count + lax.axis_index("half") * own
    return [(first + e).astype(single) for e in range(own)]


def forward_body(
    tok_ref, pack_ref, cot_ref, wg_ref, wu_ref, wd_ref, cos_ref, sin_ref, table_ref,
    normed_ref, q_ref, k_ref, v_ref, att_ref, log_ref, hid_ref, gain_ref, share_ref, otab_ref,
    tokall_ref, wall_ref, pickall_ref, xa_ref, xo_ref, ya_ref, yo_ref, wout_ref,
    xown_ref, xother_ref, yown_ref, yother_ref,
    tokv, wv, part, landed, passing, xv, other_table, pick, picked_rows, send, recv, local,
):
    wire = Wire(send, recv, local)
    s, h, r, f, groups = wire.s, wire.h, wire.r, wire.f, wire.groups
    _, fsdp, few, width = wv.shape
    q_width, k_width = q_ref.shape[1], k_ref.shape[1]
    mix_width = q_width + 2 * k_width
    size = tok_ref.shape[0]
    middle = size // 2
    wire.meet()

    pack_go = [wire.go(pack_ref.at[s ^ j], wv.at[s, f], wire.to_seq[j]) for j in range(1, groups)]
    tok_go = wire.gather(tok_ref, tokv)
    table_go = wire.go(table_ref, other_table, wire.to_half)
    own_cot = wire.near(cot_ref, ya_ref.at[s])
    wv[s, f] = pack_ref[s]
    tokv[s] = tok_ref[...]

    sources = (wg_ref, wu_ref, wd_ref)

    def weights_first(t):
        own, other = sources[t].at[h], sources[t].at[1 - h]
        target = wout_ref.at[t, h, r]
        keys = wire.by_core((other, target, wire.to_half), (own, target, wire.to_z))
        wire.go(own, target, wire.to_core)
        return keys

    def weights_next(t, keys):
        wire.come(keys[0])
        came = wout_ref.at[t, 1 - h, r]
        on_z = wire.go(came, came, wire.to_z)
        wire.go(came, came, wire.to_core)
        wire.come(keys[1])
        beside = wout_ref.at[t, h, r ^ 2]
        wire.go(beside, beside, wire.to_core)
        return on_z

    def weights_last(t, key):
        wire.come(key)
        beyond = wout_ref.at[t, 1 - h, r ^ 2]
        wire.go(beyond, beyond, wire.to_core)

    wire.come(*pack_go)
    mine = wv.at[:, f]
    a_half = wire.go(mine, mine, wire.to_half)
    a_z = wire.go(mine, mine, wire.to_z)
    parts_go = [wire.go(mine, mine, wire.to_core)]
    wire.come(a_half)
    block = wv.at[:, f ^ 4]
    b_z = wire.go(block, block, wire.to_z)
    parts_go.append(wire.go(block, block, wire.to_core))
    wire.come(a_z)
    block = wv.at[:, f ^ 2]
    parts_go.append(wire.go(block, block, wire.to_core))
    cot_half = wire.go(cot_ref, yo_ref.at[s], wire.to_half)
    gate_first = weights_first(0)
    wire.gather_on(tok_go, tokv)
    cot_go = wire.gather(cot_ref, ya_ref)
    wire.come(b_z)
    block = wv.at[:, f ^ 6]
    parts_go.append(wire.go(block, block, wire.to_core))
    up_first = weights_first(1)

    own, slots = wout_ref.shape[3], share_ref.shape[1] // 2
    capacity = (groups * size * TOP + EXPERTS - 1) // EXPERTS
    ids = own_ids(own, 2 * own)
    place_rows(table_ref[...], ids, capacity, slots, pick, share_ref, 0)
    wire.gather_end(tok_go)
    wire.come(*parts_go)
    wire.gather_on(cot_go, ya_ref)
    keep_tok = wire.near(tokv, tokall_ref)
    keep_wall = wire.near(wv, wall_ref)
    depth = groups * fsdp * few
    gains = wv[:, :, :, mix_width + q_width :].reshape(depth, width - mix_width - q_width)
    gains = gains.astype(single).T[0:8]
    gain_ref[...] = gains
    for j in range(groups):
        project_rows(
            j * size, size, tokv[j], wv[:, :, :, :mix_width].reshape(depth, mix_width),
            gains[0:1], cos_ref, sin_ref, normed_ref, q_ref, k_ref, v_ref,
        )
    attend_rows(q_ref, k_ref, v_ref, att_ref, log_ref)
    exit_own = wv[:, :, :, mix_width : mix_width + q_width].reshape(depth, q_width)
    for j in (3, 1, 2, 0):
        rows = pl.ds(pl.multiple_of((s ^ j) * size, size), size)
        partial = dot(att_ref[rows], exit_own, 1, 1)
        if j:
            part[j - 1] = partial.astype(narrow)
        else:
            part_go = wire.scatter(lambda j: part.at[j - 1], landed)
            hid_ref[...] = tok_ref[...].astype(single) + partial

    def dispatch(b, source, target):
        wire.near(source, tokv).wait()
        whole = tokv[...].reshape(groups * size, D)
        for at in range(0, D, 512):
            picked_rows[:, at : at + 512] = dot(pick[b], whole[:, at : at + 512], 1, 0).astype(narrow)
        wire.near(picked_rows, target).wait()

    def kept(j):
        return part[j - 1, (0 if j == 2 else middle) : (middle if j == 2 else size)].astype(single)

    for k in tok_go[2:]:
        wire.leave(k)
    gate_next = weights_next(0, gate_first)
    wire.scatter_on(part_go, landed, kept, passing)
    keep_tok.wait()
    own_cot.wait()
    wire.gather_end(cot_go)
    dispatch(0, ya_ref, yown_ref)
    hidden = wire.scatter_end(part_go, landed, hid_ref[...])
    hid_ref[...] = hidden
    inverse = lax.rsqrt(jnp.mean(hidden * hidden, axis=-1, keepdims=True) + epsilon)
    xv[...] = (hidden * inverse * gains[1:2]).astype(narrow)
    row_half = wire.go(xv, xo_ref.at[s], wire.to_half)
    row_go = wire.gather(xv, xa_ref)
    own_row = wire.near(xv, xa_ref.at[s])
    down_first = weights_first(2)
    wire.come(table_go)
    otab_ref[...] = other_table[...]
    place_rows(other_table[...], ids, capacity, slots, pick, share_ref, 1)
    keep_pick = wire.near(pick, pickall_ref)
    wire.gather_on(row_go, xa_ref)
    wire.come(cot_half)
    up_next = weights_next(1, up_first)
    wire.come(row_half)
    other_go = wire.gather(xo_ref.at[s], xo_ref)
    cot_other = wire.gather(yo_ref.at[s], yo_ref)
    weights_last(0, gate_next)
    own_row.wait()
    wire.gather_end(row_go)
    dispatch(0, xa_ref, xown_ref)
    wire.gather_on(other_go, xo_ref)
    wire.gather_on(cot_other, yo_ref)
    down_next = weights_next(2, down_first)
    weights_last(1, up_next)
    wire.gather_end(other_go)
    dispatch(1, xo_ref, xother_ref)
    wire.gather_end(cot_other)
    dispatch(1, yo_ref, yother_ref)
    weights_last(2, down_next)
    keep_wall.wait()
    keep_pick.wait()
    wire.finish()


def forward_call(tokens, packed, cotangent, weights, cos_table, sin_table, table, q_width, k_width, slots):
    groups, few, width = packed.shape
    _, own, part, hidden_units = weights[0].shape
    size = tokens.shape[0]
    seq_len = size * groups
    blocks = k_width // HEAD_DIM * (seq_len // QROWS)
    shape = jax.ShapeDtypeStruct
    vmem = pl.BlockSpec(memory_space=pltpu.VMEM)
    hbm = pl.BlockSpec(memory_space=pl.ANY)
    rows = shape((groups, size, D), narrow)
    count = 80
    picked = shape((own * slots, D), narrow)
    return pl.pallas_call(
        forward_body,
        in_specs=[vmem] * 3 + [hbm] * 3 + [vmem] * 3,
        out_specs=[vmem] * 10 + [hbm] * 12,
        out_shape=[
            shape((seq_len, D), narrow),
            shape((seq_len, q_width), narrow),
            shape((seq_len, k_width), narrow),
            shape((seq_len, k_width), narrow),
            shape((seq_len, q_width), narrow),
            shape((blocks, 1, HEADS // KV_HEADS * QROWS), single),
            shape((size, D), single),
            shape((8, D), single),
            shape((own, 2 * slots, 1), single),
            shape(table.shape, single),
            rows,
            shape((groups, 8, few, width), narrow),
            shape((2, own * slots, seq_len), narrow),
            rows, rows, rows, rows,
            shape((3, 2, 4, own, part, hidden_units), narrow),
            picked, picked, picked, picked,
        ],
        scratch_shapes=[
            pltpu.VMEM((groups, size, D), narrow),
            pltpu.VMEM((groups, 8, few, width), narrow),
            pltpu.VMEM((groups - 1, size, D), narrow),
            pltpu.VMEM((6, size // 2, D), narrow),
            pltpu.VMEM((2, size // 2, D), narrow),
            pltpu.VMEM((size, D), narrow),
            pltpu.VMEM(table.shape, single),
            pltpu.VMEM((2, own * slots, seq_len), narrow),
            pltpu.VMEM((own * slots, D), narrow),
            pltpu.SemaphoreType.DMA((count,)),
            pltpu.SemaphoreType.DMA((count,)),
            pltpu.SemaphoreType.DMA((24,)),
        ],
        compiler_params=pltpu.CompilerParams(collective_id=0, has_side_effects=True),
        cost_estimate=pl.CostEstimate(
            flops=200_000_000_000, bytes_accessed=100_000_000, transcendentals=0
        ),
        name="forward_exchange",
    )(tokens, packed, cotangent, *weights, cos_table, sin_table, table)


def expert_body(
    batch, own_apart, where_ref, all_ref, g_ref, u_ref, d_ref, *refs,
):
    _, halves, rings, _, part, width = all_ref.shape
    pieces = halves * rings
    x_refs, y_refs, w_ref = refs[:batch], refs[batch : 2 * batch], refs[2 * batch]
    refs = refs[2 * batch + 1 :]
    out_refs, row_refs, slot_ref = refs[:batch], refs[batch : 2 * batch], refs[2 * batch]
    gg_ref, gu_ref, gd_ref, held, sems = refs[2 * batch + 1 :]
    half, ring = where_ref[0], where_ref[1]
    e = pl.program_id(0)
    slot = lax.rem(e, 2)

    def each(expert, slot, act):
        for t, own_ref in enumerate((g_ref, u_ref, d_ref)):
            for g in range(halves):
                for r in range(rings):
                    at = g * rings + r
                    target, sem = held.at[slot, t, at], sems.at[slot, t, at]
                    if not own_apart:
                        act(pltpu.make_async_copy(all_ref.at[t, g, r, expert], target, sem))
                        continue
                    own = (half == g) & (ring == r)

                    @pl.when(own)
                    def _():
                        act(pltpu.make_async_copy(own_ref.at[g, expert], target, sem))

                    @pl.when(jnp.logical_not(own))
                    def _():
                        act(pltpu.make_async_copy(all_ref.at[t, g, r, expert], target, sem))

    @pl.when(e == 0)
    def _():
        each(e, slot, lambda copy: copy.start())

    @pl.when(e + 1 < pl.num_programs(0))
    def _():
        each(e + 1, 1 - slot, lambda copy: copy.start())

    for t in range(3):
        for at in range(pieces):
            pltpu.make_async_copy(
                all_ref.at[t, at // rings, at % rings, e], held.at[slot, t, at], sems.at[slot, t, at]
            ).wait()

    def weight(t):
        return held[slot, t].reshape(pieces * part, width)

    def write(ref, value):
        for g in range(halves):
            for r in range(rings):
                at = (g * rings + r) * part
                ref[r ^ ring if own_apart else r, g ^ half, 0] = value[at : at + part].astype(ref.dtype)

    slots = x_refs[0].shape[1]

    def split(outs, value):
        for b, ref in enumerate(outs):
            ref[0] = value[b * slots : (b + 1) * slots].astype(ref.dtype)

    rows = jnp.concatenate([ref[0] for ref in x_refs], axis=0)
    cots = jnp.concatenate([ref[0] for ref in y_refs], axis=0)
    share = w_ref[0]
    gate, up, down = weight(0), weight(1), weight(2)
    gate_pre = dot(rows, gate, 1, 0)
    up_pre = dot(rows, up, 1, 0)
    sig = jax.nn.sigmoid(gate_pre)
    mid = (gate_pre * sig * up_pre).astype(narrow)
    expert_out = dot(mid, down, 1, 1)
    cot_float = cots.astype(single)
    slot_ref[0] = jnp.sum(cot_float * expert_out, axis=-1, keepdims=True)
    split(out_refs, expert_out * share)
    out_low = (cot_float * share).astype(narrow)
    mid_grad = dot(out_low, down, 1, 0)
    write(gd_ref, dot(out_low, mid, 0, 0))
    gate_grad = (mid_grad * up_pre * sig * (1.0 + gate_pre * (1.0 - sig))).astype(narrow)
    up_grad = (mid_grad * gate_pre * sig).astype(narrow)
    split(row_refs, dot(gate_grad, gate, 1, 1) + dot(up_grad, up, 1, 1))
    write(gg_ref, dot(rows, gate_grad, 0, 0))
    write(gu_ref, dot(rows, up_grad, 0, 0))


def expert_call(where, gathered, weights, own_apart, rows, cots, share):
    _, halves, rings, own, part, width = gathered.shape
    batch = len(rows)
    _, slots, depth = rows[0].shape
    pieces = halves * rings
    weight_spec = pl.BlockSpec((rings, halves, 1, part, width), lambda e, h: (0, 0, e, 0, 0))
    row_spec = pl.BlockSpec((1, slots, depth), lambda e, h: (e, 0, 0))
    share_spec = pl.BlockSpec((1, batch * slots, 1), lambda e, h: (e, 0, 0))
    shape = jax.ShapeDtypeStruct
    row_shape = shape((own, slots, depth), narrow)
    outs = pl.pallas_call(
        functools.partial(expert_body, batch, own_apart),
        grid_spec=pltpu.PrefetchScalarGridSpec(
            num_scalar_prefetch=1,
            grid=(own,),
            in_specs=[pl.BlockSpec(memory_space=pl.ANY)] * 4
            + [row_spec] * (2 * batch)
            + [share_spec],
            out_specs=[row_spec] * (2 * batch) + [share_spec] + [weight_spec] * 3,
            scratch_shapes=[
                pltpu.VMEM((2, 3, pieces, part, width), narrow),
                pltpu.SemaphoreType.DMA((2, 3, pieces)),
            ],
        ),
        out_shape=[row_shape] * (2 * batch)
        + [shape((own, batch * slots, 1), single)]
        + [shape((rings, halves, own, part, width), narrow)] * 3,
        cost_estimate=pl.CostEstimate(
            flops=9 * 2 * own * batch * slots * depth * width,
            bytes_accessed=12 * own * depth * width + 8 * batch * own * slots * depth,
            transcendentals=0,
        ),
        name="expert_ffn",
    )(where, gathered, *weights, *rows, *cots, share)
    return outs[:batch], outs[batch : 2 * batch], outs[2 * batch], outs[2 * batch + 1 :]


def local(
    halves, rings,
    tokens, mixing_weight, output_weight, norm_gains, expert_gate, expert_up, expert_down,
    gate_logits, routes, fill_order, cotangent,
):
    groups = lax.axis_size("seq")
    column = lax.axis_index("seq")
    half = lax.axis_index("half")
    ring = lax.axis_index("ring")
    paired = halves == 2
    tok_rows = tokens.shape[1]
    seq_len = tok_rows * groups
    capacity = (seq_len * TOP + EXPERTS - 1) // EXPERTS
    local_count = expert_gate.shape[1]
    own_count = local_count // halves
    part = expert_gate.shape[0]
    fsdp_rows = mixing_weight.shape[0]
    q_width = HEADS * HEAD_DIM // groups
    k_width = KV_HEADS * HEAD_DIM // groups
    mix_width = q_width + 2 * k_width
    own_kv = KV_HEADS // groups
    own_heads = HEADS // groups
    group_size = HEADS // KV_HEADS
    score_scale = 1.0 / math.sqrt(HEAD_DIM)
    query_all = HEADS * HEAD_DIM
    key_all = KV_HEADS * HEAD_DIM

    def gather_seq(value):
        parts = [value] + [swap(value, "seq", j, groups) for j in range(1, groups)]
        whole = jnp.zeros((groups,) + value.shape, value.dtype)
        for j, item in enumerate(parts):
            whole = lax.dynamic_update_index_in_dim(whole, item, column ^ j, 0)
        return whole.reshape((seq_len,) + value.shape[1:])

    def scatter_seq(value):
        blocks = value.reshape((groups, tok_rows) + value.shape[1:])
        total = lax.dynamic_index_in_dim(blocks, column, 0, False).astype(single)
        for j in range(1, groups):
            sent = lax.dynamic_index_in_dim(blocks, column ^ j, 0, False).astype(narrow)
            total = total + swap(sent, "seq", j, groups).astype(single)
        return total

    def exchange_seq(blocks):
        whole = lax.dynamic_update_index_in_dim(
            jnp.zeros_like(blocks), lax.dynamic_index_in_dim(blocks, column, 0, False), column, 0
        )
        for j in range(1, groups):
            sent = lax.dynamic_index_in_dim(blocks, column ^ j, 0, False)
            whole = lax.dynamic_update_index_in_dim(
                whole, swap(sent, "seq", j, groups), column ^ j, 0
            )
        return whole

    packed = jnp.concatenate(
        [
            mixing_weight[:, :query_all].reshape(fsdp_rows, groups, q_width),
            mixing_weight[:, query_all : query_all + key_all].reshape(fsdp_rows, groups, k_width),
            mixing_weight[:, query_all + key_all :].reshape(fsdp_rows, groups, k_width),
            output_weight.reshape(fsdp_rows, groups, q_width),
            jnp.broadcast_to(
                jnp.pad(norm_gains, ((0, 0), (0, PAD - 2)))[:, None], (fsdp_rows, groups, PAD)
            ),
        ],
        2,
    ).transpose(1, 0, 2)
    cos_table, sin_table = rotary_tables(jnp.arange(seq_len, dtype=jnp.int32))
    cos_table, sin_table = jnp.tile(cos_table, (1, 2)), jnp.tile(sin_table, (1, 2))
    own_weights = [
        item.transpose(1, 0, 2).reshape(halves, own_count, part, FF)
        for item in (expert_gate, expert_up, expert_down)
    ]
    inputs = tokens[0].astype(single)
    slots = (capacity + 15) // 16 * 16
    if paired:
        table = jnp.concatenate(
            [
                routes[0].astype(single).T,
                gate_logits[0].T,
                jnp.broadcast_to(fill_order[0].astype(single), (8, seq_len)),
            ],
            0,
        )
        (
            normed_low, queries, keys, values, attended, logs, hidden, gains_float, share,
            other_table, tokens_all, packed, pick, _, _, _, _, gathered,
            own_x, other_x, own_y, other_y,
        ) = forward_call(
            tokens[0], packed, cotangent[0], own_weights, cos_table, sin_table, table,
            q_width, k_width, slots,
        )
        tokens_all = tokens_all.reshape(seq_len, D)
        packed = packed.reshape(D, -1)
        mixing_own = packed[:, :mix_width]
        exit_own = packed[:, mix_width : mix_width + q_width]
        seq_rows = [item.reshape(own_count, slots, D) for item in (own_x, other_x)]
        cot_rows = [item.reshape(own_count, slots, D) for item in (own_y, other_y)]
    else:
        packed = exchange_seq(packed)
        packed = lax.all_gather(packed, ("half", "ring"), axis=0, tiled=False)
        packed = packed.transpose(1, 0, 2, 3).reshape(D, -1)
        mixing_own = packed[:, :mix_width]
        exit_own = packed[:, mix_width : mix_width + q_width]
        gains_float = packed[:, mix_width + q_width : mix_width + q_width + 2].astype(single).T
        tokens_all = gather_seq(tokens[0])
        gathered = jnp.stack(
            [lax.all_gather(item[0], "ring", axis=0, tiled=False)[None] for item in own_weights]
        )
        normed_low, queries, keys, values, attended, logs, attn_part = attention_call(
            tokens_all, mixing_own, exit_own, gains_float, cos_table, sin_table
        )
        hidden = inputs + scatter_seq(attn_part)
        scale_two = lax.rsqrt(jnp.mean(hidden * hidden, axis=-1, keepdims=True) + epsilon)
        seq_rows = [gather_seq((hidden * scale_two * gains_float[1]).astype(narrow))]
        cot_rows = [gather_seq(cotangent[0])]

    if not paired:
        pair_routes = routes
        pair_order = fill_order
        pair_gating = softmax_last(gate_logits)
        expert_ids = column * local_count + half * own_count + jnp.arange(own_count, dtype=jnp.int32)
        places = jnp.arange(seq_len, dtype=jnp.int32)
        chosen = (pair_routes[..., None] == expert_ids).astype(single)
        hits = jnp.sum(chosen, axis=2)
        token_weight = jnp.sum(pair_gating[..., None] * chosen, axis=2)
        place_of = jnp.sum(
            jnp.where(pair_order[:, :, None] == places, places[None, :, None], 0), axis=1
        )
        earlier = (place_of[:, None, :] < place_of[:, :, None]).astype(narrow)
        rank = jnp.einsum(
            "btu,bue->bte", earlier, hits.astype(narrow), preferred_element_type=single
        ).astype(jnp.int32)
        kept = (hits > 0) & (rank < capacity)
        flat_place = jnp.where(kept, rank + jnp.arange(own_count, dtype=jnp.int32) * slots, -1)
        flat_ids = jnp.arange(own_count * slots, dtype=jnp.int32)
        filled = flat_place[:, :, 0:1] == flat_ids
        for e in range(1, own_count):
            filled = filled | (flat_place[:, :, e : e + 1] == flat_ids)
        select = filled.astype(narrow)
        batch = select.shape[0]
        match = flat_place[:, :, :, None] == (
            jnp.arange(own_count, dtype=jnp.int32)[:, None] * slots
            + jnp.arange(slots, dtype=jnp.int32)[None, :]
        )
        slot_weight = jnp.sum(jnp.where(match, token_weight[..., None], 0.0), axis=1)
        share = slot_weight.transpose(1, 0, 2).reshape(own_count, batch * slots, 1)

        def dispatch(rows):
            return [
                lax.dot_general(
                    select[b], item, (((0,), (0,)), ((), ())), preferred_element_type=narrow
                ).reshape(own_count, slots, D)
                for b, item in enumerate(rows)
            ]

        def combine(b, values):
            return lax.dot_general(
                select[b],
                values.reshape(own_count * slots, D),
                (((1,), (0,)), ((), ())),
                preferred_element_type=narrow,
            )

        seq_rows, cot_rows = dispatch(seq_rows), dispatch(cot_rows)

    slot_out, slot_back, slot_grad, (gate_term, up_term, down_term) = expert_call(
        jnp.stack([half, ring]), gathered, own_weights, paired,
        seq_rows, cot_rows, share,
    )
    def by_row(total):
        return total.reshape(local_count, part, FF).transpose(1, 0, 2).astype(single)

    if paired:
        flat = (own_count * slots, D)
        (
            projected_grad, normed_part, gain_sums, hidden_grad, layer_output, logits_rows,
            _, _, _, attn_grad_all, c1, c3, zb, own_terms, other_terms,
        ) = backward_call(
            [item.reshape(flat) for item in slot_back], [item.reshape(flat) for item in slot_out],
            pick, (gate_term, up_term, down_term), hidden, gains_float, cotangent[0], packed,
            queries, keys, values, logs, tokens_all, cos_table, sin_table, slot_grad, table,
            other_table,
        )
        logits_rows = logits_rows.T
        tokens_gradient, attn_total, own_last, other_last = final_call(
            normed_part, down_term, c1, zb, attn_grad_all, normed_low, projected_grad, attended,
            gain_sums, gains_float, hidden_grad, tokens[0], fsdp_rows, packed.shape[1],
        )
        tokens_gradient, layer_output = tokens_gradient[None], layer_output[None]

        def expert_gradient(own, other):
            return by_row(
                jnp.stack([jnp.where(half == 0, own, other), jnp.where(half == 0, other, own)])
            )

        gate_gradient = expert_gradient(own_terms[0], other_terms[0])
        up_gradient = expert_gradient(own_terms[1], other_terms[1])
        down_gradient = expert_gradient(own_last, other_last)
    else:
        slot_grad = slot_grad.reshape(own_count, batch, slots).transpose(1, 0, 2)
        weight_grad_tok = jnp.sum(jnp.where(match, slot_grad[:, None], 0.0), axis=3)
        route_part = jnp.sum(weight_grad_tok[:, :, None, :] * chosen, axis=-1)

        def send_routes(value):
            blocks = value.reshape(groups, tok_rows, TOP)
            total = lax.dynamic_index_in_dim(blocks, column, 0, False)
            for j in range(1, groups):
                sent = lax.dynamic_index_in_dim(blocks, column ^ j, 0, False)
                total = total + swap(sent, "seq", j, groups)
            return total

        route_grad = send_routes(route_part[0])
        gating = softmax_last(
            lax.dynamic_slice_in_dim(gate_logits[0], column * tok_rows, tok_rows, 0)
        )
        logits_rows = gating * (route_grad - jnp.sum(gating * route_grad, axis=-1, keepdims=True))

        def ring_sum(term):
            return lax.psum_scatter(term, "ring", scatter_dimension=0, tiled=False)

        normed_two_grad = scatter_seq(combine(0, slot_back[0]))
        gate_gradient, up_gradient, down_gradient = [
            by_row(ring_sum(term)) for term in (gate_term, up_term, down_term)
        ]
        moe_rows = scatter_seq(combine(0, slot_out[0]))
        layer_output = (hidden + moe_rows).astype(narrow)[None]
        back, gain_two_grad = norm_back(normed_two_grad, hidden, gains_float[1])
        hidden_grad = cotangent[0].astype(single) + back
        attn_grad_all = gather_seq(hidden_grad.astype(narrow))
        projected_grad, normed_part, gain_one_grad = attention_back_call(
            attn_grad_all, exit_own, mixing_own, queries, keys, values, logs, tokens_all,
            cos_table, sin_table,
        )
        mixing_term = dot(normed_low, projected_grad, 0, 0)
        output_term = dot(attn_grad_all, attended, 0, 0)
        gains_term = jnp.stack([gain_one_grad[0], gain_two_grad[0]], 1)
        gains_term = jnp.pad(gains_term, ((0, 0), (0, PAD - 2)))
        attn_term = jnp.concatenate([mixing_term, output_term, gains_term], 1).astype(narrow)
        attn_term = attn_term.reshape(groups, halves * rings, fsdp_rows, -1).transpose(1, 0, 2, 3)
        attn_total = lax.psum_scatter(attn_term, ("half", "ring"), scatter_dimension=0, tiled=False)
        attn_total = exchange_seq(attn_total).astype(single)
        back, _ = norm_back(scatter_seq(normed_part), inputs, gains_float[0])
        tokens_gradient = (hidden_grad + back)[None]

    def columns(first, width):
        return attn_total[:, :, first : first + width].transpose(1, 0, 2).reshape(fsdp_rows, -1)

    mixing_gradient = jnp.concatenate(
        [
            columns(0, q_width),
            columns(q_width, k_width),
            columns(q_width + k_width, k_width),
        ],
        1,
    )
    output_gradient = columns(mix_width, q_width)
    gains_gradient = jnp.sum(attn_total[:, :, mix_width + q_width :][:, :, :2], axis=0)

    return (
        layer_output,
        tokens_gradient,
        mixing_gradient,
        output_gradient,
        gains_gradient,
        gate_gradient,
        up_gradient,
        down_gradient,
        logits_rows[None],
    )


def solution(mesh):
    groups, shards = mesh.shape["seq"], mesh.shape["fsdp"]
    halves = 2 if (EXPERTS // groups) % 2 == 0 and (groups, shards) == (4, 8) else 1
    rings = shards // halves
    grid = Mesh(mesh.devices.reshape(groups, halves, rings), ("seq", "half", "ring"))
    fsdp = ("half", "ring")
    every = ("seq", "half", "ring")
    in_specs = (
        P(fsdp, "seq", None),
        P(every, None),
        P(every, None),
        P(every, None),
        P(fsdp, "seq", None),
        P(fsdp, "seq", None),
        P(fsdp, "seq", None),
        P(fsdp, None, None),
        P(fsdp, None, None),
        P(fsdp, None),
        P(fsdp, "seq", None),
    )
    out_specs = (
        P(fsdp, "seq", None),
        P(fsdp, "seq", None),
        P(every, None),
        P(every, None),
        P(every, None),
        P(fsdp, "seq", None),
        P(fsdp, "seq", None),
        P(fsdp, "seq", None),
        P(fsdp, "seq", None),
    )
    return jax.shard_map(
        functools.partial(local, halves, rings),
        mesh=grid,
        in_specs=in_specs,
        out_specs=out_specs,
        check_vma=False,
    )
```

```python
import functools
import math

import jax
import jax.numpy as jnp
import numpy as np
from jax import lax
from jax.experimental import pallas as pl
from jax.experimental.pallas import tpu as pltpu
from jax.sharding import Mesh
from jax.sharding import PartitionSpec as P

D = 1536
HEADS = 24
KV_HEADS = 8
HEAD_DIM = 64
FF = 512
EXPERTS = 40
TOP = 8
QROWS = 256
PAD = 128

epsilon = 1e-05
rope_base = 10000.0
single = jnp.float32
narrow = jnp.bfloat16
MESH = pl.DeviceIdType.MESH


def rotary_tables(positions):
    half_width = HEAD_DIM // 2
    frequency = rope_base ** (-2.0 * jnp.arange(half_width, dtype=single) / HEAD_DIM)
    angles = positions.astype(single)[:, None] * frequency[None, :]
    cos_table = jnp.cos(angles)
    sin_table = jnp.sin(angles)
    return (jnp.concatenate([cos_table, cos_table], 1), jnp.concatenate([sin_table, sin_table], 1))


def softmax_last(logit_rows):
    row_max = jnp.max(logit_rows, axis=-1, keepdims=True)
    exponent = jnp.exp(logit_rows - row_max)
    return exponent / jnp.sum(exponent, axis=-1, keepdims=True)


def swap(value, axis, step, size):
    return lax.ppermute(value, axis, [(i, i ^ step) for i in range(size)])


def dot(left, right, left_dim, right_dim):
    return lax.dot_general(
        left, right, (((left_dim,), (right_dim,)), ((), ())), preferred_element_type=single
    )


def rope(values, cos_row, sin_row):
    width = values.shape[-1]
    lane = lax.broadcasted_iota(jnp.int32, values.shape, 1) % HEAD_DIM
    turned = jnp.where(
        lane < HEAD_DIM // 2,
        -pltpu.roll(values, width - HEAD_DIM // 2, 1),
        pltpu.roll(values, HEAD_DIM // 2, 1),
    )
    return values * cos_row + turned * sin_row


def rope_back(values, cos_row, sin_row):
    width = values.shape[-1]
    lane = lax.broadcasted_iota(jnp.int32, values.shape, 1) % HEAD_DIM
    scaled = values * sin_row
    turned = jnp.where(
        lane < HEAD_DIM // 2,
        pltpu.roll(scaled, width - HEAD_DIM // 2, 1),
        -pltpu.roll(scaled, HEAD_DIM // 2, 1),
    )
    return values * cos_row + turned


def wide(table, width):
    return jnp.concatenate([table] * (width // table.shape[1]), axis=1)


def stacked(ref, at, kv, size):
    group_size = HEADS // KV_HEADS
    return jnp.concatenate(
        [
            ref[at : at + size, (kv * group_size + g) * HEAD_DIM : (kv * group_size + g + 1) * HEAD_DIM]
            for g in range(group_size)
        ],
        axis=0,
    )


def key_scores(keys, queries, at, size):
    scores = dot(keys, queries, 1, 1) * (1.0 / math.sqrt(HEAD_DIM))
    shape = scores.shape
    key_at = lax.broadcasted_iota(jnp.int32, shape, 0)
    query_at = lax.broadcasted_iota(jnp.int32, shape, 1) % size + at
    return jnp.where(key_at <= query_at, scores, -jnp.inf)


def attention_body(
    tok_ref, mix_ref, exit_ref, gain_ref, cos_ref, sin_ref,
    normed_ref, q_ref, k_ref, v_ref, att_ref, log_ref, part_ref,
):
    seq_len = tok_ref.shape[0]
    size = QROWS
    for at in range(0, seq_len, size):
        project_rows(
            at, size, tok_ref[at : at + size], mix_ref[...], gain_ref[0:1],
            cos_ref, sin_ref, normed_ref, q_ref, k_ref, v_ref,
        )
    attend_rows(q_ref, k_ref, v_ref, att_ref, log_ref)
    for at in range(0, seq_len, size):
        part_ref[at : at + size] = dot(att_ref[at : at + size], exit_ref[...], 1, 1).astype(narrow)


def attention_call(tokens_all, mixing_own, exit_own, gains, cos_table, sin_table):
    seq_len = tokens_all.shape[0]
    q_width = exit_own.shape[1]
    k_width = (mixing_own.shape[1] - q_width) // 2
    group_size = HEADS // KV_HEADS
    blocks = k_width // HEAD_DIM * (seq_len // QROWS)
    shape = jax.ShapeDtypeStruct
    return pl.pallas_call(
        attention_body,
        out_shape=[
            shape((seq_len, D), narrow),
            shape((seq_len, q_width), narrow),
            shape((seq_len, k_width), narrow),
            shape((seq_len, k_width), narrow),
            shape((seq_len, q_width), narrow),
            shape((blocks, 1, group_size * QROWS), single),
            shape((seq_len, D), narrow),
        ],
        cost_estimate=pl.CostEstimate(
            flops=2 * seq_len * D * (mixing_own.shape[1] + q_width) + 4 * seq_len**2 * q_width * 4,
            bytes_accessed=seq_len * D * 6, transcendentals=0,
        ),
        name="attention_forward",
    )(tokens_all, mixing_own, exit_own, gains, cos_table, sin_table)


def norm_back(grads, values, gain_row):
    inverse = lax.rsqrt(jnp.mean(values * values, axis=-1, keepdims=True) + epsilon)
    normal = values * inverse
    scaled = grads * gain_row
    back = inverse * (scaled - normal * jnp.mean(scaled * normal, axis=-1, keepdims=True))
    return back, jnp.sum(grads * normal, axis=0, keepdims=True)


def attend_back_rows(out_grad, q_ref, k_ref, v_ref, log_ref, pg_ref, keys_sum, values_sum):
    seq_len, k_width = k_ref.shape
    q_width = q_ref.shape[1]
    size = QROWS
    group_size = HEADS // KV_HEADS
    scale = 1.0 / math.sqrt(HEAD_DIM)
    for kv in range(k_width // HEAD_DIM):
        lanes = slice(kv * HEAD_DIM, (kv + 1) * HEAD_DIM)
        keys_sum[...] = jnp.zeros_like(keys_sum)
        values_sum[...] = jnp.zeros_like(values_sum)
        for block in range(seq_len // size):
            at = block * size
            end = at + size
            queries = stacked(q_ref, at, kv, size)
            grads = stacked(out_grad, at, kv, size)
            keys, values = k_ref[:end, lanes], v_ref[:end, lanes]
            scores = key_scores(keys, queries, at, size)
            soft = jnp.exp(scores - log_ref[kv * (seq_len // size) + block])
            values_sum[:end] += dot(soft.astype(narrow), grads, 1, 0)
            soft_grad = dot(values, grads, 1, 1)
            delta = jnp.sum(soft * soft_grad, axis=0, keepdims=True)
            scores_grad = (soft * (soft_grad - delta)).astype(narrow)
            keys_sum[:end] += dot(scores_grad, queries, 1, 0) * scale
            query_grad = dot(keys, scores_grad, 0, 0) * scale
            for g in range(group_size):
                head = kv * group_size + g
                pg_ref[at:end, head * HEAD_DIM : (head + 1) * HEAD_DIM] = (
                    query_grad[:, g * size : (g + 1) * size].T.astype(narrow)
                )
        first = q_width + kv * HEAD_DIM
        pg_ref[:, first : first + HEAD_DIM] = keys_sum[...].astype(narrow)
        first += k_width
        pg_ref[:, first : first + HEAD_DIM] = values_sum[...].astype(narrow)


def project_back_rows(pg_ref, mix_ref, tok_ref, cos_ref, sin_ref, part_ref, turned, size):
    gain = jnp.zeros((1, D), single)
    for at in range(0, tok_ref.shape[0], size):
        rows = slice(at, at + size)
        pg_ref[rows, :turned] = rope_back(
            pg_ref[rows, :turned].astype(single), wide(cos_ref[rows], turned),
            wide(sin_ref[rows], turned),
        ).astype(narrow)
        normed_part = dot(pg_ref[rows], mix_ref, 1, 1)
        if len(part_ref.shape) == 3:
            part_ref[at // size] = normed_part.astype(narrow)
        else:
            part_ref[rows] = normed_part.astype(narrow)
        values = tok_ref[rows].astype(single)
        inverse = lax.rsqrt(jnp.mean(values * values, axis=-1, keepdims=True) + epsilon)
        gain = gain + jnp.sum(normed_part * (values * inverse), axis=0, keepdims=True)
    return gain


def attention_back_body(
    grad_ref, exit_ref, mix_ref, q_ref, k_ref, v_ref, log_ref, tok_ref, cos_ref, sin_ref,
    pg_ref, part_ref, gain_ref,
    out_grad, keys_sum, values_sum,
):
    size = QROWS
    for at in range(0, tok_ref.shape[0], size):
        out_grad[at : at + size] = dot(grad_ref[at : at + size], exit_ref[...], 1, 0).astype(narrow)
    attend_back_rows(out_grad, q_ref, k_ref, v_ref, log_ref, pg_ref, keys_sum, values_sum)
    turned = q_ref.shape[1] + k_ref.shape[1]
    gain_ref[...] = project_back_rows(
        pg_ref, mix_ref[...], tok_ref, cos_ref, sin_ref, part_ref, turned, size
    )


def totals(wire, first, third, zed, buffers, out_send, own_out, half_out):
    sources = (first, third, zed)
    for g in (1, 0):
        loads = [wire.near(ref.at[g], buffers.at[i]) for i, ref in enumerate(sources)]
        for load in loads:
            load.wait()
        total = buffers[0].astype(single) + buffers[1].astype(single) + buffers[2].astype(single)
        if g:
            out_send[...] = total.astype(narrow)
            wire.go(out_send, half_out, wire.to_half)
        else:
            buffers[0] = total.astype(narrow)
            wire.near(buffers.at[0], own_out).wait()


def backward_body(
    ba_ref, bo_ref, oa_ref, oo_ref, pickall_ref, tokall_ref, normed_ref, gg_ref, gu_ref, gd_ref,
    tok_ref, att_ref, hid_ref, gain_ref, cot_ref, wall_ref, q_ref, k_ref, v_ref, log_ref, cos_ref, sin_ref,
    slot_ref, table_ref, otab_ref,
    tgrad_ref, layer_ref, lgrad_ref, attn_ref,
    ra_ref, mo_ref, ma_ref, c1_ref, c3_ref, zb_ref, own_ref, hx_ref,
    pg_ref, free, gw, r1, r2, r3, fin, attn_in,
    ag, out_grad, keys_sum, values_sum, land_a, land_b, land_h, land_m, sums, own_rows, buffers, far,
    leave, passed, passing, values, pick, stage, route_own, route_send, land_r, quarters, land_q, logits,
    send, recv, local,
):
    wire = Wire(send, recv, local)
    s, groups = wire.s, wire.groups
    size = hid_ref.shape[0]
    q_width, k_width = q_ref.shape[1], k_ref.shape[1]
    mix_width = q_width + 2 * k_width
    terms = (gg_ref, gu_ref, gd_ref)
    wire.meet()

    middle = size // 2

    def scatter(source, landing):
        return wire.scatter(lambda j: source.at[s ^ j], landing)

    def scatter_on(keys, source, landing, which):
        loads = [
            wire.near(source.at[s ^ 2, pl.ds(0, middle)], passed.at[0]),
            wire.near(source.at[s ^ 1, pl.ds(middle, middle)], passed.at[1]),
        ]
        for load in loads:
            load.wait()
        wire.scatter_on(
            keys, landing, lambda j: passed[0 if j == 2 else 1].astype(single), passing.at[which]
        )

    def quarter_sends(source, landing):
        return [
            wire.go(source.at[s ^ j], landing.at[j - 1], wire.to_seq[j]) for j in range(1, groups)
        ]

    def fetch(source, b):
        loads = [wire.near(source, values)]
        if b is not None:
            loads.append(wire.near(pickall_ref.at[b], pick))
        for load in loads:
            load.wait()

    def combine(j):
        return dot(pick[:, j * size : (j + 1) * size], values[...], 0, 0).astype(narrow)

    def combine_out(target):
        for j in range(groups):
            stage[j] = combine(j)
        wire.near(stage, target).wait()

    def own_block(source):
        wire.near(source.at[s], own_rows).wait()
        return own_rows[...].astype(single)

    core_go = []
    for t in range(3):
        core_go.append(
            (
                wire.go(terms[t].at[3], c3_ref.at[t], wire.to_core),
                wire.go(terms[t].at[1], c1_ref.at[t], wire.to_core),
            )
        )
    fetch(bo_ref, 1)
    combine_out(mo_ref)
    other_go = scatter(mo_ref, land_a)
    z_go = []

    def send_far(t):
        wire.come(core_go[t][0])
        if t >= 2:
            wire.leave(z_go[t - 2])
        for g in (1, 0):
            loads = [
                wire.near(terms[t].at[2, g], buffers.at[0]),
                wire.near(c3_ref.at[t, g], buffers.at[1]),
            ]
            for load in loads:
                load.wait()
            far[t % 2, g] = (buffers[0].astype(single) + buffers[1].astype(single)).astype(narrow)
        z_go.append(wire.go(far.at[t % 2], zb_ref.at[t], wire.to_z))

    send_far(0)
    fetch(ba_ref, 0)
    combine_out(ra_ref)
    own_go = scatter(ra_ref, land_b)
    scatter_on(other_go, mo_ref, land_a, 0)

    own_count = slot_ref.shape[0]
    slots = slot_ref.shape[1] // 2
    ids = own_ids(own_count, 2 * own_count)

    def route_rows(b, table):
        total = jnp.zeros((TOP, groups * size), single)
        for e in range(own_count):
            mine = pick[e * slots : (e + 1) * slots].astype(single)
            row = jnp.sum(mine * slot_ref[e, b * slots : (b + 1) * slots], axis=0, keepdims=True)
            total = total + jnp.where(table[0:TOP] == ids[e], row, 0.0)
        return total

    route_own[...] = route_rows(0, table_ref)
    fetch(oa_ref, None)
    combine_out(ma_ref)
    total = wire.scatter_end(other_go, land_a, own_block(mo_ref))
    sums[...] = total.astype(narrow)
    half_go = wire.go(sums, land_h, wire.to_half)
    scatter_on(own_go, ra_ref, land_b, 1)
    send_far(1)
    for k in other_go:
        wire.leave(k)
    fetch(oo_ref, 1)
    combine_out(mo_ref)
    route_send[...] = route_rows(1, otab_ref)
    route_go = wire.go(route_send, land_r, wire.to_half)
    total = wire.scatter_end(own_go, land_b, own_block(ra_ref))
    wire.come(half_go)
    total = total + land_h[...].astype(single)
    back, gain_two = norm_back(total, hid_ref[...], gain_ref[1:2])
    hidden_grad = cot_ref[...].astype(single) + back
    tgrad_ref[...] = hidden_grad
    ag[s] = hidden_grad.astype(narrow)
    grad_go = wire.gather(ag.at[s], ag)
    wire.come(route_go)
    total = route_own[...] + land_r[...]
    for j in range(groups):
        quarters[j] = total[:, j * size : (j + 1) * size]
        logits[j] = table_ref[TOP : 2 * TOP, j * size : (j + 1) * size]
    quarter_go = quarter_sends(quarters, land_q)

    leave_go = []

    def finish_term(t):
        wire.come(core_go[t][1], z_go[t])
        if t >= 2:
            wire.leave(leave_go[t - 2])
        leave_go.append(len(wire.remotes))
        totals(
            wire, terms[t].at[0], c1_ref.at[t], zb_ref.at[t], buffers, leave.at[t % 2],
            own_ref.at[t], hx_ref.at[t],
        )

    finish_term(0)
    wire.gather_on(grad_go, ag)
    send_far(2)
    tok_rows = values.at[pl.ds(0, groups * size)]
    load_tok = wire.near(tokall_ref, tok_rows)
    wire.gather_end(grad_go)
    moe_go = scatter(mo_ref, land_a)
    exit_own = wall_ref[:, mix_width : mix_width + q_width]
    for j in range(groups):
        out_grad[j * size : (j + 1) * size] = dot(ag[j], exit_own, 1, 0).astype(narrow)
    attend_back_rows(out_grad, q_ref, k_ref, v_ref, log_ref, pg_ref, keys_sum, values_sum)
    load_tok.wait()
    gain_one = project_back_rows(
        pg_ref, wall_ref[:, :mix_width], tok_rows, cos_ref, sin_ref, stage, q_width + k_width, size
    )
    norm_go = scatter(stage, land_b)
    load_normed = wire.near(normed_ref, tok_rows)
    for k in other_go[4:] + own_go[4:]:
        wire.leave(k)
    scatter_on(moe_go, mo_ref, land_a, 0)
    finish_term(1)
    wire.scatter_on(
        norm_go, land_b,
        lambda j: stage[s ^ j, pl.ds(0 if j == 2 else middle, middle)].astype(single),
        passing.at[2],
    )
    total = wire.scatter_end(moe_go, land_a, own_block(mo_ref))
    for j in (1, 2):
        pl.semaphore_signal(free, inc=1, device_id=wire.to_seq[j], device_id_type=MESH)
    wire.leave(half_go)
    sums[...] = total.astype(narrow)
    moe_half_go = wire.go(sums, land_m, wire.to_half)

    pl.semaphore_wait(free, 2)
    moe_own_go = scatter(ma_ref, land_a)

    _, shards, few, width = gw.shape
    f, last = wire.f, mix_width + q_width
    shape = (groups, shards, few)
    load_normed.wait()
    gw[:, :, :, :mix_width] = (
        dot(tok_rows[...], pg_ref[...], 0, 0).astype(narrow).reshape(shape + (mix_width,))
    )
    grads = ag[...].reshape(groups * size, D)
    gw[:, :, :, mix_width:last] = (
        dot(grads, att_ref[...], 0, 0).astype(narrow).reshape(shape + (q_width,))
    )
    gains = jnp.concatenate([gain_one, gain_two, jnp.zeros((width - last - 2, D), single)], axis=0)
    gw[:, :, :, last:] = gains.T.astype(narrow).reshape(shape + (width - last,))
    pair_go = [wire.go(gw.at[:, f ^ (m + 1)], r1.at[m // 2], wire.to_core) for m in (2, 6, 0, 4)]
    scatter_on(moe_own_go, ma_ref, land_a, 1)
    total = wire.scatter_end(norm_go, land_b, stage[s].astype(single))
    back, _ = norm_back(total, tok_ref[...].astype(single), gain_ref[0:1])
    tgrad_ref[...] += back
    wire.come(*pair_go)

    def pair_sum(m):
        return gw[:, f ^ m].astype(single) + r1[m // 2].astype(single)

    gw[:, f ^ 2] = pair_sum(2).astype(narrow)
    go_2 = wire.go(gw.at[:, f ^ 2], r2.at[0], wire.to_z)
    gw[:, f ^ 6] = pair_sum(6).astype(narrow)
    go_6 = wire.go(gw.at[:, f ^ 6], r2.at[1], wire.to_z)
    wire.come(*quarter_go)
    route_grad = quarters[s]
    for j in range(groups - 1):
        route_grad = route_grad + land_q[j]
    top = logits[s]
    exponent = jnp.exp(top - jnp.max(top, axis=0, keepdims=True))
    gating = exponent / jnp.sum(exponent, axis=0, keepdims=True)
    lgrad_ref[...] = gating * (route_grad - jnp.sum(gating * route_grad, axis=0, keepdims=True))
    finish_term(2)
    total = wire.scatter_end(moe_own_go, land_a, hid_ref[...] + own_block(ma_ref))
    wire.come(moe_half_go)
    layer_ref[...] = (total + land_m[...].astype(single)).astype(narrow)
    wire.come(go_6)
    gw[:, f ^ 4] = (pair_sum(4) + r2[1].astype(single)).astype(narrow)
    go_4 = wire.go(gw.at[:, f ^ 4], r3, wire.to_half)
    wire.come(go_2, go_4)
    fin[...] = pair_sum(0) + r2[0].astype(single) + r3[...].astype(single)
    attn_in[s] = fin[s]
    last_go = [wire.go(fin.at[s ^ j], attn_in.at[s], wire.to_seq[j]) for j in range(1, groups)]
    wire.come(*last_go)
    wire.near(attn_in, attn_ref).wait()
    wire.finish()


def backward_call(
    backs, outs, pick, terms, hidden, gains, cot, wall, q, k, v, logs, tokens_all,
    cos_table, sin_table, slot_grad, table, other_table, normed, tok, att, few,
):
    size = hidden.shape[0]
    seq_len = tokens_all.shape[0]
    groups = seq_len // size
    rings, halves, own, part, width = terms[0].shape
    slot_rows = pick.shape[1]
    shape = jax.ShapeDtypeStruct
    vmem = pl.BlockSpec(memory_space=pltpu.VMEM)
    hbm = pl.BlockSpec(memory_space=pl.ANY)
    block = (groups, size, D)
    slab = (groups, few, wall.shape[1])
    mix_width = q.shape[1] + 2 * k.shape[1]
    landing = pltpu.VMEM((6, size // 2, D), narrow)
    route = pltpu.VMEM((TOP, seq_len), single)
    count = 96
    return pl.pallas_call(
        backward_body,
        in_specs=[hbm] * 10 + [vmem] * 15,
        out_specs=[vmem] * 3 + [hbm] * 9,
        out_shape=[
            shape((size, D), single),
            shape((size, D), narrow),
            shape((TOP, size), single),
            shape(slab, single),
            shape(block, narrow),
            shape(block, narrow),
            shape(block, narrow),
            shape((3, halves, own, part, width), narrow),
            shape((3, halves, own, part, width), narrow),
            shape((3, halves, own, part, width), narrow),
            shape((3, own, part, width), narrow),
            shape((3, own, part, width), narrow),
        ],
        scratch_shapes=[
            pltpu.VMEM((seq_len, mix_width), narrow),
            pltpu.SemaphoreType.REGULAR,
            pltpu.VMEM((groups, 8) + slab[1:], narrow),
            pltpu.VMEM((4,) + slab, narrow),
            pltpu.VMEM((2,) + slab, narrow),
            pltpu.VMEM(slab, narrow),
            pltpu.VMEM(slab, single),
            pltpu.VMEM(slab, single),
            pltpu.VMEM(block, narrow),
            pltpu.VMEM(q.shape, narrow),
            pltpu.VMEM((seq_len, HEAD_DIM), single),
            pltpu.VMEM((seq_len, HEAD_DIM), single),
            landing,
            landing,
            pltpu.VMEM((size, D), narrow),
            pltpu.VMEM((size, D), narrow),
            pltpu.VMEM((size, D), narrow),
            pltpu.VMEM((size, D), narrow),
            pltpu.VMEM((3, own, part, width), narrow),
            pltpu.VMEM((2, halves, own, part, width), narrow),
            pltpu.VMEM((2, own, part, width), narrow),
            pltpu.VMEM((2, size // 2, D), narrow),
            pltpu.VMEM((3, 2, size // 2, D), narrow),
            pltpu.VMEM((slot_rows, D), narrow),
            pltpu.VMEM((slot_rows, seq_len), narrow),
            pltpu.VMEM(block, narrow),
            route,
            route,
            route,
            pltpu.VMEM((groups, TOP, size), single),
            pltpu.VMEM((groups - 1, TOP, size), single),
            pltpu.VMEM((groups, TOP, size), single),
            pltpu.SemaphoreType.DMA((count,)),
            pltpu.SemaphoreType.DMA((count,)),
            pltpu.SemaphoreType.DMA((count,)),
        ],
        compiler_params=pltpu.CompilerParams(
            collective_id=1, has_side_effects=True, vmem_limit_bytes=67_000_000
        ),
        cost_estimate=pl.CostEstimate(
            flops=150_000_000_000, bytes_accessed=100_000_000, transcendentals=0
        ),
        name="backward_exchange",
    )(
        *backs, *outs, pick, tokens_all, normed, *terms, tok, att, hidden, gains, cot, wall,
        q, k, v, logs, cos_table, sin_table, slot_grad, table, other_table,
    )


def attention_back_call(grads, exit_own, mixing_own, q, k, v, logs, tokens_all, cos_table, sin_table):
    seq_len = tokens_all.shape[0]
    shape = jax.ShapeDtypeStruct
    return pl.pallas_call(
        attention_back_body,
        out_shape=[
            shape((seq_len, mixing_own.shape[1]), narrow),
            shape((seq_len, D), narrow),
            shape((1, D), single),
        ],
        scratch_shapes=[
            pltpu.VMEM(q.shape, narrow),
            pltpu.VMEM((seq_len, HEAD_DIM), single),
            pltpu.VMEM((seq_len, HEAD_DIM), single),
        ],
        cost_estimate=pl.CostEstimate(
            flops=2 * seq_len * D * (mixing_own.shape[1] + q.shape[1])
            + 10 * seq_len**2 * q.shape[1] * 4,
            bytes_accessed=seq_len * D * 8, transcendentals=0,
        ),
        name="attention_backward",
    )(grads, exit_own, mixing_own, q, k, v, logs, tokens_all, cos_table, sin_table)


def project_rows(at, size, tok_rows, mix, gain_row, cos_ref, sin_ref, normed_ref, q_ref, k_ref, v_ref):
    rows = slice(at, at + size)
    q_width, k_width = q_ref.shape[1], k_ref.shape[1]
    values = tok_rows.astype(single)
    inverse = lax.rsqrt(jnp.mean(values * values, axis=-1, keepdims=True) + epsilon)
    normed = (values * inverse * gain_row).astype(narrow)
    normed_ref[rows] = normed
    projected = dot(normed, mix, 1, 0)
    width = q_width + k_width
    turned = rope(
        projected[:, :width], wide(cos_ref[rows], width), wide(sin_ref[rows], width)
    ).astype(narrow)
    q_ref[rows] = turned[:, :q_width]
    k_ref[rows] = turned[:, q_width:]
    v_ref[rows] = projected[:, width:].astype(narrow)


def attend_rows(q_ref, k_ref, v_ref, att_ref, log_ref):
    seq_len, k_width = k_ref.shape
    size = QROWS
    group_size = HEADS // KV_HEADS
    for kv in range(k_width // HEAD_DIM):
        lanes = slice(kv * HEAD_DIM, (kv + 1) * HEAD_DIM)
        for block in range(seq_len // size):
            at = block * size
            end = at + size
            queries = stacked(q_ref, at, kv, size)
            scores = key_scores(k_ref[:end, lanes], queries, at, size)
            top = jnp.max(scores, axis=0, keepdims=True)
            exponent = jnp.exp(scores - top)
            total = jnp.sum(exponent, axis=0, keepdims=True)
            soft = (exponent * (1.0 / total)).astype(narrow)
            log_ref[kv * (seq_len // size) + block] = top + jnp.log(total)
            out = dot(v_ref[:end, lanes], soft, 0, 0)
            for g in range(group_size):
                head = kv * group_size + g
                att_ref[at:end, head * HEAD_DIM : (head + 1) * HEAD_DIM] = (
                    out[:, g * size : (g + 1) * size].T.astype(narrow)
                )


class Wire:
    def __init__(self, send, recv, local):
        self.send, self.recv, self.local = send, recv, local
        self.remotes, self.landed, self.left, self.locals = [], [], [], 0
        s, h, r = lax.axis_index("seq"), lax.axis_index("half"), lax.axis_index("ring")
        groups = lax.axis_size("seq")
        self.s, self.h, self.r, self.f, self.groups = s, h, r, h * 4 + r, groups
        self.to_half, self.to_z, self.to_core = {"half": h ^ 1}, {"ring": r ^ 2}, {"ring": r ^ 1}
        self.to_seq = [{"seq": s ^ j} for j in range(groups)]

    def meet(self):
        barrier = pltpu.get_barrier_semaphore()
        peers = self.to_seq[1:] + [self.to_half, self.to_z, self.to_core]
        for peer in peers:
            pl.semaphore_signal(barrier, inc=1, device_id=peer, device_id_type=MESH)
        pl.semaphore_wait(barrier, len(peers))

    def go(self, source, target, peer):
        k = len(self.remotes)
        copy = pltpu.make_async_remote_copy(
            src_ref=source, dst_ref=target, send_sem=self.send.at[k], recv_sem=self.recv.at[k],
            device_id=peer, device_id_type=MESH,
        )
        copy.start()
        self.remotes.append(copy)
        self.landed.append(False)
        self.left.append(False)
        return k

    def by_core(self, *sends):
        keys = []
        made = []
        for source, target, peer in sends:
            k = len(self.remotes)
            copy = pltpu.make_async_remote_copy(
                src_ref=source, dst_ref=target, send_sem=self.send.at[k],
                recv_sem=self.recv.at[k], device_id=peer, device_id_type=MESH,
            )
            self.remotes.append(copy)
            self.landed.append(False)
            self.left.append(False)
            keys.append(k)
            made.append(copy)

        @pl.when(self.r % 2 == 0)
        def _():
            for copy in made:
                copy.start()

        @pl.when(self.r % 2 == 1)
        def _():
            for copy in reversed(made):
                copy.start()

        return keys

    def come(self, *which):
        for k in which:
            self.remotes[k].wait_recv()
            self.landed[k] = True

    def leave(self, k):
        if not self.left[k]:
            self.remotes[k].wait_send()
        self.left[k] = True

    def near(self, source, target):
        copy = pltpu.make_async_copy(source, target, self.local.at[self.locals])
        self.locals += 1
        copy.start()
        return copy

    def gather(self, source, target):
        s = self.s
        return [self.go(source, target.at[s], self.to_seq[j]) for j in (1, 2)]

    def gather_on(self, keys, target):
        s, middle = self.s, target.shape[1] // 2
        first, second = pl.ds(0, middle), pl.ds(middle, middle)
        self.come(keys[0])
        block = target.at[s ^ 1, first]
        keys.append(self.go(block, block, self.to_seq[2]))
        self.come(keys[1])
        block = target.at[s ^ 2, second]
        keys.append(self.go(block, block, self.to_seq[1]))

    def gather_end(self, keys):
        self.come(*keys[2:])

    def scatter(self, source, landing):
        middle = landing.shape[1]
        first, second = pl.ds(0, middle), pl.ds(middle, middle)
        return [
            self.go(source(3).at[first], landing.at[1], self.to_seq[1]),
            self.go(source(3).at[second], landing.at[3], self.to_seq[2]),
            self.go(source(1).at[first], landing.at[0], self.to_seq[1]),
            self.go(source(2).at[second], landing.at[2], self.to_seq[2]),
        ]

    def scatter_on(self, keys, landing, kept, passing):
        self.come(keys[0])
        passing[0] = (kept(2) + landing[1].astype(single)).astype(narrow)
        keys.append(self.go(passing.at[0], landing.at[4], self.to_seq[2]))
        self.come(keys[1])
        passing[1] = (kept(1) + landing[3].astype(single)).astype(narrow)
        keys.append(self.go(passing.at[1], landing.at[5], self.to_seq[1]))

    def scatter_end(self, keys, landing, own):
        self.come(*keys[2:])
        first = landing[0].astype(single) + landing[4].astype(single)
        second = landing[2].astype(single) + landing[5].astype(single)
        return own + jnp.concatenate([first, second], axis=0)

    def finish(self):
        for k, copy in enumerate(self.remotes):
            if not self.left[k]:
                copy.wait_send()
            if not self.landed[k]:
                copy.wait_recv()


def place_rows(table, ids, capacity, slots, pick_ref, share_ref, b):
    length = table.shape[1]
    picked, logits, order = table[0:TOP], table[TOP : 2 * TOP], table[2 * TOP : 2 * TOP + 1]
    exponent = jnp.exp(logits - jnp.max(logits, axis=0, keepdims=True))
    gating = exponent / jnp.sum(exponent, axis=0, keepdims=True)
    down = lax.broadcasted_iota(jnp.int32, (length, length), 0).astype(single)
    along = lax.broadcasted_iota(jnp.int32, (length, length), 1).astype(single)
    place_col = jnp.sum(jnp.where(order == down, along, 0.0), axis=1, keepdims=True)
    place_row = jnp.broadcast_to(place_col, (length, 128)).T[0:1]
    earlier = (place_col < place_row).astype(single).astype(narrow)
    hits = [jnp.sum((picked == i).astype(single), axis=0, keepdims=True) for i in ids]
    share = [
        jnp.sum(jnp.where(picked == i, gating, 0.0), axis=0, keepdims=True) for i in ids
    ]
    spare = jnp.zeros((8 - len(ids), length), single)
    rank = dot(jnp.concatenate(hits + [spare], axis=0).astype(narrow), earlier, 1, 0)
    slot_at = lax.broadcasted_iota(jnp.int32, (slots, length), 0).astype(single)
    for e in range(len(ids)):
        kept = (hits[e] > 0.0) & (rank[e : e + 1] < capacity)
        filled = jnp.where(kept, rank[e : e + 1], -1.0) == slot_at
        pick_ref[b, e * slots : (e + 1) * slots] = filled.astype(single).astype(narrow)
        share_ref[e, b * slots : (b + 1) * slots] = jnp.sum(
            jnp.where(filled, share[e], 0.0), axis=1, keepdims=True
        )


def own_ids(own, local_count):
    first = lax.axis_index("seq") * local_count + lax.axis_index("half") * own
    return [(first + e).astype(single) for e in range(own)]


def forward_body(
    tok_ref, pack_ref, cot_ref, wg_ref, wu_ref, wd_ref, cos_ref, sin_ref, table_ref,
    normed_ref, q_ref, k_ref, v_ref, att_ref, log_ref, hid_ref, gain_ref, share_ref, otab_ref,
    tokall_ref, wall_ref, pickall_ref, xa_ref, xo_ref, ya_ref, yo_ref, wout_ref,
    xown_ref, xother_ref, yown_ref, yother_ref,
    tokv, wv, part, landed, passing, xv, other_table, pick, picked_rows, send, recv, local,
):
    wire = Wire(send, recv, local)
    s, h, r, f, groups = wire.s, wire.h, wire.r, wire.f, wire.groups
    _, fsdp, few, width = wv.shape
    q_width, k_width = q_ref.shape[1], k_ref.shape[1]
    mix_width = q_width + 2 * k_width
    size = tok_ref.shape[0]
    middle = size // 2
    wire.meet()

    pack_go = [wire.go(pack_ref.at[s ^ j], wv.at[s, f], wire.to_seq[j]) for j in range(1, groups)]
    tok_go = wire.gather(tok_ref, tokv)
    table_go = wire.go(table_ref, other_table, wire.to_half)
    own_cot = wire.near(cot_ref, ya_ref.at[s])
    wv[s, f] = pack_ref[s]
    tokv[s] = tok_ref[...]

    sources = (wg_ref, wu_ref, wd_ref)

    def weights_first(t):
        own, other = sources[t].at[h], sources[t].at[1 - h]
        target = wout_ref.at[t, h, r]
        keys = wire.by_core((other, target, wire.to_half), (own, target, wire.to_z))
        wire.go(own, target, wire.to_core)
        return keys

    def weights_next(t, keys):
        wire.come(keys[0])
        came = wout_ref.at[t, 1 - h, r]
        on_z = wire.go(came, came, wire.to_z)
        wire.go(came, came, wire.to_core)
        wire.come(keys[1])
        beside = wout_ref.at[t, h, r ^ 2]
        wire.go(beside, beside, wire.to_core)
        return on_z

    def weights_last(t, key):
        wire.come(key)
        beyond = wout_ref.at[t, 1 - h, r ^ 2]
        wire.go(beyond, beyond, wire.to_core)

    wire.come(*pack_go)
    mine = wv.at[:, f]
    a_half = wire.go(mine, mine, wire.to_half)
    a_z = wire.go(mine, mine, wire.to_z)
    parts_go = [wire.go(mine, mine, wire.to_core)]
    wire.come(a_half)
    block = wv.at[:, f ^ 4]
    b_z = wire.go(block, block, wire.to_z)
    parts_go.append(wire.go(block, block, wire.to_core))
    wire.come(a_z)
    block = wv.at[:, f ^ 2]
    parts_go.append(wire.go(block, block, wire.to_core))
    cot_half = wire.go(cot_ref, yo_ref.at[s], wire.to_half)
    gate_first = weights_first(0)
    wire.gather_on(tok_go, tokv)
    cot_go = wire.gather(cot_ref, ya_ref)
    wire.come(b_z)
    block = wv.at[:, f ^ 6]
    parts_go.append(wire.go(block, block, wire.to_core))
    up_first = weights_first(1)

    own, slots = wout_ref.shape[3], share_ref.shape[1] // 2
    capacity = (groups * size * TOP + EXPERTS - 1) // EXPERTS
    ids = own_ids(own, 2 * own)
    place_rows(table_ref[...], ids, capacity, slots, pick, share_ref, 0)
    wire.gather_end(tok_go)
    wire.come(*parts_go)
    wire.gather_on(cot_go, ya_ref)
    keep_tok = wire.near(tokv, tokall_ref)
    keep_wall = wire.near(wv, wall_ref)
    depth = groups * fsdp * few
    gains = wv[:, :, :, mix_width + q_width :].reshape(depth, width - mix_width - q_width)
    gains = gains.astype(single).T[0:8]
    gain_ref[...] = gains
    for j in range(groups):
        project_rows(
            j * size, size, tokv[j], wv[:, :, :, :mix_width].reshape(depth, mix_width),
            gains[0:1], cos_ref, sin_ref, normed_ref, q_ref, k_ref, v_ref,
        )
    attend_rows(q_ref, k_ref, v_ref, att_ref, log_ref)
    exit_own = wv[:, :, :, mix_width : mix_width + q_width].reshape(depth, q_width)
    for j in (3, 1, 2, 0):
        rows = pl.ds(pl.multiple_of((s ^ j) * size, size), size)
        partial = dot(att_ref[rows], exit_own, 1, 1)
        if j:
            part[j - 1] = partial.astype(narrow)
        else:
            part_go = wire.scatter(lambda j: part.at[j - 1], landed)
            hid_ref[...] = tok_ref[...].astype(single) + partial

    def dispatch(b, source, target):
        wire.near(source, tokv).wait()
        whole = tokv[...].reshape(groups * size, D)
        for at in range(0, D, 512):
            picked_rows[:, at : at + 512] = dot(pick[b], whole[:, at : at + 512], 1, 0).astype(narrow)
        wire.near(picked_rows, target).wait()

    def kept(j):
        return part[j - 1, (0 if j == 2 else middle) : (middle if j == 2 else size)].astype(single)

    for k in tok_go[2:]:
        wire.leave(k)
    gate_next = weights_next(0, gate_first)
    wire.scatter_on(part_go, landed, kept, passing)
    keep_tok.wait()
    own_cot.wait()
    wire.gather_end(cot_go)
    dispatch(0, ya_ref, yown_ref)
    hidden = wire.scatter_end(part_go, landed, hid_ref[...])
    hid_ref[...] = hidden
    inverse = lax.rsqrt(jnp.mean(hidden * hidden, axis=-1, keepdims=True) + epsilon)
    xv[...] = (hidden * inverse * gains[1:2]).astype(narrow)
    row_half = wire.go(xv, xo_ref.at[s], wire.to_half)
    row_go = wire.gather(xv, xa_ref)
    own_row = wire.near(xv, xa_ref.at[s])
    down_first = weights_first(2)
    wire.come(table_go)
    otab_ref[...] = other_table[...]
    place_rows(other_table[...], ids, capacity, slots, pick, share_ref, 1)
    keep_pick = wire.near(pick, pickall_ref)
    wire.gather_on(row_go, xa_ref)
    wire.come(cot_half)
    up_next = weights_next(1, up_first)
    wire.come(row_half)
    other_go = wire.gather(xo_ref.at[s], xo_ref)
    cot_other = wire.gather(yo_ref.at[s], yo_ref)
    weights_last(0, gate_next)
    own_row.wait()
    wire.gather_end(row_go)
    dispatch(0, xa_ref, xown_ref)
    wire.gather_on(other_go, xo_ref)
    wire.gather_on(cot_other, yo_ref)
    down_next = weights_next(2, down_first)
    weights_last(1, up_next)
    wire.gather_end(other_go)
    dispatch(1, xo_ref, xother_ref)
    wire.gather_end(cot_other)
    dispatch(1, yo_ref, yother_ref)
    weights_last(2, down_next)
    keep_wall.wait()
    keep_pick.wait()
    wire.finish()


def forward_call(tokens, packed, cotangent, weights, cos_table, sin_table, table, q_width, k_width, slots):
    groups, few, width = packed.shape
    _, own, part, hidden_units = weights[0].shape
    size = tokens.shape[0]
    seq_len = size * groups
    blocks = k_width // HEAD_DIM * (seq_len // QROWS)
    shape = jax.ShapeDtypeStruct
    vmem = pl.BlockSpec(memory_space=pltpu.VMEM)
    hbm = pl.BlockSpec(memory_space=pl.ANY)
    rows = shape((groups, size, D), narrow)
    count = 80
    picked = shape((own * slots, D), narrow)
    return pl.pallas_call(
        forward_body,
        in_specs=[vmem] * 3 + [hbm] * 3 + [vmem] * 3,
        out_specs=[vmem] * 10 + [hbm] * 12,
        out_shape=[
            shape((seq_len, D), narrow),
            shape((seq_len, q_width), narrow),
            shape((seq_len, k_width), narrow),
            shape((seq_len, k_width), narrow),
            shape((seq_len, q_width), narrow),
            shape((blocks, 1, HEADS // KV_HEADS * QROWS), single),
            shape((size, D), single),
            shape((8, D), single),
            shape((own, 2 * slots, 1), single),
            shape(table.shape, single),
            rows,
            shape((groups, 8, few, width), narrow),
            shape((2, own * slots, seq_len), narrow),
            rows, rows, rows, rows,
            shape((3, 2, 4, own, part, hidden_units), narrow),
            picked, picked, picked, picked,
        ],
        scratch_shapes=[
            pltpu.VMEM((groups, size, D), narrow),
            pltpu.VMEM((groups, 8, few, width), narrow),
            pltpu.VMEM((groups - 1, size, D), narrow),
            pltpu.VMEM((6, size // 2, D), narrow),
            pltpu.VMEM((2, size // 2, D), narrow),
            pltpu.VMEM((size, D), narrow),
            pltpu.VMEM(table.shape, single),
            pltpu.VMEM((2, own * slots, seq_len), narrow),
            pltpu.VMEM((own * slots, D), narrow),
            pltpu.SemaphoreType.DMA((count,)),
            pltpu.SemaphoreType.DMA((count,)),
            pltpu.SemaphoreType.DMA((24,)),
        ],
        compiler_params=pltpu.CompilerParams(collective_id=0, has_side_effects=True),
        cost_estimate=pl.CostEstimate(
            flops=200_000_000_000, bytes_accessed=100_000_000, transcendentals=0
        ),
        name="forward_exchange",
    )(tokens, packed, cotangent, *weights, cos_table, sin_table, table)


def expert_body(
    batch, own_apart, where_ref, all_ref, g_ref, u_ref, d_ref, *refs,
):
    _, halves, rings, _, part, width = all_ref.shape
    pieces = halves * rings
    x_refs, y_refs, w_ref = refs[:batch], refs[batch : 2 * batch], refs[2 * batch]
    refs = refs[2 * batch + 1 :]
    out_refs, row_refs, slot_ref = refs[:batch], refs[batch : 2 * batch], refs[2 * batch]
    gg_ref, gu_ref, gd_ref, held, sems = refs[2 * batch + 1 :]
    half, ring = where_ref[0], where_ref[1]
    e = pl.program_id(0)
    slot = lax.rem(e, 2)

    def each(expert, slot, act):
        for t, own_ref in enumerate((g_ref, u_ref, d_ref)):
            for g in range(halves):
                for r in range(rings):
                    at = g * rings + r
                    target, sem = held.at[slot, t, at], sems.at[slot, t, at]
                    if not own_apart:
                        act(pltpu.make_async_copy(all_ref.at[t, g, r, expert], target, sem))
                        continue
                    own = (half == g) & (ring == r)

                    @pl.when(own)
                    def _():
                        act(pltpu.make_async_copy(own_ref.at[g, expert], target, sem))

                    @pl.when(jnp.logical_not(own))
                    def _():
                        act(pltpu.make_async_copy(all_ref.at[t, g, r, expert], target, sem))

    @pl.when(e == 0)
    def _():
        each(e, slot, lambda copy: copy.start())

    @pl.when(e + 1 < pl.num_programs(0))
    def _():
        each(e + 1, 1 - slot, lambda copy: copy.start())

    for t in range(3):
        for at in range(pieces):
            pltpu.make_async_copy(
                all_ref.at[t, at // rings, at % rings, e], held.at[slot, t, at], sems.at[slot, t, at]
            ).wait()

    def weight(t):
        return held[slot, t].reshape(pieces * part, width)

    def write(ref, value):
        for g in range(halves):
            for r in range(rings):
                at = (g * rings + r) * part
                ref[r ^ ring if own_apart else r, g ^ half, 0] = value[at : at + part].astype(ref.dtype)

    slots = x_refs[0].shape[1]

    def split(outs, value):
        for b, ref in enumerate(outs):
            ref[0] = value[b * slots : (b + 1) * slots].astype(ref.dtype)

    rows = jnp.concatenate([ref[0] for ref in x_refs], axis=0)
    cots = jnp.concatenate([ref[0] for ref in y_refs], axis=0)
    share = w_ref[0]
    gate, up, down = weight(0), weight(1), weight(2)
    gate_pre = dot(rows, gate, 1, 0)
    up_pre = dot(rows, up, 1, 0)
    sig = jax.nn.sigmoid(gate_pre)
    mid = (gate_pre * sig * up_pre).astype(narrow)
    expert_out = dot(mid, down, 1, 1)
    cot_float = cots.astype(single)
    slot_ref[0] = jnp.sum(cot_float * expert_out, axis=-1, keepdims=True)
    split(out_refs, expert_out * share)
    out_low = (cot_float * share).astype(narrow)
    mid_grad = dot(out_low, down, 1, 0)
    write(gd_ref, dot(out_low, mid, 0, 0))
    gate_grad = (mid_grad * up_pre * sig * (1.0 + gate_pre * (1.0 - sig))).astype(narrow)
    up_grad = (mid_grad * gate_pre * sig).astype(narrow)
    split(row_refs, dot(gate_grad, gate, 1, 1) + dot(up_grad, up, 1, 1))
    both = dot(rows, jnp.concatenate([gate_grad, up_grad], axis=1), 0, 0)
    write(gg_ref, both[:, :width])
    write(gu_ref, both[:, width:])


def expert_call(where, gathered, weights, own_apart, rows, cots, share):
    _, halves, rings, own, part, width = gathered.shape
    batch = len(rows)
    _, slots, depth = rows[0].shape
    pieces = halves * rings
    weight_spec = pl.BlockSpec((rings, halves, 1, part, width), lambda e, h: (0, 0, e, 0, 0))
    row_spec = pl.BlockSpec((1, slots, depth), lambda e, h: (e, 0, 0))
    share_spec = pl.BlockSpec((1, batch * slots, 1), lambda e, h: (e, 0, 0))
    shape = jax.ShapeDtypeStruct
    row_shape = shape((own, slots, depth), narrow)
    outs = pl.pallas_call(
        functools.partial(expert_body, batch, own_apart),
        grid_spec=pltpu.PrefetchScalarGridSpec(
            num_scalar_prefetch=1,
            grid=(own,),
            in_specs=[pl.BlockSpec(memory_space=pl.ANY)] * 4
            + [row_spec] * (2 * batch)
            + [share_spec],
            out_specs=[row_spec] * (2 * batch) + [share_spec] + [weight_spec] * 3,
            scratch_shapes=[
                pltpu.VMEM((2, 3, pieces, part, width), narrow),
                pltpu.SemaphoreType.DMA((2, 3, pieces)),
            ],
        ),
        out_shape=[row_shape] * (2 * batch)
        + [shape((own, batch * slots, 1), single)]
        + [shape((rings, halves, own, part, width), narrow)] * 3,
        cost_estimate=pl.CostEstimate(
            flops=9 * 2 * own * batch * slots * depth * width,
            bytes_accessed=12 * own * depth * width + 8 * batch * own * slots * depth,
            transcendentals=0,
        ),
        name="expert_ffn",
    )(where, gathered, *weights, *rows, *cots, share)
    return outs[:batch], outs[batch : 2 * batch], outs[2 * batch], outs[2 * batch + 1 :]


def local(
    halves, rings,
    tokens, mixing_weight, output_weight, norm_gains, expert_gate, expert_up, expert_down,
    gate_logits, routes, fill_order, cotangent,
):
    groups = lax.axis_size("seq")
    column = lax.axis_index("seq")
    half = lax.axis_index("half")
    ring = lax.axis_index("ring")
    paired = halves == 2
    tok_rows = tokens.shape[1]
    seq_len = tok_rows * groups
    capacity = (seq_len * TOP + EXPERTS - 1) // EXPERTS
    local_count = expert_gate.shape[1]
    own_count = local_count // halves
    part = expert_gate.shape[0]
    fsdp_rows = mixing_weight.shape[0]
    q_width = HEADS * HEAD_DIM // groups
    k_width = KV_HEADS * HEAD_DIM // groups
    mix_width = q_width + 2 * k_width
    own_kv = KV_HEADS // groups
    own_heads = HEADS // groups
    group_size = HEADS // KV_HEADS
    score_scale = 1.0 / math.sqrt(HEAD_DIM)
    query_all = HEADS * HEAD_DIM
    key_all = KV_HEADS * HEAD_DIM

    def gather_seq(value):
        parts = [value] + [swap(value, "seq", j, groups) for j in range(1, groups)]
        whole = jnp.zeros((groups,) + value.shape, value.dtype)
        for j, item in enumerate(parts):
            whole = lax.dynamic_update_index_in_dim(whole, item, column ^ j, 0)
        return whole.reshape((seq_len,) + value.shape[1:])

    def scatter_seq(value):
        blocks = value.reshape((groups, tok_rows) + value.shape[1:])
        total = lax.dynamic_index_in_dim(blocks, column, 0, False).astype(single)
        for j in range(1, groups):
            sent = lax.dynamic_index_in_dim(blocks, column ^ j, 0, False).astype(narrow)
            total = total + swap(sent, "seq", j, groups).astype(single)
        return total

    def exchange_seq(blocks):
        whole = lax.dynamic_update_index_in_dim(
            jnp.zeros_like(blocks), lax.dynamic_index_in_dim(blocks, column, 0, False), column, 0
        )
        for j in range(1, groups):
            sent = lax.dynamic_index_in_dim(blocks, column ^ j, 0, False)
            whole = lax.dynamic_update_index_in_dim(
                whole, swap(sent, "seq", j, groups), column ^ j, 0
            )
        return whole

    packed = jnp.concatenate(
        [
            mixing_weight[:, :query_all].reshape(fsdp_rows, groups, q_width),
            mixing_weight[:, query_all : query_all + key_all].reshape(fsdp_rows, groups, k_width),
            mixing_weight[:, query_all + key_all :].reshape(fsdp_rows, groups, k_width),
            output_weight.reshape(fsdp_rows, groups, q_width),
            jnp.broadcast_to(
                jnp.pad(norm_gains, ((0, 0), (0, PAD - 2)))[:, None], (fsdp_rows, groups, PAD)
            ),
        ],
        2,
    ).transpose(1, 0, 2)
    cos_table, sin_table = rotary_tables(jnp.arange(seq_len, dtype=jnp.int32))
    cos_table, sin_table = jnp.tile(cos_table, (1, 2)), jnp.tile(sin_table, (1, 2))
    own_weights = [
        item.transpose(1, 0, 2).reshape(halves, own_count, part, FF)
        for item in (expert_gate, expert_up, expert_down)
    ]
    inputs = tokens[0].astype(single)
    slots = (capacity + 15) // 16 * 16
    if paired:
        table = jnp.concatenate(
            [
                routes[0].astype(single).T,
                gate_logits[0].T,
                jnp.broadcast_to(fill_order[0].astype(single), (8, seq_len)),
            ],
            0,
        )
        (
            normed_low, queries, keys, values, attended, logs, hidden, gains_float, share,
            other_table, tokens_all, packed, pick, _, _, _, _, gathered,
            own_x, other_x, own_y, other_y,
        ) = forward_call(
            tokens[0], packed, cotangent[0], own_weights, cos_table, sin_table, table,
            q_width, k_width, slots,
        )
        tokens_all = tokens_all.reshape(seq_len, D)
        packed = packed.reshape(D, -1)
        mixing_own = packed[:, :mix_width]
        exit_own = packed[:, mix_width : mix_width + q_width]
        seq_rows = [item.reshape(own_count, slots, D) for item in (own_x, other_x)]
        cot_rows = [item.reshape(own_count, slots, D) for item in (own_y, other_y)]
    else:
        packed = exchange_seq(packed)
        packed = lax.all_gather(packed, ("half", "ring"), axis=0, tiled=False)
        packed = packed.transpose(1, 0, 2, 3).reshape(D, -1)
        mixing_own = packed[:, :mix_width]
        exit_own = packed[:, mix_width : mix_width + q_width]
        gains_float = packed[:, mix_width + q_width : mix_width + q_width + 2].astype(single).T
        tokens_all = gather_seq(tokens[0])
        gathered = jnp.stack(
            [lax.all_gather(item[0], "ring", axis=0, tiled=False)[None] for item in own_weights]
        )
        normed_low, queries, keys, values, attended, logs, attn_part = attention_call(
            tokens_all, mixing_own, exit_own, gains_float, cos_table, sin_table
        )
        hidden = inputs + scatter_seq(attn_part)
        scale_two = lax.rsqrt(jnp.mean(hidden * hidden, axis=-1, keepdims=True) + epsilon)
        seq_rows = [gather_seq((hidden * scale_two * gains_float[1]).astype(narrow))]
        cot_rows = [gather_seq(cotangent[0])]

    if not paired:
        pair_routes = routes
        pair_order = fill_order
        pair_gating = softmax_last(gate_logits)
        expert_ids = column * local_count + half * own_count + jnp.arange(own_count, dtype=jnp.int32)
        places = jnp.arange(seq_len, dtype=jnp.int32)
        chosen = (pair_routes[..., None] == expert_ids).astype(single)
        hits = jnp.sum(chosen, axis=2)
        token_weight = jnp.sum(pair_gating[..., None] * chosen, axis=2)
        place_of = jnp.sum(
            jnp.where(pair_order[:, :, None] == places, places[None, :, None], 0), axis=1
        )
        earlier = (place_of[:, None, :] < place_of[:, :, None]).astype(narrow)
        rank = jnp.einsum(
            "btu,bue->bte", earlier, hits.astype(narrow), preferred_element_type=single
        ).astype(jnp.int32)
        kept = (hits > 0) & (rank < capacity)
        flat_place = jnp.where(kept, rank + jnp.arange(own_count, dtype=jnp.int32) * slots, -1)
        flat_ids = jnp.arange(own_count * slots, dtype=jnp.int32)
        filled = flat_place[:, :, 0:1] == flat_ids
        for e in range(1, own_count):
            filled = filled | (flat_place[:, :, e : e + 1] == flat_ids)
        select = filled.astype(narrow)
        batch = select.shape[0]
        match = flat_place[:, :, :, None] == (
            jnp.arange(own_count, dtype=jnp.int32)[:, None] * slots
            + jnp.arange(slots, dtype=jnp.int32)[None, :]
        )
        slot_weight = jnp.sum(jnp.where(match, token_weight[..., None], 0.0), axis=1)
        share = slot_weight.transpose(1, 0, 2).reshape(own_count, batch * slots, 1)

        def dispatch(rows):
            return [
                lax.dot_general(
                    select[b], item, (((0,), (0,)), ((), ())), preferred_element_type=narrow
                ).reshape(own_count, slots, D)
                for b, item in enumerate(rows)
            ]

        def combine(b, values):
            return lax.dot_general(
                select[b],
                values.reshape(own_count * slots, D),
                (((1,), (0,)), ((), ())),
                preferred_element_type=narrow,
            )

        seq_rows, cot_rows = dispatch(seq_rows), dispatch(cot_rows)

    slot_out, slot_back, slot_grad, (gate_term, up_term, down_term) = expert_call(
        jnp.stack([half, ring]), gathered, own_weights, paired,
        seq_rows, cot_rows, share,
    )
    def by_row(total):
        return total.reshape(local_count, part, FF).transpose(1, 0, 2).astype(single)

    if paired:
        flat = (own_count * slots, D)
        (
            tokens_gradient, layer_output, logits_rows, attn_total,
            _, _, _, _, _, _, own_terms, other_terms,
        ) = backward_call(
            [item.reshape(flat) for item in slot_back], [item.reshape(flat) for item in slot_out],
            pick, (gate_term, up_term, down_term), hidden, gains_float, cotangent[0], packed,
            queries, keys, values, logs, tokens_all, cos_table, sin_table, slot_grad, table,
            other_table, normed_low, tokens[0], attended, fsdp_rows,
        )
        logits_rows = logits_rows.T
        tokens_gradient, layer_output = tokens_gradient[None], layer_output[None]

        def expert_gradient(own, other):
            return by_row(
                jnp.stack([jnp.where(half == 0, own, other), jnp.where(half == 0, other, own)])
            )

        gate_gradient = expert_gradient(own_terms[0], other_terms[0])
        up_gradient = expert_gradient(own_terms[1], other_terms[1])
        down_gradient = expert_gradient(own_terms[2], other_terms[2])
    else:
        slot_grad = slot_grad.reshape(own_count, batch, slots).transpose(1, 0, 2)
        weight_grad_tok = jnp.sum(jnp.where(match, slot_grad[:, None], 0.0), axis=3)
        route_part = jnp.sum(weight_grad_tok[:, :, None, :] * chosen, axis=-1)

        def send_routes(value):
            blocks = value.reshape(groups, tok_rows, TOP)
            total = lax.dynamic_index_in_dim(blocks, column, 0, False)
            for j in range(1, groups):
                sent = lax.dynamic_index_in_dim(blocks, column ^ j, 0, False)
                total = total + swap(sent, "seq", j, groups)
            return total

        route_grad = send_routes(route_part[0])
        gating = softmax_last(
            lax.dynamic_slice_in_dim(gate_logits[0], column * tok_rows, tok_rows, 0)
        )
        logits_rows = gating * (route_grad - jnp.sum(gating * route_grad, axis=-1, keepdims=True))

        def ring_sum(term):
            return lax.psum_scatter(term, "ring", scatter_dimension=0, tiled=False)

        normed_two_grad = scatter_seq(combine(0, slot_back[0]))
        gate_gradient, up_gradient, down_gradient = [
            by_row(ring_sum(term)) for term in (gate_term, up_term, down_term)
        ]
        moe_rows = scatter_seq(combine(0, slot_out[0]))
        layer_output = (hidden + moe_rows).astype(narrow)[None]
        back, gain_two_grad = norm_back(normed_two_grad, hidden, gains_float[1])
        hidden_grad = cotangent[0].astype(single) + back
        attn_grad_all = gather_seq(hidden_grad.astype(narrow))
        projected_grad, normed_part, gain_one_grad = attention_back_call(
            attn_grad_all, exit_own, mixing_own, queries, keys, values, logs, tokens_all,
            cos_table, sin_table,
        )
        mixing_term = dot(normed_low, projected_grad, 0, 0)
        output_term = dot(attn_grad_all, attended, 0, 0)
        gains_term = jnp.stack([gain_one_grad[0], gain_two_grad[0]], 1)
        gains_term = jnp.pad(gains_term, ((0, 0), (0, PAD - 2)))
        attn_term = jnp.concatenate([mixing_term, output_term, gains_term], 1).astype(narrow)
        attn_term = attn_term.reshape(groups, halves * rings, fsdp_rows, -1).transpose(1, 0, 2, 3)
        attn_total = lax.psum_scatter(attn_term, ("half", "ring"), scatter_dimension=0, tiled=False)
        attn_total = exchange_seq(attn_total).astype(single)
        back, _ = norm_back(scatter_seq(normed_part), inputs, gains_float[0])
        tokens_gradient = (hidden_grad + back)[None]

    def columns(first, width):
        return attn_total[:, :, first : first + width].transpose(1, 0, 2).reshape(fsdp_rows, -1)

    mixing_gradient = jnp.concatenate(
        [
            columns(0, q_width),
            columns(q_width, k_width),
            columns(q_width + k_width, k_width),
        ],
        1,
    )
    output_gradient = columns(mix_width, q_width)
    gains_gradient = jnp.sum(attn_total[:, :, mix_width + q_width :][:, :, :2], axis=0)

    return (
        layer_output,
        tokens_gradient,
        mixing_gradient,
        output_gradient,
        gains_gradient,
        gate_gradient,
        up_gradient,
        down_gradient,
        logits_rows[None],
    )


def solution(mesh):
    groups, shards = mesh.shape["seq"], mesh.shape["fsdp"]
    halves = 2 if (EXPERTS // groups) % 2 == 0 and (groups, shards) == (4, 8) else 1
    rings = shards // halves
    grid = Mesh(mesh.devices.reshape(groups, halves, rings), ("seq", "half", "ring"))
    fsdp = ("half", "ring")
    every = ("seq", "half", "ring")
    in_specs = (
        P(fsdp, "seq", None),
        P(every, None),
        P(every, None),
        P(every, None),
        P(fsdp, "seq", None),
        P(fsdp, "seq", None),
        P(fsdp, "seq", None),
        P(fsdp, None, None),
        P(fsdp, None, None),
        P(fsdp, None),
        P(fsdp, "seq", None),
    )
    out_specs = (
        P(fsdp, "seq", None),
        P(fsdp, "seq", None),
        P(every, None),
        P(every, None),
        P(every, None),
        P(fsdp, "seq", None),
        P(fsdp, "seq", None),
        P(fsdp, "seq", None),
        P(fsdp, "seq", None),
    )
    return jax.shard_map(
        functools.partial(local, halves, rings),
        mesh=grid,
        in_specs=in_specs,
        out_specs=out_specs,
        check_vma=False,
    )
```

```python
import functools
import math

import jax
import jax.numpy as jnp
import numpy as np
from jax import lax
from jax.experimental import pallas as pl
from jax.experimental.pallas import tpu as pltpu
from jax.sharding import Mesh
from jax.sharding import PartitionSpec as P

D = 1536
HEADS = 24
KV_HEADS = 8
HEAD_DIM = 64
FF = 512
EXPERTS = 40
TOP = 8
QROWS = 256
PAD = 128

epsilon = 1e-05
rope_base = 10000.0
single = jnp.float32
narrow = jnp.bfloat16
MESH = pl.DeviceIdType.MESH


def rotary_tables(positions):
    half_width = HEAD_DIM // 2
    frequency = rope_base ** (-2.0 * jnp.arange(half_width, dtype=single) / HEAD_DIM)
    angles = positions.astype(single)[:, None] * frequency[None, :]
    cos_table = jnp.cos(angles)
    sin_table = jnp.sin(angles)
    return (jnp.concatenate([cos_table, cos_table], 1), jnp.concatenate([sin_table, sin_table], 1))


def softmax_last(logit_rows):
    row_max = jnp.max(logit_rows, axis=-1, keepdims=True)
    exponent = jnp.exp(logit_rows - row_max)
    return exponent / jnp.sum(exponent, axis=-1, keepdims=True)


def swap(value, axis, step, size):
    return lax.ppermute(value, axis, [(i, i ^ step) for i in range(size)])


def dot(left, right, left_dim, right_dim):
    return lax.dot_general(
        left, right, (((left_dim,), (right_dim,)), ((), ())), preferred_element_type=single
    )


def rope(values, cos_row, sin_row):
    width = values.shape[-1]
    lane = lax.broadcasted_iota(jnp.int32, values.shape, 1) % HEAD_DIM
    turned = jnp.where(
        lane < HEAD_DIM // 2,
        -pltpu.roll(values, width - HEAD_DIM // 2, 1),
        pltpu.roll(values, HEAD_DIM // 2, 1),
    )
    return values * cos_row + turned * sin_row


def rope_back(values, cos_row, sin_row):
    width = values.shape[-1]
    lane = lax.broadcasted_iota(jnp.int32, values.shape, 1) % HEAD_DIM
    scaled = values * sin_row
    turned = jnp.where(
        lane < HEAD_DIM // 2,
        pltpu.roll(scaled, width - HEAD_DIM // 2, 1),
        -pltpu.roll(scaled, HEAD_DIM // 2, 1),
    )
    return values * cos_row + turned


def wide(table, width):
    return jnp.concatenate([table] * (width // table.shape[1]), axis=1)


def stacked(ref, at, kv, size):
    group_size = HEADS // KV_HEADS
    return jnp.concatenate(
        [
            ref[at : at + size, (kv * group_size + g) * HEAD_DIM : (kv * group_size + g + 1) * HEAD_DIM]
            for g in range(group_size)
        ],
        axis=0,
    )


def key_scores(keys, queries, at, size):
    scores = dot(keys, queries, 1, 1) * (1.0 / math.sqrt(HEAD_DIM))
    shape = scores.shape
    key_at = lax.broadcasted_iota(jnp.int32, shape, 0)
    query_at = lax.broadcasted_iota(jnp.int32, shape, 1) % size + at
    return jnp.where(key_at <= query_at, scores, -jnp.inf)


def attention_body(
    tok_ref, mix_ref, exit_ref, gain_ref, cos_ref, sin_ref,
    normed_ref, q_ref, k_ref, v_ref, att_ref, log_ref, part_ref,
):
    seq_len = tok_ref.shape[0]
    size = QROWS
    for at in range(0, seq_len, size):
        project_rows(
            at, size, tok_ref[at : at + size], mix_ref[...], gain_ref[0:1],
            cos_ref, sin_ref, normed_ref, q_ref, k_ref, v_ref,
        )
    attend_rows(q_ref, k_ref, v_ref, att_ref, log_ref)
    for at in range(0, seq_len, size):
        part_ref[at : at + size] = dot(att_ref[at : at + size], exit_ref[...], 1, 1).astype(narrow)


def attention_call(tokens_all, mixing_own, exit_own, gains, cos_table, sin_table):
    seq_len = tokens_all.shape[0]
    q_width = exit_own.shape[1]
    k_width = (mixing_own.shape[1] - q_width) // 2
    group_size = HEADS // KV_HEADS
    blocks = k_width // HEAD_DIM * (seq_len // QROWS)
    shape = jax.ShapeDtypeStruct
    return pl.pallas_call(
        attention_body,
        out_shape=[
            shape((seq_len, D), narrow),
            shape((seq_len, q_width), narrow),
            shape((seq_len, k_width), narrow),
            shape((seq_len, k_width), narrow),
            shape((seq_len, q_width), narrow),
            shape((blocks, 1, group_size * QROWS), single),
            shape((seq_len, D), narrow),
        ],
        cost_estimate=pl.CostEstimate(
            flops=2 * seq_len * D * (mixing_own.shape[1] + q_width) + 4 * seq_len**2 * q_width * 4,
            bytes_accessed=seq_len * D * 6, transcendentals=0,
        ),
        name="attention_forward",
    )(tokens_all, mixing_own, exit_own, gains, cos_table, sin_table)


def norm_back(grads, values, gain_row):
    inverse = lax.rsqrt(jnp.mean(values * values, axis=-1, keepdims=True) + epsilon)
    normal = values * inverse
    scaled = grads * gain_row
    back = inverse * (scaled - normal * jnp.mean(scaled * normal, axis=-1, keepdims=True))
    return back, jnp.sum(grads * normal, axis=0, keepdims=True)


def attend_back_rows(out_grad, q_ref, k_ref, v_ref, log_ref, pg_ref, keys_sum, values_sum):
    seq_len, k_width = k_ref.shape
    q_width = q_ref.shape[1]
    size = QROWS
    group_size = HEADS // KV_HEADS
    scale = 1.0 / math.sqrt(HEAD_DIM)
    for kv in range(k_width // HEAD_DIM):
        lanes = slice(kv * HEAD_DIM, (kv + 1) * HEAD_DIM)
        keys_sum[...] = jnp.zeros_like(keys_sum)
        values_sum[...] = jnp.zeros_like(values_sum)
        for block in range(seq_len // size):
            at = block * size
            end = at + size
            queries = stacked(q_ref, at, kv, size)
            grads = stacked(out_grad, at, kv, size)
            keys, values = k_ref[:end, lanes], v_ref[:end, lanes]
            scores = key_scores(keys, queries, at, size)
            soft = jnp.exp(scores - log_ref[kv * (seq_len // size) + block])
            values_sum[:end] += dot(soft.astype(narrow), grads, 1, 0)
            soft_grad = dot(values, grads, 1, 1)
            delta = jnp.sum(soft * soft_grad, axis=0, keepdims=True)
            scores_grad = (soft * (soft_grad - delta)).astype(narrow)
            keys_sum[:end] += dot(scores_grad, queries, 1, 0) * scale
            query_grad = dot(keys, scores_grad, 0, 0) * scale
            for g in range(group_size):
                head = kv * group_size + g
                pg_ref[at:end, head * HEAD_DIM : (head + 1) * HEAD_DIM] = (
                    query_grad[:, g * size : (g + 1) * size].T.astype(narrow)
                )
        first = q_width + kv * HEAD_DIM
        pg_ref[:, first : first + HEAD_DIM] = keys_sum[...].astype(narrow)
        first += k_width
        pg_ref[:, first : first + HEAD_DIM] = values_sum[...].astype(narrow)


def project_back_rows(pg_ref, mix_ref, tok_ref, cos_ref, sin_ref, part_ref, turned, size):
    gain = jnp.zeros((1, D), single)
    for at in range(0, tok_ref.shape[0], size):
        rows = slice(at, at + size)
        pg_ref[rows, :turned] = rope_back(
            pg_ref[rows, :turned].astype(single), wide(cos_ref[rows], turned),
            wide(sin_ref[rows], turned),
        ).astype(narrow)
        normed_part = dot(pg_ref[rows], mix_ref, 1, 1)
        if len(part_ref.shape) == 3:
            part_ref[at // size] = normed_part.astype(narrow)
        else:
            part_ref[rows] = normed_part.astype(narrow)
        values = tok_ref[rows].astype(single)
        inverse = lax.rsqrt(jnp.mean(values * values, axis=-1, keepdims=True) + epsilon)
        gain = gain + jnp.sum(normed_part * (values * inverse), axis=0, keepdims=True)
    return gain


def attention_back_body(
    grad_ref, exit_ref, mix_ref, q_ref, k_ref, v_ref, log_ref, tok_ref, cos_ref, sin_ref,
    pg_ref, part_ref, gain_ref,
    out_grad, keys_sum, values_sum,
):
    size = QROWS
    for at in range(0, tok_ref.shape[0], size):
        out_grad[at : at + size] = dot(grad_ref[at : at + size], exit_ref[...], 1, 0).astype(narrow)
    attend_back_rows(out_grad, q_ref, k_ref, v_ref, log_ref, pg_ref, keys_sum, values_sum)
    turned = q_ref.shape[1] + k_ref.shape[1]
    gain_ref[...] = project_back_rows(
        pg_ref, mix_ref[...], tok_ref, cos_ref, sin_ref, part_ref, turned, size
    )


def totals(wire, begin, first, third, zed, buffers, out_send, own_out, half_out):
    sources = (first, third, zed)
    for g in (1, 0):
        loads = [wire.near(ref.at[g], buffers.at[i]) for i, ref in enumerate(sources)]
        for load in loads:
            load.wait()
        total = buffers[0].astype(single) + buffers[1].astype(single) + buffers[2].astype(single)
        if g:
            out_send[...] = total.astype(narrow)
            key = wire.plan(out_send, half_out, wire.to_half)
            begin(key)
        else:
            buffers[0] = total.astype(narrow)
            wire.near(buffers.at[0], own_out).wait()


def backward_body(
    ba_ref, bo_ref, oa_ref, oo_ref, pickall_ref, tokall_ref, normed_ref, gg_ref, gu_ref, gd_ref,
    tok_ref, att_ref, hid_ref, gain_ref, cot_ref, wall_ref, q_ref, k_ref, v_ref, log_ref, cos_ref, sin_ref,
    slot_ref, table_ref, otab_ref,
    tgrad_ref, layer_ref, lgrad_ref, attn_ref,
    ra_ref, mo_ref, ma_ref, c1_ref, c3_ref, zb_ref, own_ref, hx_ref,
    pg_ref, free, gw, r1, r2, r3, fin, attn_in,
    ag, out_grad, keys_sum, values_sum, land_a, land_b, land_h, land_m, sums, own_rows, buffers, far,
    leave, passed, passing, values, pick, stage, route_own, route_send, land_r, quarters, land_q, logits,
    send, recv, local,
):
    wire = Wire(send, recv, local)
    s, groups = wire.s, wire.groups
    size = hid_ref.shape[0]
    q_width, k_width = q_ref.shape[1], k_ref.shape[1]
    mix_width = q_width + 2 * k_width
    terms = (gg_ref, gu_ref, gd_ref)
    wire.meet()

    middle = size // 2

    def scatter(source, landing):
        return wire.scatter(lambda j: source.at[s ^ j], landing)

    def scatter_on(keys, source, landing, which):
        loads = [
            wire.near(source.at[s ^ 2, pl.ds(0, middle)], passed.at[0]),
            wire.near(source.at[s ^ 1, pl.ds(middle, middle)], passed.at[1]),
        ]
        for load in loads:
            load.wait()
        wire.scatter_on(
            keys, landing, lambda j: passed[0 if j == 2 else 1].astype(single), passing.at[which]
        )

    def quarter_sends(source, landing):
        return [
            wire.go(source.at[s ^ j], landing.at[j - 1], wire.to_seq[j]) for j in range(1, groups)
        ]

    def fetch(source, b):
        loads = [wire.near(source, values)]
        if b is not None:
            loads.append(wire.near(pickall_ref.at[b], pick))
        for load in loads:
            load.wait()

    def combine(j):
        return dot(pick[:, j * size : (j + 1) * size], values[...], 0, 0).astype(narrow)

    def combine_out(target):
        for j in range(groups):
            stage[j] = combine(j)
        wire.near(stage, target).wait()

    def own_block(source):
        wire.near(source.at[s], own_rows).wait()
        return own_rows[...].astype(single)

    core_go = []
    for t in range(3):
        core_go.append(
            (
                wire.go(terms[t].at[3], c3_ref.at[t], wire.to_core),
                wire.go(terms[t].at[1], c1_ref.at[t], wire.to_core),
            )
        )
    fetch(bo_ref, 1)
    combine_out(mo_ref)
    other_go = scatter(mo_ref, land_a)
    z_go = []

    def send_far(t):
        wire.come(core_go[t][0])
        if t >= 2:
            for k in z_go[t - 2]:
                wire.leave(k)
        z_go.append([])
        for g in (1, 0):
            loads = [
                wire.near(terms[t].at[2, g], buffers.at[0]),
                wire.near(c3_ref.at[t, g], buffers.at[1]),
            ]
            for load in loads:
                load.wait()
            far[t % 2, g] = (buffers[0].astype(single) + buffers[1].astype(single)).astype(narrow)
            z_go[t].append(wire.go(far.at[t % 2, g], zb_ref.at[t, g], wire.to_z))

    send_far(0)
    fetch(ba_ref, 0)
    combine_out(ra_ref)
    own_go = scatter(ra_ref, land_b)
    scatter_on(other_go, mo_ref, land_a, 0)

    own_count = slot_ref.shape[0]
    slots = slot_ref.shape[1] // 2
    ids = own_ids(own_count, 2 * own_count)

    def route_rows(b, table):
        total = jnp.zeros((TOP, groups * size), single)
        for e in range(own_count):
            mine = pick[e * slots : (e + 1) * slots].astype(single)
            row = jnp.sum(mine * slot_ref[e, b * slots : (b + 1) * slots], axis=0, keepdims=True)
            total = total + jnp.where(table[0:TOP] == ids[e], row, 0.0)
        return total

    route_own[...] = route_rows(0, table_ref)
    fetch(oa_ref, None)
    combine_out(ma_ref)
    total = wire.scatter_end(other_go, land_a, own_block(mo_ref))
    sums[...] = total.astype(narrow)
    half_go = wire.go(sums, land_h, wire.to_half)
    scatter_on(own_go, ra_ref, land_b, 1)
    send_far(1)
    for k in other_go:
        wire.leave(k)
    fetch(oo_ref, 1)
    combine_out(mo_ref)
    route_send[...] = route_rows(1, otab_ref)
    route_go = wire.go(route_send, land_r, wire.to_half)
    total = wire.scatter_end(own_go, land_b, own_block(ra_ref))
    wire.come(half_go)
    total = total + land_h[...].astype(single)
    back, gain_two = norm_back(total, hid_ref[...], gain_ref[1:2])
    hidden_grad = cot_ref[...].astype(single) + back
    tgrad_ref[...] = hidden_grad
    ag[s] = hidden_grad.astype(narrow)
    grad_go = wire.gather(ag.at[s], ag)
    wire.come(route_go)
    total = route_own[...] + land_r[...]
    for j in range(groups):
        quarters[j] = total[:, j * size : (j + 1) * size]
        logits[j] = table_ref[TOP : 2 * TOP, j * size : (j + 1) * size]
    quarter_go = quarter_sends(quarters, land_q)

    leave_go = []

    def now(k):
        wire.remotes[k].start()

    def finish_term(t, begin):
        wire.come(core_go[t][1], *z_go[t])
        if t >= 2:
            wire.leave(leave_go[t - 2])
        leave_go.append(len(wire.remotes))
        totals(
            wire, begin, terms[t].at[0], c1_ref.at[t], zb_ref.at[t], buffers, leave.at[t % 2],
            own_ref.at[t], hx_ref.at[t],
        )

    finish_term(0, now)
    wire.gather_on(grad_go, ag)
    send_far(2)
    tok_rows = values.at[pl.ds(0, groups * size)]
    load_tok = wire.near(tokall_ref, tok_rows)
    wire.gather_end(grad_go)
    moe_go = scatter(mo_ref, land_a)
    exit_own = wall_ref[:, mix_width : mix_width + q_width]
    for j in range(groups):
        out_grad[j * size : (j + 1) * size] = dot(ag[j], exit_own, 1, 0).astype(narrow)
    attend_back_rows(out_grad, q_ref, k_ref, v_ref, log_ref, pg_ref, keys_sum, values_sum)
    load_tok.wait()
    gain_one = project_back_rows(
        pg_ref, wall_ref[:, :mix_width], tok_rows, cos_ref, sin_ref, stage, q_width + k_width, size
    )
    norm_go = scatter(stage, land_b)
    load_normed = wire.near(normed_ref, tok_rows)
    for k in other_go[4:] + own_go[4:]:
        wire.leave(k)
    scatter_on(moe_go, mo_ref, land_a, 0)
    finish_term(1, now)
    wire.scatter_on(
        norm_go, land_b,
        lambda j: stage[s ^ j, pl.ds(0 if j == 2 else middle, middle)].astype(single),
        passing.at[2],
    )
    total = wire.scatter_end(moe_go, land_a, own_block(mo_ref))
    for j in (1, 2):
        pl.semaphore_signal(free, inc=1, device_id=wire.to_seq[j], device_id_type=MESH)
    wire.leave(half_go)
    sums[...] = total.astype(narrow)
    moe_half_go = wire.go(sums, land_m, wire.to_half)

    pl.semaphore_wait(free, 2)
    moe_own_go = scatter(ma_ref, land_a)

    _, shards, few, width = gw.shape
    f, last = wire.f, mix_width + q_width
    shape = (groups, shards, few)
    load_normed.wait()
    gw[:, :, :, :mix_width] = (
        dot(tok_rows[...], pg_ref[...], 0, 0).astype(narrow).reshape(shape + (mix_width,))
    )
    grads = ag[...].reshape(groups * size, D)
    gw[:, :, :, mix_width:last] = (
        dot(grads, att_ref[...], 0, 0).astype(narrow).reshape(shape + (q_width,))
    )
    gains = jnp.concatenate([gain_one, gain_two, jnp.zeros((width - last - 2, D), single)], axis=0)
    gw[:, :, :, last:] = gains.T.astype(narrow).reshape(shape + (width - last,))
    pair_go = [wire.go(gw.at[:, f ^ (m + 1)], r1.at[m // 2], wire.to_core) for m in (2, 6, 0, 4)]
    scatter_on(moe_own_go, ma_ref, land_a, 1)
    total = wire.scatter_end(norm_go, land_b, stage[s].astype(single))
    back, _ = norm_back(total, tok_ref[...].astype(single), gain_ref[0:1])
    tgrad_ref[...] += back
    wire.come(*pair_go)

    def pair_sum(m):
        return gw[:, f ^ m].astype(single) + r1[m // 2].astype(single)

    gw[:, f ^ 2] = pair_sum(2).astype(narrow)
    go_2 = wire.go(gw.at[:, f ^ 2], r2.at[0], wire.to_z)
    gw[:, f ^ 6] = pair_sum(6).astype(narrow)
    go_6 = wire.go(gw.at[:, f ^ 6], r2.at[1], wire.to_z)
    wire.come(*quarter_go)
    route_grad = quarters[s]
    for j in range(groups - 1):
        route_grad = route_grad + land_q[j]
    top = logits[s]
    exponent = jnp.exp(top - jnp.max(top, axis=0, keepdims=True))
    gating = exponent / jnp.sum(exponent, axis=0, keepdims=True)
    lgrad_ref[...] = gating * (route_grad - jnp.sum(gating * route_grad, axis=0, keepdims=True))
    held = []
    finish_term(2, held.append)
    total = wire.scatter_end(moe_own_go, land_a, hid_ref[...] + own_block(ma_ref))
    wire.come(moe_half_go)
    layer_ref[...] = (total + land_m[...].astype(single)).astype(narrow)
    wire.come(go_6)
    gw[:, f ^ 4] = (pair_sum(4) + r2[1].astype(single)).astype(narrow)
    go_4 = wire.go(gw.at[:, f ^ 4], r3, wire.to_half)
    now(held[0])
    wire.come(go_2, go_4)
    fin[...] = pair_sum(0) + r2[0].astype(single) + r3[...].astype(single)
    attn_in[s] = fin[s]
    last_go = [wire.go(fin.at[s ^ j], attn_in.at[s], wire.to_seq[j]) for j in range(1, groups)]
    wire.come(*last_go)
    wire.near(attn_in, attn_ref).wait()
    wire.finish()


def backward_call(
    backs, outs, pick, terms, hidden, gains, cot, wall, q, k, v, logs, tokens_all,
    cos_table, sin_table, slot_grad, table, other_table, normed, tok, att, few,
):
    size = hidden.shape[0]
    seq_len = tokens_all.shape[0]
    groups = seq_len // size
    rings, halves, own, part, width = terms[0].shape
    slot_rows = pick.shape[1]
    shape = jax.ShapeDtypeStruct
    vmem = pl.BlockSpec(memory_space=pltpu.VMEM)
    hbm = pl.BlockSpec(memory_space=pl.ANY)
    block = (groups, size, D)
    slab = (groups, few, wall.shape[1])
    mix_width = q.shape[1] + 2 * k.shape[1]
    landing = pltpu.VMEM((6, size // 2, D), narrow)
    route = pltpu.VMEM((TOP, seq_len), single)
    count = 96
    return pl.pallas_call(
        backward_body,
        in_specs=[hbm] * 10 + [vmem] * 15,
        out_specs=[vmem] * 3 + [hbm] * 9,
        out_shape=[
            shape((size, D), single),
            shape((size, D), narrow),
            shape((TOP, size), single),
            shape(slab, single),
            shape(block, narrow),
            shape(block, narrow),
            shape(block, narrow),
            shape((3, halves, own, part, width), narrow),
            shape((3, halves, own, part, width), narrow),
            shape((3, halves, own, part, width), narrow),
            shape((3, own, part, width), narrow),
            shape((3, own, part, width), narrow),
        ],
        scratch_shapes=[
            pltpu.VMEM((seq_len, mix_width), narrow),
            pltpu.SemaphoreType.REGULAR,
            pltpu.VMEM((groups, 8) + slab[1:], narrow),
            pltpu.VMEM((4,) + slab, narrow),
            pltpu.VMEM((2,) + slab, narrow),
            pltpu.VMEM(slab, narrow),
            pltpu.VMEM(slab, single),
            pltpu.VMEM(slab, single),
            pltpu.VMEM(block, narrow),
            pltpu.VMEM(q.shape, narrow),
            pltpu.VMEM((seq_len, HEAD_DIM), single),
            pltpu.VMEM((seq_len, HEAD_DIM), single),
            landing,
            landing,
            pltpu.VMEM((size, D), narrow),
            pltpu.VMEM((size, D), narrow),
            pltpu.VMEM((size, D), narrow),
            pltpu.VMEM((size, D), narrow),
            pltpu.VMEM((3, own, part, width), narrow),
            pltpu.VMEM((2, halves, own, part, width), narrow),
            pltpu.VMEM((2, own, part, width), narrow),
            pltpu.VMEM((2, size // 2, D), narrow),
            pltpu.VMEM((3, 2, size // 2, D), narrow),
            pltpu.VMEM((slot_rows, D), narrow),
            pltpu.VMEM((slot_rows, seq_len), narrow),
            pltpu.VMEM(block, narrow),
            route,
            route,
            route,
            pltpu.VMEM((groups, TOP, size), single),
            pltpu.VMEM((groups - 1, TOP, size), single),
            pltpu.VMEM((groups, TOP, size), single),
            pltpu.SemaphoreType.DMA((count,)),
            pltpu.SemaphoreType.DMA((count,)),
            pltpu.SemaphoreType.DMA((count,)),
        ],
        compiler_params=pltpu.CompilerParams(
            collective_id=1, has_side_effects=True, vmem_limit_bytes=67_000_000
        ),
        cost_estimate=pl.CostEstimate(
            flops=150_000_000_000, bytes_accessed=100_000_000, transcendentals=0
        ),
        name="backward_exchange",
    )(
        *backs, *outs, pick, tokens_all, normed, *terms, tok, att, hidden, gains, cot, wall,
        q, k, v, logs, cos_table, sin_table, slot_grad, table, other_table,
    )


def attention_back_call(grads, exit_own, mixing_own, q, k, v, logs, tokens_all, cos_table, sin_table):
    seq_len = tokens_all.shape[0]
    shape = jax.ShapeDtypeStruct
    return pl.pallas_call(
        attention_back_body,
        out_shape=[
            shape((seq_len, mixing_own.shape[1]), narrow),
            shape((seq_len, D), narrow),
            shape((1, D), single),
        ],
        scratch_shapes=[
            pltpu.VMEM(q.shape, narrow),
            pltpu.VMEM((seq_len, HEAD_DIM), single),
            pltpu.VMEM((seq_len, HEAD_DIM), single),
        ],
        cost_estimate=pl.CostEstimate(
            flops=2 * seq_len * D * (mixing_own.shape[1] + q.shape[1])
            + 10 * seq_len**2 * q.shape[1] * 4,
            bytes_accessed=seq_len * D * 8, transcendentals=0,
        ),
        name="attention_backward",
    )(grads, exit_own, mixing_own, q, k, v, logs, tokens_all, cos_table, sin_table)


def project_rows(at, size, tok_rows, mix, gain_row, cos_ref, sin_ref, normed_ref, q_ref, k_ref, v_ref):
    rows = slice(at, at + size)
    q_width, k_width = q_ref.shape[1], k_ref.shape[1]
    values = tok_rows.astype(single)
    inverse = lax.rsqrt(jnp.mean(values * values, axis=-1, keepdims=True) + epsilon)
    normed = (values * inverse * gain_row).astype(narrow)
    normed_ref[rows] = normed
    projected = dot(normed, mix, 1, 0)
    width = q_width + k_width
    turned = rope(
        projected[:, :width], wide(cos_ref[rows], width), wide(sin_ref[rows], width)
    ).astype(narrow)
    q_ref[rows] = turned[:, :q_width]
    k_ref[rows] = turned[:, q_width:]
    v_ref[rows] = projected[:, width:].astype(narrow)


def attend_rows(q_ref, k_ref, v_ref, att_ref, log_ref):
    seq_len, k_width = k_ref.shape
    size = QROWS
    group_size = HEADS // KV_HEADS
    for kv in range(k_width // HEAD_DIM):
        lanes = slice(kv * HEAD_DIM, (kv + 1) * HEAD_DIM)
        for block in range(seq_len // size):
            at = block * size
            end = at + size
            queries = stacked(q_ref, at, kv, size)
            scores = key_scores(k_ref[:end, lanes], queries, at, size)
            top = jnp.max(scores, axis=0, keepdims=True)
            exponent = jnp.exp(scores - top)
            total = jnp.sum(exponent, axis=0, keepdims=True)
            soft = (exponent * (1.0 / total)).astype(narrow)
            log_ref[kv * (seq_len // size) + block] = top + jnp.log(total)
            out = dot(v_ref[:end, lanes], soft, 0, 0)
            for g in range(group_size):
                head = kv * group_size + g
                att_ref[at:end, head * HEAD_DIM : (head + 1) * HEAD_DIM] = (
                    out[:, g * size : (g + 1) * size].T.astype(narrow)
                )


class Wire:
    def __init__(self, send, recv, local):
        self.send, self.recv, self.local = send, recv, local
        self.remotes, self.landed, self.left, self.locals = [], [], [], 0
        s, h, r = lax.axis_index("seq"), lax.axis_index("half"), lax.axis_index("ring")
        groups = lax.axis_size("seq")
        self.s, self.h, self.r, self.f, self.groups = s, h, r, h * 4 + r, groups
        self.to_half, self.to_z, self.to_core = {"half": h ^ 1}, {"ring": r ^ 2}, {"ring": r ^ 1}
        self.to_seq = [{"seq": s ^ j} for j in range(groups)]

    def meet(self):
        barrier = pltpu.get_barrier_semaphore()
        peers = self.to_seq[1:] + [self.to_half, self.to_z, self.to_core]
        for peer in peers:
            pl.semaphore_signal(barrier, inc=1, device_id=peer, device_id_type=MESH)
        pl.semaphore_wait(barrier, len(peers))

    def go(self, source, target, peer):
        k = self.plan(source, target, peer)
        self.remotes[k].start()
        return k

    def plan(self, source, target, peer):
        k = len(self.remotes)
        self.remotes.append(
            pltpu.make_async_remote_copy(
                src_ref=source, dst_ref=target, send_sem=self.send.at[k],
                recv_sem=self.recv.at[k], device_id=peer, device_id_type=MESH,
            )
        )
        self.landed.append(False)
        self.left.append(False)
        return k

    def by_core(self, *sends):
        keys = [self.plan(*send) for send in sends]

        @pl.when(self.r % 2 == 0)
        def _():
            for k in keys:
                self.remotes[k].start()

        @pl.when(self.r % 2 == 1)
        def _():
            for k in reversed(keys):
                self.remotes[k].start()

        return keys

    def come(self, *which):
        for k in which:
            self.remotes[k].wait_recv()
            self.landed[k] = True

    def leave(self, k):
        if not self.left[k]:
            self.remotes[k].wait_send()
        self.left[k] = True

    def near(self, source, target):
        copy = pltpu.make_async_copy(source, target, self.local.at[self.locals])
        self.locals += 1
        copy.start()
        return copy

    def gather(self, source, target):
        s = self.s
        return [self.go(source, target.at[s], self.to_seq[j]) for j in (1, 2)]

    def gather_on(self, keys, target):
        s, middle = self.s, target.shape[1] // 2
        first, second = pl.ds(0, middle), pl.ds(middle, middle)
        self.come(keys[0])
        block = target.at[s ^ 1, first]
        keys.append(self.go(block, block, self.to_seq[2]))
        self.come(keys[1])
        block = target.at[s ^ 2, second]
        keys.append(self.go(block, block, self.to_seq[1]))

    def gather_end(self, keys):
        self.come(*keys[2:])

    def scatter(self, source, landing):
        middle = landing.shape[1]
        first, second = pl.ds(0, middle), pl.ds(middle, middle)
        return [
            self.go(source(3).at[first], landing.at[1], self.to_seq[1]),
            self.go(source(3).at[second], landing.at[3], self.to_seq[2]),
            self.go(source(1).at[first], landing.at[0], self.to_seq[1]),
            self.go(source(2).at[second], landing.at[2], self.to_seq[2]),
        ]

    def scatter_on(self, keys, landing, kept, passing):
        self.come(keys[0])
        passing[0] = (kept(2) + landing[1].astype(single)).astype(narrow)
        keys.append(self.go(passing.at[0], landing.at[4], self.to_seq[2]))
        self.come(keys[1])
        passing[1] = (kept(1) + landing[3].astype(single)).astype(narrow)
        keys.append(self.go(passing.at[1], landing.at[5], self.to_seq[1]))

    def scatter_end(self, keys, landing, own):
        self.come(*keys[2:])
        first = landing[0].astype(single) + landing[4].astype(single)
        second = landing[2].astype(single) + landing[5].astype(single)
        return own + jnp.concatenate([first, second], axis=0)

    def finish(self):
        for k, copy in enumerate(self.remotes):
            if not self.left[k]:
                copy.wait_send()
            if not self.landed[k]:
                copy.wait_recv()


def place_rows(table, ids, capacity, slots, pick_ref, share_ref, b):
    length = table.shape[1]
    picked, logits, order = table[0:TOP], table[TOP : 2 * TOP], table[2 * TOP : 2 * TOP + 1]
    exponent = jnp.exp(logits - jnp.max(logits, axis=0, keepdims=True))
    gating = exponent / jnp.sum(exponent, axis=0, keepdims=True)
    down = lax.broadcasted_iota(jnp.int32, (length, length), 0).astype(single)
    along = lax.broadcasted_iota(jnp.int32, (length, length), 1).astype(single)
    place_col = jnp.sum(jnp.where(order == down, along, 0.0), axis=1, keepdims=True)
    place_row = jnp.broadcast_to(place_col, (length, 128)).T[0:1]
    earlier = (place_col < place_row).astype(single).astype(narrow)
    hits = [jnp.sum((picked == i).astype(single), axis=0, keepdims=True) for i in ids]
    share = [
        jnp.sum(jnp.where(picked == i, gating, 0.0), axis=0, keepdims=True) for i in ids
    ]
    spare = jnp.zeros((8 - len(ids), length), single)
    rank = dot(jnp.concatenate(hits + [spare], axis=0).astype(narrow), earlier, 1, 0)
    slot_at = lax.broadcasted_iota(jnp.int32, (slots, length), 0).astype(single)
    for e in range(len(ids)):
        kept = (hits[e] > 0.0) & (rank[e : e + 1] < capacity)
        filled = jnp.where(kept, rank[e : e + 1], -1.0) == slot_at
        pick_ref[b, e * slots : (e + 1) * slots] = filled.astype(single).astype(narrow)
        share_ref[e, b * slots : (b + 1) * slots] = jnp.sum(
            jnp.where(filled, share[e], 0.0), axis=1, keepdims=True
        )


def own_ids(own, local_count):
    first = lax.axis_index("seq") * local_count + lax.axis_index("half") * own
    return [(first + e).astype(single) for e in range(own)]


def forward_body(
    tok_ref, pack_ref, cot_ref, wg_ref, wu_ref, wd_ref, cos_ref, sin_ref, table_ref,
    normed_ref, q_ref, k_ref, v_ref, att_ref, log_ref, hid_ref, gain_ref, share_ref, otab_ref,
    tokall_ref, wall_ref, pickall_ref, xa_ref, xo_ref, ya_ref, yo_ref, wout_ref,
    xown_ref, xother_ref, yown_ref, yother_ref,
    tokv, wv, part, landed, passing, xv, other_table, pick, picked_rows, send, recv, local,
):
    wire = Wire(send, recv, local)
    s, h, r, f, groups = wire.s, wire.h, wire.r, wire.f, wire.groups
    _, fsdp, few, width = wv.shape
    q_width, k_width = q_ref.shape[1], k_ref.shape[1]
    mix_width = q_width + 2 * k_width
    size = tok_ref.shape[0]
    middle = size // 2
    wire.meet()

    pack_go = [wire.go(pack_ref.at[s ^ j], wv.at[s, f], wire.to_seq[j]) for j in range(1, groups)]
    tok_go = wire.gather(tok_ref, tokv)
    table_go = wire.go(table_ref, other_table, wire.to_half)
    own_cot = wire.near(cot_ref, ya_ref.at[s])
    wv[s, f] = pack_ref[s]
    tokv[s] = tok_ref[...]

    sources = (wg_ref, wu_ref, wd_ref)

    def weights_first(t):
        own, other = sources[t].at[h], sources[t].at[1 - h]
        target = wout_ref.at[t, h, r]
        keys = wire.by_core((other, target, wire.to_half), (own, target, wire.to_z))
        wire.go(own, target, wire.to_core)
        return keys

    def weights_next(t, keys):
        wire.come(keys[0])
        came = wout_ref.at[t, 1 - h, r]
        on_z = wire.go(came, came, wire.to_z)
        wire.go(came, came, wire.to_core)
        wire.come(keys[1])
        beside = wout_ref.at[t, h, r ^ 2]
        wire.go(beside, beside, wire.to_core)
        return on_z

    def weights_last(t, key):
        wire.come(key)
        beyond = wout_ref.at[t, 1 - h, r ^ 2]
        wire.go(beyond, beyond, wire.to_core)

    wire.come(*pack_go)
    mine = wv.at[:, f]
    a_half = wire.go(mine, mine, wire.to_half)
    a_z = wire.go(mine, mine, wire.to_z)
    parts_go = [wire.go(mine, mine, wire.to_core)]
    wire.come(a_half)
    block = wv.at[:, f ^ 4]
    b_z = wire.go(block, block, wire.to_z)
    parts_go.append(wire.go(block, block, wire.to_core))
    wire.come(a_z)
    block = wv.at[:, f ^ 2]
    parts_go.append(wire.go(block, block, wire.to_core))
    cot_half = wire.go(cot_ref, yo_ref.at[s], wire.to_half)
    gate_first = weights_first(0)
    wire.gather_on(tok_go, tokv)
    cot_go = wire.gather(cot_ref, ya_ref)
    wire.come(b_z)
    block = wv.at[:, f ^ 6]
    parts_go.append(wire.go(block, block, wire.to_core))
    up_first = weights_first(1)

    own, slots = wout_ref.shape[3], share_ref.shape[1] // 2
    capacity = (groups * size * TOP + EXPERTS - 1) // EXPERTS
    ids = own_ids(own, 2 * own)
    place_rows(table_ref[...], ids, capacity, slots, pick, share_ref, 0)
    wire.gather_end(tok_go)
    wire.come(*parts_go)
    wire.gather_on(cot_go, ya_ref)
    keep_tok = wire.near(tokv, tokall_ref)
    keep_wall = wire.near(wv, wall_ref)
    depth = groups * fsdp * few
    gains = wv[:, :, :, mix_width + q_width :].reshape(depth, width - mix_width - q_width)
    gains = gains.astype(single).T[0:8]
    gain_ref[...] = gains
    for j in range(groups):
        project_rows(
            j * size, size, tokv[j], wv[:, :, :, :mix_width].reshape(depth, mix_width),
            gains[0:1], cos_ref, sin_ref, normed_ref, q_ref, k_ref, v_ref,
        )
    attend_rows(q_ref, k_ref, v_ref, att_ref, log_ref)
    exit_own = wv[:, :, :, mix_width : mix_width + q_width].reshape(depth, q_width)
    for j in (3, 1, 2, 0):
        rows = pl.ds(pl.multiple_of((s ^ j) * size, size), size)
        partial = dot(att_ref[rows], exit_own, 1, 1)
        if j:
            part[j - 1] = partial.astype(narrow)
        else:
            part_go = wire.scatter(lambda j: part.at[j - 1], landed)
            hid_ref[...] = tok_ref[...].astype(single) + partial

    def dispatch(b, source, target):
        wire.near(source, tokv).wait()
        whole = tokv[...].reshape(groups * size, D)
        for at in range(0, D, 512):
            picked_rows[:, at : at + 512] = dot(pick[b], whole[:, at : at + 512], 1, 0).astype(narrow)
        wire.near(picked_rows, target).wait()

    def kept(j):
        return part[j - 1, (0 if j == 2 else middle) : (middle if j == 2 else size)].astype(single)

    for k in tok_go[2:]:
        wire.leave(k)
    gate_next = weights_next(0, gate_first)
    wire.scatter_on(part_go, landed, kept, passing)
    keep_tok.wait()
    own_cot.wait()
    wire.gather_end(cot_go)
    dispatch(0, ya_ref, yown_ref)
    hidden = wire.scatter_end(part_go, landed, hid_ref[...])
    hid_ref[...] = hidden
    inverse = lax.rsqrt(jnp.mean(hidden * hidden, axis=-1, keepdims=True) + epsilon)
    xv[...] = (hidden * inverse * gains[1:2]).astype(narrow)
    row_half = wire.go(xv, xo_ref.at[s], wire.to_half)
    row_go = wire.gather(xv, xa_ref)
    own_row = wire.near(xv, xa_ref.at[s])
    down_first = weights_first(2)
    wire.come(table_go)
    otab_ref[...] = other_table[...]
    place_rows(other_table[...], ids, capacity, slots, pick, share_ref, 1)
    keep_pick = wire.near(pick, pickall_ref)
    wire.gather_on(row_go, xa_ref)
    wire.come(cot_half)
    up_next = weights_next(1, up_first)
    wire.come(row_half)
    other_go = wire.gather(xo_ref.at[s], xo_ref)
    cot_other = wire.gather(yo_ref.at[s], yo_ref)
    weights_last(0, gate_next)
    own_row.wait()
    wire.gather_end(row_go)
    dispatch(0, xa_ref, xown_ref)
    wire.gather_on(other_go, xo_ref)
    wire.gather_on(cot_other, yo_ref)
    down_next = weights_next(2, down_first)
    weights_last(1, up_next)
    wire.gather_end(other_go)
    dispatch(1, xo_ref, xother_ref)
    wire.gather_end(cot_other)
    dispatch(1, yo_ref, yother_ref)
    weights_last(2, down_next)
    keep_wall.wait()
    keep_pick.wait()
    wire.finish()


def forward_call(tokens, packed, cotangent, weights, cos_table, sin_table, table, q_width, k_width, slots):
    groups, few, width = packed.shape
    _, own, part, hidden_units = weights[0].shape
    size = tokens.shape[0]
    seq_len = size * groups
    blocks = k_width // HEAD_DIM * (seq_len // QROWS)
    shape = jax.ShapeDtypeStruct
    vmem = pl.BlockSpec(memory_space=pltpu.VMEM)
    hbm = pl.BlockSpec(memory_space=pl.ANY)
    rows = shape((groups, size, D), narrow)
    count = 80
    picked = shape((own * slots, D), narrow)
    return pl.pallas_call(
        forward_body,
        in_specs=[vmem] * 3 + [hbm] * 3 + [vmem] * 3,
        out_specs=[vmem] * 10 + [hbm] * 12,
        out_shape=[
            shape((seq_len, D), narrow),
            shape((seq_len, q_width), narrow),
            shape((seq_len, k_width), narrow),
            shape((seq_len, k_width), narrow),
            shape((seq_len, q_width), narrow),
            shape((blocks, 1, HEADS // KV_HEADS * QROWS), single),
            shape((size, D), single),
            shape((8, D), single),
            shape((own, 2 * slots, 1), single),
            shape(table.shape, single),
            rows,
            shape((groups, 8, few, width), narrow),
            shape((2, own * slots, seq_len), narrow),
            rows, rows, rows, rows,
            shape((3, 2, 4, own, part, hidden_units), narrow),
            picked, picked, picked, picked,
        ],
        scratch_shapes=[
            pltpu.VMEM((groups, size, D), narrow),
            pltpu.VMEM((groups, 8, few, width), narrow),
            pltpu.VMEM((groups - 1, size, D), narrow),
            pltpu.VMEM((6, size // 2, D), narrow),
            pltpu.VMEM((2, size // 2, D), narrow),
            pltpu.VMEM((size, D), narrow),
            pltpu.VMEM(table.shape, single),
            pltpu.VMEM((2, own * slots, seq_len), narrow),
            pltpu.VMEM((own * slots, D), narrow),
            pltpu.SemaphoreType.DMA((count,)),
            pltpu.SemaphoreType.DMA((count,)),
            pltpu.SemaphoreType.DMA((24,)),
        ],
        compiler_params=pltpu.CompilerParams(collective_id=0, has_side_effects=True),
        cost_estimate=pl.CostEstimate(
            flops=200_000_000_000, bytes_accessed=100_000_000, transcendentals=0
        ),
        name="forward_exchange",
    )(tokens, packed, cotangent, *weights, cos_table, sin_table, table)


def expert_body(
    batch, own_apart, where_ref, all_ref, g_ref, u_ref, d_ref, *refs,
):
    _, halves, rings, _, part, width = all_ref.shape
    pieces = halves * rings
    x_refs, y_refs, w_ref = refs[:batch], refs[batch : 2 * batch], refs[2 * batch]
    refs = refs[2 * batch + 1 :]
    out_refs, row_refs, slot_ref = refs[:batch], refs[batch : 2 * batch], refs[2 * batch]
    gg_ref, gu_ref, gd_ref, held, sems = refs[2 * batch + 1 :]
    half, ring = where_ref[0], where_ref[1]
    e = pl.program_id(0)
    slot = lax.rem(e, 2)

    def each(expert, slot, act):
        for t, own_ref in enumerate((g_ref, u_ref, d_ref)):
            for g in range(halves):
                for r in range(rings):
                    at = g * rings + r
                    target, sem = held.at[slot, t, at], sems.at[slot, t, at]
                    if not own_apart:
                        act(pltpu.make_async_copy(all_ref.at[t, g, r, expert], target, sem))
                        continue
                    own = (half == g) & (ring == r)

                    @pl.when(own)
                    def _():
                        act(pltpu.make_async_copy(own_ref.at[g, expert], target, sem))

                    @pl.when(jnp.logical_not(own))
                    def _():
                        act(pltpu.make_async_copy(all_ref.at[t, g, r, expert], target, sem))

    @pl.when(e == 0)
    def _():
        each(e, slot, lambda copy: copy.start())

    @pl.when(e + 1 < pl.num_programs(0))
    def _():
        each(e + 1, 1 - slot, lambda copy: copy.start())

    for t in range(3):
        for at in range(pieces):
            pltpu.make_async_copy(
                all_ref.at[t, at // rings, at % rings, e], held.at[slot, t, at], sems.at[slot, t, at]
            ).wait()

    def weight(t):
        return held[slot, t].reshape(pieces * part, width)

    def write(ref, value):
        for g in range(halves):
            for r in range(rings):
                at = (g * rings + r) * part
                ref[r ^ ring if own_apart else r, g ^ half, 0] = value[at : at + part].astype(ref.dtype)

    slots = x_refs[0].shape[1]

    def split(outs, value):
        for b, ref in enumerate(outs):
            ref[0] = value[b * slots : (b + 1) * slots].astype(ref.dtype)

    rows = jnp.concatenate([ref[0] for ref in x_refs], axis=0)
    cots = jnp.concatenate([ref[0] for ref in y_refs], axis=0)
    share = w_ref[0]
    gate, up, down = weight(0), weight(1), weight(2)
    gate_pre = dot(rows, gate, 1, 0)
    up_pre = dot(rows, up, 1, 0)
    sig = jax.nn.sigmoid(gate_pre)
    mid = (gate_pre * sig * up_pre).astype(narrow)
    expert_out = dot(mid, down, 1, 1)
    cot_float = cots.astype(single)
    slot_ref[0] = jnp.sum(cot_float * expert_out, axis=-1, keepdims=True)
    split(out_refs, expert_out * share)
    out_low = (cot_float * share).astype(narrow)
    mid_grad = dot(out_low, down, 1, 0)
    write(gd_ref, dot(out_low, mid, 0, 0))
    gate_grad = (mid_grad * up_pre * sig * (1.0 + gate_pre * (1.0 - sig))).astype(narrow)
    up_grad = (mid_grad * gate_pre * sig).astype(narrow)
    split(row_refs, dot(gate_grad, gate, 1, 1) + dot(up_grad, up, 1, 1))
    both = dot(rows, jnp.concatenate([gate_grad, up_grad], axis=1), 0, 0)
    write(gg_ref, both[:, :width])
    write(gu_ref, both[:, width:])


def expert_call(where, gathered, weights, own_apart, rows, cots, share):
    _, halves, rings, own, part, width = gathered.shape
    batch = len(rows)
    _, slots, depth = rows[0].shape
    pieces = halves * rings
    weight_spec = pl.BlockSpec((rings, halves, 1, part, width), lambda e, h: (0, 0, e, 0, 0))
    row_spec = pl.BlockSpec((1, slots, depth), lambda e, h: (e, 0, 0))
    share_spec = pl.BlockSpec((1, batch * slots, 1), lambda e, h: (e, 0, 0))
    shape = jax.ShapeDtypeStruct
    row_shape = shape((own, slots, depth), narrow)
    outs = pl.pallas_call(
        functools.partial(expert_body, batch, own_apart),
        grid_spec=pltpu.PrefetchScalarGridSpec(
            num_scalar_prefetch=1,
            grid=(own,),
            in_specs=[pl.BlockSpec(memory_space=pl.ANY)] * 4
            + [row_spec] * (2 * batch)
            + [share_spec],
            out_specs=[row_spec] * (2 * batch) + [share_spec] + [weight_spec] * 3,
            scratch_shapes=[
                pltpu.VMEM((2, 3, pieces, part, width), narrow),
                pltpu.SemaphoreType.DMA((2, 3, pieces)),
            ],
        ),
        out_shape=[row_shape] * (2 * batch)
        + [shape((own, batch * slots, 1), single)]
        + [shape((rings, halves, own, part, width), narrow)] * 3,
        cost_estimate=pl.CostEstimate(
            flops=9 * 2 * own * batch * slots * depth * width,
            bytes_accessed=12 * own * depth * width + 8 * batch * own * slots * depth,
            transcendentals=0,
        ),
        name="expert_ffn",
    )(where, gathered, *weights, *rows, *cots, share)
    return outs[:batch], outs[batch : 2 * batch], outs[2 * batch], outs[2 * batch + 1 :]


def local(
    halves, rings,
    tokens, mixing_weight, output_weight, norm_gains, expert_gate, expert_up, expert_down,
    gate_logits, routes, fill_order, cotangent,
):
    groups = lax.axis_size("seq")
    column = lax.axis_index("seq")
    half = lax.axis_index("half")
    ring = lax.axis_index("ring")
    paired = halves == 2
    tok_rows = tokens.shape[1]
    seq_len = tok_rows * groups
    capacity = (seq_len * TOP + EXPERTS - 1) // EXPERTS
    local_count = expert_gate.shape[1]
    own_count = local_count // halves
    part = expert_gate.shape[0]
    fsdp_rows = mixing_weight.shape[0]
    q_width = HEADS * HEAD_DIM // groups
    k_width = KV_HEADS * HEAD_DIM // groups
    mix_width = q_width + 2 * k_width
    own_kv = KV_HEADS // groups
    own_heads = HEADS // groups
    group_size = HEADS // KV_HEADS
    score_scale = 1.0 / math.sqrt(HEAD_DIM)
    query_all = HEADS * HEAD_DIM
    key_all = KV_HEADS * HEAD_DIM

    def gather_seq(value):
        parts = [value] + [swap(value, "seq", j, groups) for j in range(1, groups)]
        whole = jnp.zeros((groups,) + value.shape, value.dtype)
        for j, item in enumerate(parts):
            whole = lax.dynamic_update_index_in_dim(whole, item, column ^ j, 0)
        return whole.reshape((seq_len,) + value.shape[1:])

    def scatter_seq(value):
        blocks = value.reshape((groups, tok_rows) + value.shape[1:])
        total = lax.dynamic_index_in_dim(blocks, column, 0, False).astype(single)
        for j in range(1, groups):
            sent = lax.dynamic_index_in_dim(blocks, column ^ j, 0, False).astype(narrow)
            total = total + swap(sent, "seq", j, groups).astype(single)
        return total

    def exchange_seq(blocks):
        whole = lax.dynamic_update_index_in_dim(
            jnp.zeros_like(blocks), lax.dynamic_index_in_dim(blocks, column, 0, False), column, 0
        )
        for j in range(1, groups):
            sent = lax.dynamic_index_in_dim(blocks, column ^ j, 0, False)
            whole = lax.dynamic_update_index_in_dim(
                whole, swap(sent, "seq", j, groups), column ^ j, 0
            )
        return whole

    packed = jnp.concatenate(
        [
            mixing_weight[:, :query_all].reshape(fsdp_rows, groups, q_width),
            mixing_weight[:, query_all : query_all + key_all].reshape(fsdp_rows, groups, k_width),
            mixing_weight[:, query_all + key_all :].reshape(fsdp_rows, groups, k_width),
            output_weight.reshape(fsdp_rows, groups, q_width),
            jnp.broadcast_to(
                jnp.pad(norm_gains, ((0, 0), (0, PAD - 2)))[:, None], (fsdp_rows, groups, PAD)
            ),
        ],
        2,
    ).transpose(1, 0, 2)
    cos_table, sin_table = rotary_tables(jnp.arange(seq_len, dtype=jnp.int32))
    cos_table, sin_table = jnp.tile(cos_table, (1, 2)), jnp.tile(sin_table, (1, 2))
    own_weights = [
        item.transpose(1, 0, 2).reshape(halves, own_count, part, FF)
        for item in (expert_gate, expert_up, expert_down)
    ]
    inputs = tokens[0].astype(single)
    slots = (capacity + 15) // 16 * 16
    if paired:
        table = jnp.concatenate(
            [
                routes[0].astype(single).T,
                gate_logits[0].T,
                jnp.broadcast_to(fill_order[0].astype(single), (8, seq_len)),
            ],
            0,
        )
        (
            normed_low, queries, keys, values, attended, logs, hidden, gains_float, share,
            other_table, tokens_all, packed, pick, _, _, _, _, gathered,
            own_x, other_x, own_y, other_y,
        ) = forward_call(
            tokens[0], packed, cotangent[0], own_weights, cos_table, sin_table, table,
            q_width, k_width, slots,
        )
        tokens_all = tokens_all.reshape(seq_len, D)
        packed = packed.reshape(D, -1)
        mixing_own = packed[:, :mix_width]
        exit_own = packed[:, mix_width : mix_width + q_width]
        seq_rows = [item.reshape(own_count, slots, D) for item in (own_x, other_x)]
        cot_rows = [item.reshape(own_count, slots, D) for item in (own_y, other_y)]
    else:
        packed = exchange_seq(packed)
        packed = lax.all_gather(packed, ("half", "ring"), axis=0, tiled=False)
        packed = packed.transpose(1, 0, 2, 3).reshape(D, -1)
        mixing_own = packed[:, :mix_width]
        exit_own = packed[:, mix_width : mix_width + q_width]
        gains_float = packed[:, mix_width + q_width : mix_width + q_width + 2].astype(single).T
        tokens_all = gather_seq(tokens[0])
        gathered = jnp.stack(
            [lax.all_gather(item[0], "ring", axis=0, tiled=False)[None] for item in own_weights]
        )
        normed_low, queries, keys, values, attended, logs, attn_part = attention_call(
            tokens_all, mixing_own, exit_own, gains_float, cos_table, sin_table
        )
        hidden = inputs + scatter_seq(attn_part)
        scale_two = lax.rsqrt(jnp.mean(hidden * hidden, axis=-1, keepdims=True) + epsilon)
        seq_rows = [gather_seq((hidden * scale_two * gains_float[1]).astype(narrow))]
        cot_rows = [gather_seq(cotangent[0])]

    if not paired:
        pair_routes = routes
        pair_order = fill_order
        pair_gating = softmax_last(gate_logits)
        expert_ids = column * local_count + half * own_count + jnp.arange(own_count, dtype=jnp.int32)
        places = jnp.arange(seq_len, dtype=jnp.int32)
        chosen = (pair_routes[..., None] == expert_ids).astype(single)
        hits = jnp.sum(chosen, axis=2)
        token_weight = jnp.sum(pair_gating[..., None] * chosen, axis=2)
        place_of = jnp.sum(
            jnp.where(pair_order[:, :, None] == places, places[None, :, None], 0), axis=1
        )
        earlier = (place_of[:, None, :] < place_of[:, :, None]).astype(narrow)
        rank = jnp.einsum(
            "btu,bue->bte", earlier, hits.astype(narrow), preferred_element_type=single
        ).astype(jnp.int32)
        kept = (hits > 0) & (rank < capacity)
        flat_place = jnp.where(kept, rank + jnp.arange(own_count, dtype=jnp.int32) * slots, -1)
        flat_ids = jnp.arange(own_count * slots, dtype=jnp.int32)
        filled = flat_place[:, :, 0:1] == flat_ids
        for e in range(1, own_count):
            filled = filled | (flat_place[:, :, e : e + 1] == flat_ids)
        select = filled.astype(narrow)
        batch = select.shape[0]
        match = flat_place[:, :, :, None] == (
            jnp.arange(own_count, dtype=jnp.int32)[:, None] * slots
            + jnp.arange(slots, dtype=jnp.int32)[None, :]
        )
        slot_weight = jnp.sum(jnp.where(match, token_weight[..., None], 0.0), axis=1)
        share = slot_weight.transpose(1, 0, 2).reshape(own_count, batch * slots, 1)

        def dispatch(rows):
            return [
                lax.dot_general(
                    select[b], item, (((0,), (0,)), ((), ())), preferred_element_type=narrow
                ).reshape(own_count, slots, D)
                for b, item in enumerate(rows)
            ]

        def combine(b, values):
            return lax.dot_general(
                select[b],
                values.reshape(own_count * slots, D),
                (((1,), (0,)), ((), ())),
                preferred_element_type=narrow,
            )

        seq_rows, cot_rows = dispatch(seq_rows), dispatch(cot_rows)

    slot_out, slot_back, slot_grad, (gate_term, up_term, down_term) = expert_call(
        jnp.stack([half, ring]), gathered, own_weights, paired,
        seq_rows, cot_rows, share,
    )
    def by_row(total):
        return total.reshape(local_count, part, FF).transpose(1, 0, 2).astype(single)

    if paired:
        flat = (own_count * slots, D)
        (
            tokens_gradient, layer_output, logits_rows, attn_total,
            _, _, _, _, _, _, own_terms, other_terms,
        ) = backward_call(
            [item.reshape(flat) for item in slot_back], [item.reshape(flat) for item in slot_out],
            pick, (gate_term, up_term, down_term), hidden, gains_float, cotangent[0], packed,
            queries, keys, values, logs, tokens_all, cos_table, sin_table, slot_grad, table,
            other_table, normed_low, tokens[0], attended, fsdp_rows,
        )
        logits_rows = logits_rows.T
        tokens_gradient, layer_output = tokens_gradient[None], layer_output[None]

        def expert_gradient(own, other):
            return by_row(
                jnp.stack([jnp.where(half == 0, own, other), jnp.where(half == 0, other, own)])
            )

        gate_gradient = expert_gradient(own_terms[0], other_terms[0])
        up_gradient = expert_gradient(own_terms[1], other_terms[1])
        down_gradient = expert_gradient(own_terms[2], other_terms[2])
    else:
        slot_grad = slot_grad.reshape(own_count, batch, slots).transpose(1, 0, 2)
        weight_grad_tok = jnp.sum(jnp.where(match, slot_grad[:, None], 0.0), axis=3)
        route_part = jnp.sum(weight_grad_tok[:, :, None, :] * chosen, axis=-1)

        def send_routes(value):
            blocks = value.reshape(groups, tok_rows, TOP)
            total = lax.dynamic_index_in_dim(blocks, column, 0, False)
            for j in range(1, groups):
                sent = lax.dynamic_index_in_dim(blocks, column ^ j, 0, False)
                total = total + swap(sent, "seq", j, groups)
            return total

        route_grad = send_routes(route_part[0])
        gating = softmax_last(
            lax.dynamic_slice_in_dim(gate_logits[0], column * tok_rows, tok_rows, 0)
        )
        logits_rows = gating * (route_grad - jnp.sum(gating * route_grad, axis=-1, keepdims=True))

        def ring_sum(term):
            return lax.psum_scatter(term, "ring", scatter_dimension=0, tiled=False)

        normed_two_grad = scatter_seq(combine(0, slot_back[0]))
        gate_gradient, up_gradient, down_gradient = [
            by_row(ring_sum(term)) for term in (gate_term, up_term, down_term)
        ]
        moe_rows = scatter_seq(combine(0, slot_out[0]))
        layer_output = (hidden + moe_rows).astype(narrow)[None]
        back, gain_two_grad = norm_back(normed_two_grad, hidden, gains_float[1])
        hidden_grad = cotangent[0].astype(single) + back
        attn_grad_all = gather_seq(hidden_grad.astype(narrow))
        projected_grad, normed_part, gain_one_grad = attention_back_call(
            attn_grad_all, exit_own, mixing_own, queries, keys, values, logs, tokens_all,
            cos_table, sin_table,
        )
        mixing_term = dot(normed_low, projected_grad, 0, 0)
        output_term = dot(attn_grad_all, attended, 0, 0)
        gains_term = jnp.stack([gain_one_grad[0], gain_two_grad[0]], 1)
        gains_term = jnp.pad(gains_term, ((0, 0), (0, PAD - 2)))
        attn_term = jnp.concatenate([mixing_term, output_term, gains_term], 1).astype(narrow)
        attn_term = attn_term.reshape(groups, halves * rings, fsdp_rows, -1).transpose(1, 0, 2, 3)
        attn_total = lax.psum_scatter(attn_term, ("half", "ring"), scatter_dimension=0, tiled=False)
        attn_total = exchange_seq(attn_total).astype(single)
        back, _ = norm_back(scatter_seq(normed_part), inputs, gains_float[0])
        tokens_gradient = (hidden_grad + back)[None]

    def columns(first, width):
        return attn_total[:, :, first : first + width].transpose(1, 0, 2).reshape(fsdp_rows, -1)

    mixing_gradient = jnp.concatenate(
        [
            columns(0, q_width),
            columns(q_width, k_width),
            columns(q_width + k_width, k_width),
        ],
        1,
    )
    output_gradient = columns(mix_width, q_width)
    gains_gradient = jnp.sum(attn_total[:, :, mix_width + q_width :][:, :, :2], axis=0)

    return (
        layer_output,
        tokens_gradient,
        mixing_gradient,
        output_gradient,
        gains_gradient,
        gate_gradient,
        up_gradient,
        down_gradient,
        logits_rows[None],
    )


def solution(mesh):
    groups, shards = mesh.shape["seq"], mesh.shape["fsdp"]
    halves = 2 if (EXPERTS // groups) % 2 == 0 and (groups, shards) == (4, 8) else 1
    rings = shards // halves
    grid = Mesh(mesh.devices.reshape(groups, halves, rings), ("seq", "half", "ring"))
    fsdp = ("half", "ring")
    every = ("seq", "half", "ring")
    in_specs = (
        P(fsdp, "seq", None),
        P(every, None),
        P(every, None),
        P(every, None),
        P(fsdp, "seq", None),
        P(fsdp, "seq", None),
        P(fsdp, "seq", None),
        P(fsdp, None, None),
        P(fsdp, None, None),
        P(fsdp, None),
        P(fsdp, "seq", None),
    )
    out_specs = (
        P(fsdp, "seq", None),
        P(fsdp, "seq", None),
        P(every, None),
        P(every, None),
        P(every, None),
        P(fsdp, "seq", None),
        P(fsdp, "seq", None),
        P(fsdp, "seq", None),
        P(fsdp, "seq", None),
    )
    return jax.shard_map(
        functools.partial(local, halves, rings),
        mesh=grid,
        in_specs=in_specs,
        out_specs=out_specs,
        check_vma=False,
    )
```

```python
import functools
import math

import jax
import jax.numpy as jnp
import numpy as np
from jax import lax
from jax.experimental import pallas as pl
from jax.experimental.pallas import tpu as pltpu
from jax.sharding import Mesh
from jax.sharding import PartitionSpec as P

D = 1536
HEADS = 24
KV_HEADS = 8
HEAD_DIM = 64
FF = 512
EXPERTS = 40
TOP = 8
QROWS = 256
PAD = 128

epsilon = 1e-05
rope_base = 10000.0
single = jnp.float32
narrow = jnp.bfloat16
MESH = pl.DeviceIdType.MESH


def rotary_tables(positions):
    half_width = HEAD_DIM // 2
    frequency = rope_base ** (-2.0 * jnp.arange(half_width, dtype=single) / HEAD_DIM)
    angles = positions.astype(single)[:, None] * frequency[None, :]
    cos_table = jnp.cos(angles)
    sin_table = jnp.sin(angles)
    return (jnp.concatenate([cos_table, cos_table], 1), jnp.concatenate([sin_table, sin_table], 1))


def softmax_last(logit_rows):
    row_max = jnp.max(logit_rows, axis=-1, keepdims=True)
    exponent = jnp.exp(logit_rows - row_max)
    return exponent / jnp.sum(exponent, axis=-1, keepdims=True)


def swap(value, axis, step, size):
    return lax.ppermute(value, axis, [(i, i ^ step) for i in range(size)])


def dot(left, right, left_dim, right_dim):
    return lax.dot_general(
        left, right, (((left_dim,), (right_dim,)), ((), ())), preferred_element_type=single
    )


def rope(values, cos_row, sin_row):
    width = values.shape[-1]
    lane = lax.broadcasted_iota(jnp.int32, values.shape, 1) % HEAD_DIM
    turned = jnp.where(
        lane < HEAD_DIM // 2,
        -pltpu.roll(values, width - HEAD_DIM // 2, 1),
        pltpu.roll(values, HEAD_DIM // 2, 1),
    )
    return values * cos_row + turned * sin_row


def rope_back(values, cos_row, sin_row):
    width = values.shape[-1]
    lane = lax.broadcasted_iota(jnp.int32, values.shape, 1) % HEAD_DIM
    scaled = values * sin_row
    turned = jnp.where(
        lane < HEAD_DIM // 2,
        pltpu.roll(scaled, width - HEAD_DIM // 2, 1),
        -pltpu.roll(scaled, HEAD_DIM // 2, 1),
    )
    return values * cos_row + turned


def wide(table, width):
    return jnp.concatenate([table] * (width // table.shape[1]), axis=1)


def stacked(ref, at, kv, size):
    group_size = HEADS // KV_HEADS
    return jnp.concatenate(
        [
            ref[at : at + size, (kv * group_size + g) * HEAD_DIM : (kv * group_size + g + 1) * HEAD_DIM]
            for g in range(group_size)
        ],
        axis=0,
    )


def key_scores(keys, queries, at, size):
    scores = dot(keys, queries, 1, 1) * (1.0 / math.sqrt(HEAD_DIM))
    shape = scores.shape
    key_at = lax.broadcasted_iota(jnp.int32, shape, 0)
    query_at = lax.broadcasted_iota(jnp.int32, shape, 1) % size + at
    return jnp.where(key_at <= query_at, scores, -jnp.inf)


def attention_body(
    tok_ref, mix_ref, exit_ref, gain_ref, cos_ref, sin_ref,
    normed_ref, q_ref, k_ref, v_ref, att_ref, log_ref, part_ref,
):
    seq_len = tok_ref.shape[0]
    size = QROWS
    for at in range(0, seq_len, size):
        project_rows(
            at, size, tok_ref[at : at + size], mix_ref[...], gain_ref[0:1],
            cos_ref, sin_ref, normed_ref, q_ref, k_ref, v_ref,
        )
    attend_rows(q_ref, k_ref, v_ref, att_ref, log_ref)
    for at in range(0, seq_len, size):
        part_ref[at : at + size] = dot(att_ref[at : at + size], exit_ref[...], 1, 1).astype(narrow)


def attention_call(tokens_all, mixing_own, exit_own, gains, cos_table, sin_table):
    seq_len = tokens_all.shape[0]
    q_width = exit_own.shape[1]
    k_width = (mixing_own.shape[1] - q_width) // 2
    group_size = HEADS // KV_HEADS
    blocks = k_width // HEAD_DIM * (seq_len // QROWS)
    shape = jax.ShapeDtypeStruct
    return pl.pallas_call(
        attention_body,
        out_shape=[
            shape((seq_len, D), narrow),
            shape((seq_len, q_width), narrow),
            shape((seq_len, k_width), narrow),
            shape((seq_len, k_width), narrow),
            shape((seq_len, q_width), narrow),
            shape((blocks, 1, group_size * QROWS), single),
            shape((seq_len, D), narrow),
        ],
        cost_estimate=pl.CostEstimate(
            flops=2 * seq_len * D * (mixing_own.shape[1] + q_width) + 4 * seq_len**2 * q_width * 4,
            bytes_accessed=seq_len * D * 6, transcendentals=0,
        ),
        name="attention_forward",
    )(tokens_all, mixing_own, exit_own, gains, cos_table, sin_table)


def norm_back(grads, values, gain_row):
    inverse = lax.rsqrt(jnp.mean(values * values, axis=-1, keepdims=True) + epsilon)
    normal = values * inverse
    scaled = grads * gain_row
    back = inverse * (scaled - normal * jnp.mean(scaled * normal, axis=-1, keepdims=True))
    return back, jnp.sum(grads * normal, axis=0, keepdims=True)


def attend_back_rows(out_grad, q_ref, k_ref, v_ref, log_ref, pg_ref, keys_sum, values_sum):
    seq_len, k_width = k_ref.shape
    q_width = q_ref.shape[1]
    size = QROWS
    group_size = HEADS // KV_HEADS
    scale = 1.0 / math.sqrt(HEAD_DIM)
    for kv in range(k_width // HEAD_DIM):
        lanes = slice(kv * HEAD_DIM, (kv + 1) * HEAD_DIM)
        keys_sum[...] = jnp.zeros_like(keys_sum)
        values_sum[...] = jnp.zeros_like(values_sum)
        for block in range(seq_len // size):
            at = block * size
            end = at + size
            queries = stacked(q_ref, at, kv, size)
            grads = stacked(out_grad, at, kv, size)
            keys, values = k_ref[:end, lanes], v_ref[:end, lanes]
            scores = key_scores(keys, queries, at, size)
            soft = jnp.exp(scores - log_ref[kv * (seq_len // size) + block])
            values_sum[:end] += dot(soft.astype(narrow), grads, 1, 0)
            soft_grad = dot(values, grads, 1, 1)
            delta = jnp.sum(soft * soft_grad, axis=0, keepdims=True)
            scores_grad = (soft * (soft_grad - delta)).astype(narrow)
            keys_sum[:end] += dot(scores_grad, queries, 1, 0) * scale
            query_grad = dot(keys, scores_grad, 0, 0) * scale
            for g in range(group_size):
                head = kv * group_size + g
                pg_ref[at:end, head * HEAD_DIM : (head + 1) * HEAD_DIM] = (
                    query_grad[:, g * size : (g + 1) * size].T.astype(narrow)
                )
        first = q_width + kv * HEAD_DIM
        pg_ref[:, first : first + HEAD_DIM] = keys_sum[...].astype(narrow)
        first += k_width
        pg_ref[:, first : first + HEAD_DIM] = values_sum[...].astype(narrow)


def project_back_rows(pg_ref, mix_ref, tok_ref, cos_ref, sin_ref, part_ref, turned, size):
    gain = jnp.zeros((1, D), single)
    for at in range(0, tok_ref.shape[0], size):
        rows = slice(at, at + size)
        pg_ref[rows, :turned] = rope_back(
            pg_ref[rows, :turned].astype(single), wide(cos_ref[rows], turned),
            wide(sin_ref[rows], turned),
        ).astype(narrow)
        normed_part = dot(pg_ref[rows], mix_ref, 1, 1)
        if len(part_ref.shape) == 3:
            part_ref[at // size] = normed_part.astype(narrow)
        else:
            part_ref[rows] = normed_part.astype(narrow)
        values = tok_ref[rows].astype(single)
        inverse = lax.rsqrt(jnp.mean(values * values, axis=-1, keepdims=True) + epsilon)
        gain = gain + jnp.sum(normed_part * (values * inverse), axis=0, keepdims=True)
    return gain


def attention_back_body(
    grad_ref, exit_ref, mix_ref, q_ref, k_ref, v_ref, log_ref, tok_ref, cos_ref, sin_ref,
    pg_ref, part_ref, gain_ref,
    out_grad, keys_sum, values_sum,
):
    size = QROWS
    for at in range(0, tok_ref.shape[0], size):
        out_grad[at : at + size] = dot(grad_ref[at : at + size], exit_ref[...], 1, 0).astype(narrow)
    attend_back_rows(out_grad, q_ref, k_ref, v_ref, log_ref, pg_ref, keys_sum, values_sum)
    turned = q_ref.shape[1] + k_ref.shape[1]
    gain_ref[...] = project_back_rows(
        pg_ref, mix_ref[...], tok_ref, cos_ref, sin_ref, part_ref, turned, size
    )


def totals(wire, begin, first, third, zed, buffers, out_send, own_out, half_out):
    sources = (first, third, zed)
    for g in (1, 0):
        loads = [wire.near(ref.at[g], buffers.at[i]) for i, ref in enumerate(sources)]
        for load in loads:
            load.wait()
        total = buffers[0].astype(single) + buffers[1].astype(single) + buffers[2].astype(single)
        if g:
            out_send[...] = total.astype(narrow)
            key = wire.plan(out_send, half_out, wire.to_half)
            begin(key)
        else:
            buffers[0] = total.astype(narrow)
            wire.near(buffers.at[0], own_out).wait()


def backward_body(
    ba_ref, bo_ref, oa_ref, oo_ref, pickall_ref, tokall_ref, normed_ref, gg_ref, gu_ref, gd_ref,
    tok_ref, att_ref, hid_ref, gain_ref, cot_ref, wall_ref, q_ref, k_ref, v_ref, log_ref, cos_ref, sin_ref,
    slot_ref, table_ref, otab_ref,
    tgrad_ref, layer_ref, lgrad_ref, attn_ref,
    ra_ref, mo_ref, ma_ref, c1_ref, c3_ref, zb_ref, own_ref, hx_ref,
    pg_ref, free, gw, r1, r2, r3, fin, attn_in,
    ag, out_grad, keys_sum, values_sum, land_a, land_b, land_h, land_m, sums, own_rows, buffers, far,
    leave, passed, passing, values, pick, stage, route_own, route_send, land_r, quarters, land_q, logits,
    send, recv, local,
):
    wire = Wire(send, recv, local)
    s, groups = wire.s, wire.groups
    size = hid_ref.shape[0]
    q_width, k_width = q_ref.shape[1], k_ref.shape[1]
    mix_width = q_width + 2 * k_width
    terms = (gg_ref, gu_ref, gd_ref)
    wire.meet()

    middle = size // 2

    def scatter(source, landing):
        return wire.scatter(lambda j: source.at[s ^ j], landing)

    def scatter_on(keys, source, landing, which):
        loads = [
            wire.near(source.at[s ^ 2, pl.ds(0, middle)], passed.at[0]),
            wire.near(source.at[s ^ 1, pl.ds(middle, middle)], passed.at[1]),
        ]
        for load in loads:
            load.wait()
        wire.scatter_on(
            keys, landing, lambda j: passed[0 if j == 2 else 1].astype(single), passing.at[which]
        )

    def quarter_sends(source, landing):
        return [
            wire.go(source.at[s ^ j], landing.at[j - 1], wire.to_seq[j]) for j in range(1, groups)
        ]

    def fetch(source, b):
        loads = [wire.near(source, values)]
        if b is not None:
            loads.append(wire.near(pickall_ref.at[b], pick))
        for load in loads:
            load.wait()

    def combine(j):
        return dot(pick[:, j * size : (j + 1) * size], values[...], 0, 0).astype(narrow)

    def combine_out(target):
        for j in range(groups):
            stage[j] = combine(j)
        wire.near(stage, target).wait()

    def own_block(source):
        wire.near(source.at[s], own_rows).wait()
        return own_rows[...].astype(single)

    core_go = []
    for t in range(3):
        core_go.append(
            (
                wire.go(terms[t].at[3], c3_ref.at[t], wire.to_core),
                wire.go(terms[t].at[1], c1_ref.at[t], wire.to_core),
            )
        )
    z_go = []

    def send_far(t, which=(1, 0)):
        if which[0]:
            wire.come(core_go[t][0])
            z_go.append([])
        if t >= 2:
            for k in z_go[t - 2]:
                wire.leave(k)
        for g in which:
            loads = [
                wire.near(terms[t].at[2, g], buffers.at[0]),
                wire.near(c3_ref.at[t, g], buffers.at[1]),
            ]
            for load in loads:
                load.wait()
            far[t % 2, g] = (buffers[0].astype(single) + buffers[1].astype(single)).astype(narrow)
            z_go[t].append(wire.go(far.at[t % 2, g], zb_ref.at[t, g], wire.to_z))

    send_far(0, (1,))
    fetch(bo_ref, 1)
    combine_out(mo_ref)
    other_go = scatter(mo_ref, land_a)
    send_far(0, (0,))
    fetch(ba_ref, 0)
    combine_out(ra_ref)
    own_go = scatter(ra_ref, land_b)
    scatter_on(other_go, mo_ref, land_a, 0)

    own_count = slot_ref.shape[0]
    slots = slot_ref.shape[1] // 2
    ids = own_ids(own_count, 2 * own_count)

    def route_rows(b, table):
        total = jnp.zeros((TOP, groups * size), single)
        for e in range(own_count):
            mine = pick[e * slots : (e + 1) * slots].astype(single)
            row = jnp.sum(mine * slot_ref[e, b * slots : (b + 1) * slots], axis=0, keepdims=True)
            total = total + jnp.where(table[0:TOP] == ids[e], row, 0.0)
        return total

    route_own[...] = route_rows(0, table_ref)
    fetch(oa_ref, None)
    combine_out(ma_ref)
    total = wire.scatter_end(other_go, land_a, own_block(mo_ref))
    sums[...] = total.astype(narrow)
    half_go = wire.go(sums, land_h, wire.to_half)
    scatter_on(own_go, ra_ref, land_b, 1)
    send_far(1)
    for k in other_go:
        wire.leave(k)
    fetch(oo_ref, 1)
    combine_out(mo_ref)
    route_send[...] = route_rows(1, otab_ref)
    route_go = wire.go(route_send, land_r, wire.to_half)
    total = wire.scatter_end(own_go, land_b, own_block(ra_ref))
    wire.come(half_go)
    total = total + land_h[...].astype(single)
    back, gain_two = norm_back(total, hid_ref[...], gain_ref[1:2])
    hidden_grad = cot_ref[...].astype(single) + back
    tgrad_ref[...] = hidden_grad
    ag[s] = hidden_grad.astype(narrow)
    grad_go = wire.gather(ag.at[s], ag)
    wire.come(route_go)
    total = route_own[...] + land_r[...]
    for j in range(groups):
        quarters[j] = total[:, j * size : (j + 1) * size]
        logits[j] = table_ref[TOP : 2 * TOP, j * size : (j + 1) * size]
    quarter_go = quarter_sends(quarters, land_q)

    leave_go = []

    def now(k):
        wire.remotes[k].start()

    def finish_term(t, begin):
        wire.come(core_go[t][1], *z_go[t])
        if t >= 2:
            wire.leave(leave_go[t - 2])
        leave_go.append(len(wire.remotes))
        totals(
            wire, begin, terms[t].at[0], c1_ref.at[t], zb_ref.at[t], buffers, leave.at[t % 2],
            own_ref.at[t], hx_ref.at[t],
        )

    finish_term(0, now)
    wire.gather_on(grad_go, ag)
    send_far(2)
    tok_rows = values.at[pl.ds(0, groups * size)]
    load_tok = wire.near(tokall_ref, tok_rows)
    wire.gather_end(grad_go)
    moe_go = scatter(mo_ref, land_a)
    exit_own = wall_ref[:, mix_width : mix_width + q_width]
    for j in range(groups):
        out_grad[j * size : (j + 1) * size] = dot(ag[j], exit_own, 1, 0).astype(narrow)
    attend_back_rows(out_grad, q_ref, k_ref, v_ref, log_ref, pg_ref, keys_sum, values_sum)
    load_tok.wait()
    gain_one = project_back_rows(
        pg_ref, wall_ref[:, :mix_width], tok_rows, cos_ref, sin_ref, stage, q_width + k_width, size
    )
    norm_go = scatter(stage, land_b)
    load_normed = wire.near(normed_ref, tok_rows)
    for k in other_go[4:] + own_go[4:]:
        wire.leave(k)
    scatter_on(moe_go, mo_ref, land_a, 0)
    finish_term(1, now)
    wire.scatter_on(
        norm_go, land_b,
        lambda j: stage[s ^ j, pl.ds(0 if j == 2 else middle, middle)].astype(single),
        passing.at[2],
    )
    total = wire.scatter_end(moe_go, land_a, own_block(mo_ref))
    for j in (1, 2):
        pl.semaphore_signal(free, inc=1, device_id=wire.to_seq[j], device_id_type=MESH)
    wire.leave(half_go)
    sums[...] = total.astype(narrow)
    moe_half_go = wire.go(sums, land_m, wire.to_half)

    pl.semaphore_wait(free, 2)
    moe_own_go = scatter(ma_ref, land_a)

    _, shards, few, width = gw.shape
    f, last = wire.f, mix_width + q_width
    shape = (groups, shards, few)
    load_normed.wait()
    gw[:, :, :, :mix_width] = (
        dot(tok_rows[...], pg_ref[...], 0, 0).astype(narrow).reshape(shape + (mix_width,))
    )
    grads = ag[...].reshape(groups * size, D)
    gw[:, :, :, mix_width:last] = (
        dot(grads, att_ref[...], 0, 0).astype(narrow).reshape(shape + (q_width,))
    )
    gains = jnp.concatenate([gain_one, gain_two, jnp.zeros((width - last - 2, D), single)], axis=0)
    gw[:, :, :, last:] = gains.T.astype(narrow).reshape(shape + (width - last,))
    pair_go = [wire.go(gw.at[:, f ^ (m + 1)], r1.at[m // 2], wire.to_core) for m in (2, 6, 0, 4)]
    scatter_on(moe_own_go, ma_ref, land_a, 1)
    total = wire.scatter_end(norm_go, land_b, stage[s].astype(single))
    back, _ = norm_back(total, tok_ref[...].astype(single), gain_ref[0:1])
    tgrad_ref[...] += back
    wire.come(*pair_go)

    def pair_sum(m):
        return gw[:, f ^ m].astype(single) + r1[m // 2].astype(single)

    gw[:, f ^ 2] = pair_sum(2).astype(narrow)
    go_2 = wire.go(gw.at[:, f ^ 2], r2.at[0], wire.to_z)
    gw[:, f ^ 6] = pair_sum(6).astype(narrow)
    go_6 = wire.go(gw.at[:, f ^ 6], r2.at[1], wire.to_z)
    wire.come(*quarter_go)
    route_grad = quarters[s]
    for j in range(groups - 1):
        route_grad = route_grad + land_q[j]
    top = logits[s]
    exponent = jnp.exp(top - jnp.max(top, axis=0, keepdims=True))
    gating = exponent / jnp.sum(exponent, axis=0, keepdims=True)
    lgrad_ref[...] = gating * (route_grad - jnp.sum(gating * route_grad, axis=0, keepdims=True))
    held = []
    finish_term(2, held.append)
    total = wire.scatter_end(moe_own_go, land_a, hid_ref[...] + own_block(ma_ref))
    wire.come(moe_half_go)
    layer_ref[...] = (total + land_m[...].astype(single)).astype(narrow)
    wire.come(go_6)
    gw[:, f ^ 4] = (pair_sum(4) + r2[1].astype(single)).astype(narrow)
    go_4 = wire.go(gw.at[:, f ^ 4], r3, wire.to_half)
    now(held[0])
    wire.come(go_2, go_4)
    fin[...] = pair_sum(0) + r2[0].astype(single) + r3[...].astype(single)
    attn_in[s] = fin[s]
    last_go = [wire.go(fin.at[s ^ j], attn_in.at[s], wire.to_seq[j]) for j in range(1, groups)]
    wire.come(*last_go)
    wire.near(attn_in, attn_ref).wait()
    wire.finish()


def backward_call(
    backs, outs, pick, terms, hidden, gains, cot, wall, q, k, v, logs, tokens_all,
    cos_table, sin_table, slot_grad, table, other_table, normed, tok, att, few,
):
    size = hidden.shape[0]
    seq_len = tokens_all.shape[0]
    groups = seq_len // size
    rings, halves, own, part, width = terms[0].shape
    slot_rows = pick.shape[1]
    shape = jax.ShapeDtypeStruct
    vmem = pl.BlockSpec(memory_space=pltpu.VMEM)
    hbm = pl.BlockSpec(memory_space=pl.ANY)
    block = (groups, size, D)
    slab = (groups, few, wall.shape[1])
    mix_width = q.shape[1] + 2 * k.shape[1]
    landing = pltpu.VMEM((6, size // 2, D), narrow)
    route = pltpu.VMEM((TOP, seq_len), single)
    count = 96
    return pl.pallas_call(
        backward_body,
        in_specs=[hbm] * 10 + [vmem] * 15,
        out_specs=[vmem] * 3 + [hbm] * 9,
        out_shape=[
            shape((size, D), single),
            shape((size, D), narrow),
            shape((TOP, size), single),
            shape(slab, single),
            shape(block, narrow),
            shape(block, narrow),
            shape(block, narrow),
            shape((3, halves, own, part, width), narrow),
            shape((3, halves, own, part, width), narrow),
            shape((3, halves, own, part, width), narrow),
            shape((3, own, part, width), narrow),
            shape((3, own, part, width), narrow),
        ],
        scratch_shapes=[
            pltpu.VMEM((seq_len, mix_width), narrow),
            pltpu.SemaphoreType.REGULAR,
            pltpu.VMEM((groups, 8) + slab[1:], narrow),
            pltpu.VMEM((4,) + slab, narrow),
            pltpu.VMEM((2,) + slab, narrow),
            pltpu.VMEM(slab, narrow),
            pltpu.VMEM(slab, single),
            pltpu.VMEM(slab, single),
            pltpu.VMEM(block, narrow),
            pltpu.VMEM(q.shape, narrow),
            pltpu.VMEM((seq_len, HEAD_DIM), single),
            pltpu.VMEM((seq_len, HEAD_DIM), single),
            landing,
            landing,
            pltpu.VMEM((size, D), narrow),
            pltpu.VMEM((size, D), narrow),
            pltpu.VMEM((size, D), narrow),
            pltpu.VMEM((size, D), narrow),
            pltpu.VMEM((3, own, part, width), narrow),
            pltpu.VMEM((2, halves, own, part, width), narrow),
            pltpu.VMEM((2, own, part, width), narrow),
            pltpu.VMEM((2, size // 2, D), narrow),
            pltpu.VMEM((3, 2, size // 2, D), narrow),
            pltpu.VMEM((slot_rows, D), narrow),
            pltpu.VMEM((slot_rows, seq_len), narrow),
            pltpu.VMEM(block, narrow),
            route,
            route,
            route,
            pltpu.VMEM((groups, TOP, size), single),
            pltpu.VMEM((groups - 1, TOP, size), single),
            pltpu.VMEM((groups, TOP, size), single),
            pltpu.SemaphoreType.DMA((count,)),
            pltpu.SemaphoreType.DMA((count,)),
            pltpu.SemaphoreType.DMA((count,)),
        ],
        compiler_params=pltpu.CompilerParams(
            collective_id=1, has_side_effects=True, vmem_limit_bytes=67_000_000
        ),
        cost_estimate=pl.CostEstimate(
            flops=150_000_000_000, bytes_accessed=100_000_000, transcendentals=0
        ),
        name="backward_exchange",
    )(
        *backs, *outs, pick, tokens_all, normed, *terms, tok, att, hidden, gains, cot, wall,
        q, k, v, logs, cos_table, sin_table, slot_grad, table, other_table,
    )


def attention_back_call(grads, exit_own, mixing_own, q, k, v, logs, tokens_all, cos_table, sin_table):
    seq_len = tokens_all.shape[0]
    shape = jax.ShapeDtypeStruct
    return pl.pallas_call(
        attention_back_body,
        out_shape=[
            shape((seq_len, mixing_own.shape[1]), narrow),
            shape((seq_len, D), narrow),
            shape((1, D), single),
        ],
        scratch_shapes=[
            pltpu.VMEM(q.shape, narrow),
            pltpu.VMEM((seq_len, HEAD_DIM), single),
            pltpu.VMEM((seq_len, HEAD_DIM), single),
        ],
        cost_estimate=pl.CostEstimate(
            flops=2 * seq_len * D * (mixing_own.shape[1] + q.shape[1])
            + 10 * seq_len**2 * q.shape[1] * 4,
            bytes_accessed=seq_len * D * 8, transcendentals=0,
        ),
        name="attention_backward",
    )(grads, exit_own, mixing_own, q, k, v, logs, tokens_all, cos_table, sin_table)


def project_rows(at, size, tok_rows, mix, gain_row, cos_ref, sin_ref, normed_ref, q_ref, k_ref, v_ref):
    rows = slice(at, at + size)
    q_width, k_width = q_ref.shape[1], k_ref.shape[1]
    values = tok_rows.astype(single)
    inverse = lax.rsqrt(jnp.mean(values * values, axis=-1, keepdims=True) + epsilon)
    normed = (values * inverse * gain_row).astype(narrow)
    normed_ref[rows] = normed
    projected = dot(normed, mix, 1, 0)
    width = q_width + k_width
    turned = rope(
        projected[:, :width], wide(cos_ref[rows], width), wide(sin_ref[rows], width)
    ).astype(narrow)
    q_ref[rows] = turned[:, :q_width]
    k_ref[rows] = turned[:, q_width:]
    v_ref[rows] = projected[:, width:].astype(narrow)


def attend_rows(q_ref, k_ref, v_ref, att_ref, log_ref):
    seq_len, k_width = k_ref.shape
    size = QROWS
    group_size = HEADS // KV_HEADS
    for kv in range(k_width // HEAD_DIM):
        lanes = slice(kv * HEAD_DIM, (kv + 1) * HEAD_DIM)
        for block in range(seq_len // size):
            at = block * size
            end = at + size
            queries = stacked(q_ref, at, kv, size)
            scores = key_scores(k_ref[:end, lanes], queries, at, size)
            top = jnp.max(scores, axis=0, keepdims=True)
            exponent = jnp.exp(scores - top)
            total = jnp.sum(exponent, axis=0, keepdims=True)
            soft = (exponent * (1.0 / total)).astype(narrow)
            log_ref[kv * (seq_len // size) + block] = top + jnp.log(total)
            out = dot(v_ref[:end, lanes], soft, 0, 0)
            for g in range(group_size):
                head = kv * group_size + g
                att_ref[at:end, head * HEAD_DIM : (head + 1) * HEAD_DIM] = (
                    out[:, g * size : (g + 1) * size].T.astype(narrow)
                )


class Wire:
    def __init__(self, send, recv, local):
        self.send, self.recv, self.local = send, recv, local
        self.remotes, self.landed, self.left, self.locals = [], [], [], 0
        s, h, r = lax.axis_index("seq"), lax.axis_index("half"), lax.axis_index("ring")
        groups = lax.axis_size("seq")
        self.s, self.h, self.r, self.f, self.groups = s, h, r, h * 4 + r, groups
        self.to_half, self.to_z, self.to_core = {"half": h ^ 1}, {"ring": r ^ 2}, {"ring": r ^ 1}
        self.to_seq = [{"seq": s ^ j} for j in range(groups)]

    def meet(self):
        barrier = pltpu.get_barrier_semaphore()
        peers = self.to_seq[1:] + [self.to_half, self.to_z, self.to_core]
        for peer in peers:
            pl.semaphore_signal(barrier, inc=1, device_id=peer, device_id_type=MESH)
        pl.semaphore_wait(barrier, len(peers))

    def go(self, source, target, peer):
        k = self.plan(source, target, peer)
        self.remotes[k].start()
        return k

    def plan(self, source, target, peer):
        k = len(self.remotes)
        self.remotes.append(
            pltpu.make_async_remote_copy(
                src_ref=source, dst_ref=target, send_sem=self.send.at[k],
                recv_sem=self.recv.at[k], device_id=peer, device_id_type=MESH,
            )
        )
        self.landed.append(False)
        self.left.append(False)
        return k

    def by_core(self, *sends):
        keys = [self.plan(*send) for send in sends]

        @pl.when(self.r % 2 == 0)
        def _():
            for k in keys:
                self.remotes[k].start()

        @pl.when(self.r % 2 == 1)
        def _():
            for k in reversed(keys):
                self.remotes[k].start()

        return keys

    def come(self, *which):
        for k in which:
            self.remotes[k].wait_recv()
            self.landed[k] = True

    def leave(self, k):
        if not self.left[k]:
            self.remotes[k].wait_send()
        self.left[k] = True

    def near(self, source, target):
        copy = pltpu.make_async_copy(source, target, self.local.at[self.locals])
        self.locals += 1
        copy.start()
        return copy

    def gather(self, source, target):
        s = self.s
        return [self.go(source, target.at[s], self.to_seq[j]) for j in (1, 2)]

    def gather_on(self, keys, target):
        s, middle = self.s, target.shape[1] // 2
        first, second = pl.ds(0, middle), pl.ds(middle, middle)
        self.come(keys[0])
        block = target.at[s ^ 1, first]
        keys.append(self.go(block, block, self.to_seq[2]))
        self.come(keys[1])
        block = target.at[s ^ 2, second]
        keys.append(self.go(block, block, self.to_seq[1]))

    def gather_end(self, keys):
        self.come(*keys[2:])

    def scatter(self, source, landing):
        middle = landing.shape[1]
        first, second = pl.ds(0, middle), pl.ds(middle, middle)
        return [
            self.go(source(3).at[first], landing.at[1], self.to_seq[1]),
            self.go(source(3).at[second], landing.at[3], self.to_seq[2]),
            self.go(source(1).at[first], landing.at[0], self.to_seq[1]),
            self.go(source(2).at[second], landing.at[2], self.to_seq[2]),
        ]

    def scatter_on(self, keys, landing, kept, passing):
        self.come(keys[0])
        passing[0] = (kept(2) + landing[1].astype(single)).astype(narrow)
        keys.append(self.go(passing.at[0], landing.at[4], self.to_seq[2]))
        self.come(keys[1])
        passing[1] = (kept(1) + landing[3].astype(single)).astype(narrow)
        keys.append(self.go(passing.at[1], landing.at[5], self.to_seq[1]))

    def scatter_end(self, keys, landing, own):
        self.come(*keys[2:])
        first = landing[0].astype(single) + landing[4].astype(single)
        second = landing[2].astype(single) + landing[5].astype(single)
        return own + jnp.concatenate([first, second], axis=0)

    def finish(self):
        for k, copy in enumerate(self.remotes):
            if not self.left[k]:
                copy.wait_send()
            if not self.landed[k]:
                copy.wait_recv()


def place_rows(table, ids, capacity, slots, pick_ref, share_ref, b):
    length = table.shape[1]
    picked, logits, order = table[0:TOP], table[TOP : 2 * TOP], table[2 * TOP : 2 * TOP + 1]
    exponent = jnp.exp(logits - jnp.max(logits, axis=0, keepdims=True))
    gating = exponent / jnp.sum(exponent, axis=0, keepdims=True)
    down = lax.broadcasted_iota(jnp.int32, (length, length), 0).astype(single)
    along = lax.broadcasted_iota(jnp.int32, (length, length), 1).astype(single)
    place_col = jnp.sum(jnp.where(order == down, along, 0.0), axis=1, keepdims=True)
    place_row = jnp.broadcast_to(place_col, (length, 128)).T[0:1]
    earlier = (place_col < place_row).astype(single).astype(narrow)
    hits = [jnp.sum((picked == i).astype(single), axis=0, keepdims=True) for i in ids]
    share = [
        jnp.sum(jnp.where(picked == i, gating, 0.0), axis=0, keepdims=True) for i in ids
    ]
    spare = jnp.zeros((8 - len(ids), length), single)
    rank = dot(jnp.concatenate(hits + [spare], axis=0).astype(narrow), earlier, 1, 0)
    slot_at = lax.broadcasted_iota(jnp.int32, (slots, length), 0).astype(single)
    for e in range(len(ids)):
        kept = (hits[e] > 0.0) & (rank[e : e + 1] < capacity)
        filled = jnp.where(kept, rank[e : e + 1], -1.0) == slot_at
        pick_ref[b, e * slots : (e + 1) * slots] = filled.astype(single).astype(narrow)
        share_ref[e, b * slots : (b + 1) * slots] = jnp.sum(
            jnp.where(filled, share[e], 0.0), axis=1, keepdims=True
        )


def own_ids(own, local_count):
    first = lax.axis_index("seq") * local_count + lax.axis_index("half") * own
    return [(first + e).astype(single) for e in range(own)]


def forward_body(
    tok_ref, pack_ref, cot_ref, wg_ref, wu_ref, wd_ref, cos_ref, sin_ref, table_ref,
    normed_ref, q_ref, k_ref, v_ref, att_ref, log_ref, hid_ref, gain_ref, share_ref, otab_ref,
    tokall_ref, wall_ref, pickall_ref, xa_ref, xo_ref, ya_ref, yo_ref, wout_ref,
    xown_ref, xother_ref, yown_ref, yother_ref,
    tokv, wv, part, landed, passing, xv, other_table, pick, picked_rows, send, recv, local,
):
    wire = Wire(send, recv, local)
    s, h, r, f, groups = wire.s, wire.h, wire.r, wire.f, wire.groups
    _, fsdp, few, width = wv.shape
    q_width, k_width = q_ref.shape[1], k_ref.shape[1]
    mix_width = q_width + 2 * k_width
    size = tok_ref.shape[0]
    middle = size // 2
    wire.meet()

    pack_go = [wire.go(pack_ref.at[s ^ j], wv.at[s, f], wire.to_seq[j]) for j in range(1, groups)]
    tok_go = wire.gather(tok_ref, tokv)
    table_go = wire.go(table_ref, other_table, wire.to_half)
    own_cot = wire.near(cot_ref, ya_ref.at[s])
    wv[s, f] = pack_ref[s]
    tokv[s] = tok_ref[...]

    sources = (wg_ref, wu_ref, wd_ref)

    def weights_first(t):
        own, other = sources[t].at[h], sources[t].at[1 - h]
        target = wout_ref.at[t, h, r]
        keys = wire.by_core((other, target, wire.to_half), (own, target, wire.to_z))
        wire.go(own, target, wire.to_core)
        return keys

    def weights_next(t, keys):
        wire.come(keys[0])
        came = wout_ref.at[t, 1 - h, r]
        on_z = wire.go(came, came, wire.to_z)
        wire.go(came, came, wire.to_core)
        wire.come(keys[1])
        beside = wout_ref.at[t, h, r ^ 2]
        wire.go(beside, beside, wire.to_core)
        return on_z

    def weights_last(t, key):
        wire.come(key)
        beyond = wout_ref.at[t, 1 - h, r ^ 2]
        wire.go(beyond, beyond, wire.to_core)

    wire.come(*pack_go)
    mine = wv.at[:, f]
    a_half = wire.go(mine, mine, wire.to_half)
    a_z = wire.go(mine, mine, wire.to_z)
    parts_go = [wire.go(mine, mine, wire.to_core)]
    wire.come(a_half)
    block = wv.at[:, f ^ 4]
    b_z = wire.go(block, block, wire.to_z)
    parts_go.append(wire.go(block, block, wire.to_core))
    wire.come(a_z)
    block = wv.at[:, f ^ 2]
    parts_go.append(wire.go(block, block, wire.to_core))
    cot_half = wire.go(cot_ref, yo_ref.at[s], wire.to_half)
    gate_first = weights_first(0)
    wire.gather_on(tok_go, tokv)
    cot_go = wire.gather(cot_ref, ya_ref)
    wire.come(b_z)
    block = wv.at[:, f ^ 6]
    parts_go.append(wire.go(block, block, wire.to_core))
    up_first = weights_first(1)

    own, slots = wout_ref.shape[3], share_ref.shape[1] // 2
    capacity = (groups * size * TOP + EXPERTS - 1) // EXPERTS
    ids = own_ids(own, 2 * own)
    place_rows(table_ref[...], ids, capacity, slots, pick, share_ref, 0)
    wire.gather_end(tok_go)
    wire.come(*parts_go)
    wire.gather_on(cot_go, ya_ref)
    keep_tok = wire.near(tokv, tokall_ref)
    keep_wall = wire.near(wv, wall_ref)
    depth = groups * fsdp * few
    gains = wv[:, :, :, mix_width + q_width :].reshape(depth, width - mix_width - q_width)
    gains = gains.astype(single).T[0:8]
    gain_ref[...] = gains
    for j in range(groups):
        project_rows(
            j * size, size, tokv[j], wv[:, :, :, :mix_width].reshape(depth, mix_width),
            gains[0:1], cos_ref, sin_ref, normed_ref, q_ref, k_ref, v_ref,
        )
    attend_rows(q_ref, k_ref, v_ref, att_ref, log_ref)
    exit_own = wv[:, :, :, mix_width : mix_width + q_width].reshape(depth, q_width)
    for j in (3, 1, 2, 0):
        rows = pl.ds(pl.multiple_of((s ^ j) * size, size), size)
        partial = dot(att_ref[rows], exit_own, 1, 1)
        if j:
            part[j - 1] = partial.astype(narrow)
        else:
            part_go = wire.scatter(lambda j: part.at[j - 1], landed)
            hid_ref[...] = tok_ref[...].astype(single) + partial

    def dispatch(b, source, target):
        wire.near(source, tokv).wait()
        whole = tokv[...].reshape(groups * size, D)
        for at in range(0, D, 512):
            picked_rows[:, at : at + 512] = dot(pick[b], whole[:, at : at + 512], 1, 0).astype(narrow)
        wire.near(picked_rows, target).wait()

    def kept(j):
        return part[j - 1, (0 if j == 2 else middle) : (middle if j == 2 else size)].astype(single)

    for k in tok_go[2:]:
        wire.leave(k)
    gate_next = weights_next(0, gate_first)
    wire.scatter_on(part_go, landed, kept, passing)
    keep_tok.wait()
    own_cot.wait()
    wire.gather_end(cot_go)
    dispatch(0, ya_ref, yown_ref)
    hidden = wire.scatter_end(part_go, landed, hid_ref[...])
    hid_ref[...] = hidden
    inverse = lax.rsqrt(jnp.mean(hidden * hidden, axis=-1, keepdims=True) + epsilon)
    xv[...] = (hidden * inverse * gains[1:2]).astype(narrow)
    row_half = wire.go(xv, xo_ref.at[s], wire.to_half)
    row_go = wire.gather(xv, xa_ref)
    own_row = wire.near(xv, xa_ref.at[s])
    down_first = weights_first(2)
    wire.come(table_go)
    otab_ref[...] = other_table[...]
    place_rows(other_table[...], ids, capacity, slots, pick, share_ref, 1)
    keep_pick = wire.near(pick, pickall_ref)
    wire.gather_on(row_go, xa_ref)
    wire.come(cot_half)
    up_next = weights_next(1, up_first)
    wire.come(row_half)
    other_go = wire.gather(xo_ref.at[s], xo_ref)
    cot_other = wire.gather(yo_ref.at[s], yo_ref)
    weights_last(0, gate_next)
    own_row.wait()
    wire.gather_end(row_go)
    dispatch(0, xa_ref, xown_ref)
    wire.gather_on(other_go, xo_ref)
    wire.gather_on(cot_other, yo_ref)
    down_next = weights_next(2, down_first)
    weights_last(1, up_next)
    wire.gather_end(other_go)
    dispatch(1, xo_ref, xother_ref)
    wire.gather_end(cot_other)
    dispatch(1, yo_ref, yother_ref)
    weights_last(2, down_next)
    keep_wall.wait()
    keep_pick.wait()
    wire.finish()


def forward_call(tokens, packed, cotangent, weights, cos_table, sin_table, table, q_width, k_width, slots):
    groups, few, width = packed.shape
    _, own, part, hidden_units = weights[0].shape
    size = tokens.shape[0]
    seq_len = size * groups
    blocks = k_width // HEAD_DIM * (seq_len // QROWS)
    shape = jax.ShapeDtypeStruct
    vmem = pl.BlockSpec(memory_space=pltpu.VMEM)
    hbm = pl.BlockSpec(memory_space=pl.ANY)
    rows = shape((groups, size, D), narrow)
    count = 80
    picked = shape((own * slots, D), narrow)
    return pl.pallas_call(
        forward_body,
        in_specs=[vmem] * 3 + [hbm] * 3 + [vmem] * 3,
        out_specs=[vmem] * 10 + [hbm] * 12,
        out_shape=[
            shape((seq_len, D), narrow),
            shape((seq_len, q_width), narrow),
            shape((seq_len, k_width), narrow),
            shape((seq_len, k_width), narrow),
            shape((seq_len, q_width), narrow),
            shape((blocks, 1, HEADS // KV_HEADS * QROWS), single),
            shape((size, D), single),
            shape((8, D), single),
            shape((own, 2 * slots, 1), single),
            shape(table.shape, single),
            rows,
            shape((groups, 8, few, width), narrow),
            shape((2, own * slots, seq_len), narrow),
            rows, rows, rows, rows,
            shape((3, 2, 4, own, part, hidden_units), narrow),
            picked, picked, picked, picked,
        ],
        scratch_shapes=[
            pltpu.VMEM((groups, size, D), narrow),
            pltpu.VMEM((groups, 8, few, width), narrow),
            pltpu.VMEM((groups - 1, size, D), narrow),
            pltpu.VMEM((6, size // 2, D), narrow),
            pltpu.VMEM((2, size // 2, D), narrow),
            pltpu.VMEM((size, D), narrow),
            pltpu.VMEM(table.shape, single),
            pltpu.VMEM((2, own * slots, seq_len), narrow),
            pltpu.VMEM((own * slots, D), narrow),
            pltpu.SemaphoreType.DMA((count,)),
            pltpu.SemaphoreType.DMA((count,)),
            pltpu.SemaphoreType.DMA((24,)),
        ],
        compiler_params=pltpu.CompilerParams(collective_id=0, has_side_effects=True),
        cost_estimate=pl.CostEstimate(
            flops=200_000_000_000, bytes_accessed=100_000_000, transcendentals=0
        ),
        name="forward_exchange",
    )(tokens, packed, cotangent, *weights, cos_table, sin_table, table)


def expert_body(
    batch, own_apart, where_ref, all_ref, g_ref, u_ref, d_ref, *refs,
):
    _, halves, rings, _, part, width = all_ref.shape
    pieces = halves * rings
    x_refs, y_refs, w_ref = refs[:batch], refs[batch : 2 * batch], refs[2 * batch]
    refs = refs[2 * batch + 1 :]
    out_refs, row_refs, slot_ref = refs[:batch], refs[batch : 2 * batch], refs[2 * batch]
    gg_ref, gu_ref, gd_ref, held, sems = refs[2 * batch + 1 :]
    half, ring = where_ref[0], where_ref[1]
    e = pl.program_id(0)
    slot = lax.rem(e, 2)

    def each(expert, slot, act):
        for t, own_ref in enumerate((g_ref, u_ref, d_ref)):
            for g in range(halves):
                for r in range(rings):
                    at = g * rings + r
                    target, sem = held.at[slot, t, at], sems.at[slot, t, at]
                    if not own_apart:
                        act(pltpu.make_async_copy(all_ref.at[t, g, r, expert], target, sem))
                        continue
                    own = (half == g) & (ring == r)

                    @pl.when(own)
                    def _():
                        act(pltpu.make_async_copy(own_ref.at[g, expert], target, sem))

                    @pl.when(jnp.logical_not(own))
                    def _():
                        act(pltpu.make_async_copy(all_ref.at[t, g, r, expert], target, sem))

    @pl.when(e == 0)
    def _():
        each(e, slot, lambda copy: copy.start())

    @pl.when(e + 1 < pl.num_programs(0))
    def _():
        each(e + 1, 1 - slot, lambda copy: copy.start())

    for t in range(3):
        for at in range(pieces):
            pltpu.make_async_copy(
                all_ref.at[t, at // rings, at % rings, e], held.at[slot, t, at], sems.at[slot, t, at]
            ).wait()

    def weight(t):
        return held[slot, t].reshape(pieces * part, width)

    def write(ref, value):
        for g in range(halves):
            for r in range(rings):
                at = (g * rings + r) * part
                ref[r ^ ring if own_apart else r, g ^ half, 0] = value[at : at + part].astype(ref.dtype)

    slots = x_refs[0].shape[1]

    def split(outs, value):
        for b, ref in enumerate(outs):
            ref[0] = value[b * slots : (b + 1) * slots].astype(ref.dtype)

    rows = jnp.concatenate([ref[0] for ref in x_refs], axis=0)
    cots = jnp.concatenate([ref[0] for ref in y_refs], axis=0)
    share = w_ref[0]
    gate, up, down = weight(0), weight(1), weight(2)
    gate_pre = dot(rows, gate, 1, 0)
    up_pre = dot(rows, up, 1, 0)
    sig = jax.nn.sigmoid(gate_pre)
    mid = (gate_pre * sig * up_pre).astype(narrow)
    expert_out = dot(mid, down, 1, 1)
    cot_float = cots.astype(single)
    slot_ref[0] = jnp.sum(cot_float * expert_out, axis=-1, keepdims=True)
    split(out_refs, expert_out * share)
    out_low = (cot_float * share).astype(narrow)
    mid_grad = dot(out_low, down, 1, 0)
    write(gd_ref, dot(out_low, mid, 0, 0))
    gate_grad = (mid_grad * up_pre * sig * (1.0 + gate_pre * (1.0 - sig))).astype(narrow)
    up_grad = (mid_grad * gate_pre * sig).astype(narrow)
    split(row_refs, dot(gate_grad, gate, 1, 1) + dot(up_grad, up, 1, 1))
    both = dot(rows, jnp.concatenate([gate_grad, up_grad], axis=1), 0, 0)
    write(gg_ref, both[:, :width])
    write(gu_ref, both[:, width:])


def expert_call(where, gathered, weights, own_apart, rows, cots, share):
    _, halves, rings, own, part, width = gathered.shape
    batch = len(rows)
    _, slots, depth = rows[0].shape
    pieces = halves * rings
    weight_spec = pl.BlockSpec((rings, halves, 1, part, width), lambda e, h: (0, 0, e, 0, 0))
    row_spec = pl.BlockSpec((1, slots, depth), lambda e, h: (e, 0, 0))
    share_spec = pl.BlockSpec((1, batch * slots, 1), lambda e, h: (e, 0, 0))
    shape = jax.ShapeDtypeStruct
    row_shape = shape((own, slots, depth), narrow)
    outs = pl.pallas_call(
        functools.partial(expert_body, batch, own_apart),
        grid_spec=pltpu.PrefetchScalarGridSpec(
            num_scalar_prefetch=1,
            grid=(own,),
            in_specs=[pl.BlockSpec(memory_space=pl.ANY)] * 4
            + [row_spec] * (2 * batch)
            + [share_spec],
            out_specs=[row_spec] * (2 * batch) + [share_spec] + [weight_spec] * 3,
            scratch_shapes=[
                pltpu.VMEM((2, 3, pieces, part, width), narrow),
                pltpu.SemaphoreType.DMA((2, 3, pieces)),
            ],
        ),
        out_shape=[row_shape] * (2 * batch)
        + [shape((own, batch * slots, 1), single)]
        + [shape((rings, halves, own, part, width), narrow)] * 3,
        cost_estimate=pl.CostEstimate(
            flops=9 * 2 * own * batch * slots * depth * width,
            bytes_accessed=12 * own * depth * width + 8 * batch * own * slots * depth,
            transcendentals=0,
        ),
        name="expert_ffn",
    )(where, gathered, *weights, *rows, *cots, share)
    return outs[:batch], outs[batch : 2 * batch], outs[2 * batch], outs[2 * batch + 1 :]


def local(
    halves, rings,
    tokens, mixing_weight, output_weight, norm_gains, expert_gate, expert_up, expert_down,
    gate_logits, routes, fill_order, cotangent,
):
    groups = lax.axis_size("seq")
    column = lax.axis_index("seq")
    half = lax.axis_index("half")
    ring = lax.axis_index("ring")
    paired = halves == 2
    tok_rows = tokens.shape[1]
    seq_len = tok_rows * groups
    capacity = (seq_len * TOP + EXPERTS - 1) // EXPERTS
    local_count = expert_gate.shape[1]
    own_count = local_count // halves
    part = expert_gate.shape[0]
    fsdp_rows = mixing_weight.shape[0]
    q_width = HEADS * HEAD_DIM // groups
    k_width = KV_HEADS * HEAD_DIM // groups
    mix_width = q_width + 2 * k_width
    own_kv = KV_HEADS // groups
    own_heads = HEADS // groups
    group_size = HEADS // KV_HEADS
    score_scale = 1.0 / math.sqrt(HEAD_DIM)
    query_all = HEADS * HEAD_DIM
    key_all = KV_HEADS * HEAD_DIM

    def gather_seq(value):
        parts = [value] + [swap(value, "seq", j, groups) for j in range(1, groups)]
        whole = jnp.zeros((groups,) + value.shape, value.dtype)
        for j, item in enumerate(parts):
            whole = lax.dynamic_update_index_in_dim(whole, item, column ^ j, 0)
        return whole.reshape((seq_len,) + value.shape[1:])

    def scatter_seq(value):
        blocks = value.reshape((groups, tok_rows) + value.shape[1:])
        total = lax.dynamic_index_in_dim(blocks, column, 0, False).astype(single)
        for j in range(1, groups):
            sent = lax.dynamic_index_in_dim(blocks, column ^ j, 0, False).astype(narrow)
            total = total + swap(sent, "seq", j, groups).astype(single)
        return total

    def exchange_seq(blocks):
        whole = lax.dynamic_update_index_in_dim(
            jnp.zeros_like(blocks), lax.dynamic_index_in_dim(blocks, column, 0, False), column, 0
        )
        for j in range(1, groups):
            sent = lax.dynamic_index_in_dim(blocks, column ^ j, 0, False)
            whole = lax.dynamic_update_index_in_dim(
                whole, swap(sent, "seq", j, groups), column ^ j, 0
            )
        return whole

    packed = jnp.concatenate(
        [
            mixing_weight[:, :query_all].reshape(fsdp_rows, groups, q_width),
            mixing_weight[:, query_all : query_all + key_all].reshape(fsdp_rows, groups, k_width),
            mixing_weight[:, query_all + key_all :].reshape(fsdp_rows, groups, k_width),
            output_weight.reshape(fsdp_rows, groups, q_width),
            jnp.broadcast_to(
                jnp.pad(norm_gains, ((0, 0), (0, PAD - 2)))[:, None], (fsdp_rows, groups, PAD)
            ),
        ],
        2,
    ).transpose(1, 0, 2)
    cos_table, sin_table = rotary_tables(jnp.arange(seq_len, dtype=jnp.int32))
    cos_table, sin_table = jnp.tile(cos_table, (1, 2)), jnp.tile(sin_table, (1, 2))
    own_weights = [
        item.transpose(1, 0, 2).reshape(halves, own_count, part, FF)
        for item in (expert_gate, expert_up, expert_down)
    ]
    inputs = tokens[0].astype(single)
    slots = (capacity + 15) // 16 * 16
    if paired:
        table = jnp.concatenate(
            [
                routes[0].astype(single).T,
                gate_logits[0].T,
                jnp.broadcast_to(fill_order[0].astype(single), (8, seq_len)),
            ],
            0,
        )
        (
            normed_low, queries, keys, values, attended, logs, hidden, gains_float, share,
            other_table, tokens_all, packed, pick, _, _, _, _, gathered,
            own_x, other_x, own_y, other_y,
        ) = forward_call(
            tokens[0], packed, cotangent[0], own_weights, cos_table, sin_table, table,
            q_width, k_width, slots,
        )
        tokens_all = tokens_all.reshape(seq_len, D)
        packed = packed.reshape(D, -1)
        mixing_own = packed[:, :mix_width]
        exit_own = packed[:, mix_width : mix_width + q_width]
        seq_rows = [item.reshape(own_count, slots, D) for item in (own_x, other_x)]
        cot_rows = [item.reshape(own_count, slots, D) for item in (own_y, other_y)]
    else:
        packed = exchange_seq(packed)
        packed = lax.all_gather(packed, ("half", "ring"), axis=0, tiled=False)
        packed = packed.transpose(1, 0, 2, 3).reshape(D, -1)
        mixing_own = packed[:, :mix_width]
        exit_own = packed[:, mix_width : mix_width + q_width]
        gains_float = packed[:, mix_width + q_width : mix_width + q_width + 2].astype(single).T
        tokens_all = gather_seq(tokens[0])
        gathered = jnp.stack(
            [lax.all_gather(item[0], "ring", axis=0, tiled=False)[None] for item in own_weights]
        )
        normed_low, queries, keys, values, attended, logs, attn_part = attention_call(
            tokens_all, mixing_own, exit_own, gains_float, cos_table, sin_table
        )
        hidden = inputs + scatter_seq(attn_part)
        scale_two = lax.rsqrt(jnp.mean(hidden * hidden, axis=-1, keepdims=True) + epsilon)
        seq_rows = [gather_seq((hidden * scale_two * gains_float[1]).astype(narrow))]
        cot_rows = [gather_seq(cotangent[0])]

    if not paired:
        pair_routes = routes
        pair_order = fill_order
        pair_gating = softmax_last(gate_logits)
        expert_ids = column * local_count + half * own_count + jnp.arange(own_count, dtype=jnp.int32)
        places = jnp.arange(seq_len, dtype=jnp.int32)
        chosen = (pair_routes[..., None] == expert_ids).astype(single)
        hits = jnp.sum(chosen, axis=2)
        token_weight = jnp.sum(pair_gating[..., None] * chosen, axis=2)
        place_of = jnp.sum(
            jnp.where(pair_order[:, :, None] == places, places[None, :, None], 0), axis=1
        )
        earlier = (place_of[:, None, :] < place_of[:, :, None]).astype(narrow)
        rank = jnp.einsum(
            "btu,bue->bte", earlier, hits.astype(narrow), preferred_element_type=single
        ).astype(jnp.int32)
        kept = (hits > 0) & (rank < capacity)
        flat_place = jnp.where(kept, rank + jnp.arange(own_count, dtype=jnp.int32) * slots, -1)
        flat_ids = jnp.arange(own_count * slots, dtype=jnp.int32)
        filled = flat_place[:, :, 0:1] == flat_ids
        for e in range(1, own_count):
            filled = filled | (flat_place[:, :, e : e + 1] == flat_ids)
        select = filled.astype(narrow)
        batch = select.shape[0]
        match = flat_place[:, :, :, None] == (
            jnp.arange(own_count, dtype=jnp.int32)[:, None] * slots
            + jnp.arange(slots, dtype=jnp.int32)[None, :]
        )
        slot_weight = jnp.sum(jnp.where(match, token_weight[..., None], 0.0), axis=1)
        share = slot_weight.transpose(1, 0, 2).reshape(own_count, batch * slots, 1)

        def dispatch(rows):
            return [
                lax.dot_general(
                    select[b], item, (((0,), (0,)), ((), ())), preferred_element_type=narrow
                ).reshape(own_count, slots, D)
                for b, item in enumerate(rows)
            ]

        def combine(b, values):
            return lax.dot_general(
                select[b],
                values.reshape(own_count * slots, D),
                (((1,), (0,)), ((), ())),
                preferred_element_type=narrow,
            )

        seq_rows, cot_rows = dispatch(seq_rows), dispatch(cot_rows)

    slot_out, slot_back, slot_grad, (gate_term, up_term, down_term) = expert_call(
        jnp.stack([half, ring]), gathered, own_weights, paired,
        seq_rows, cot_rows, share,
    )
    def by_row(total):
        return total.reshape(local_count, part, FF).transpose(1, 0, 2).astype(single)

    if paired:
        flat = (own_count * slots, D)
        (
            tokens_gradient, layer_output, logits_rows, attn_total,
            _, _, _, _, _, _, own_terms, other_terms,
        ) = backward_call(
            [item.reshape(flat) for item in slot_back], [item.reshape(flat) for item in slot_out],
            pick, (gate_term, up_term, down_term), hidden, gains_float, cotangent[0], packed,
            queries, keys, values, logs, tokens_all, cos_table, sin_table, slot_grad, table,
            other_table, normed_low, tokens[0], attended, fsdp_rows,
        )
        logits_rows = logits_rows.T
        tokens_gradient, layer_output = tokens_gradient[None], layer_output[None]

        def expert_gradient(own, other):
            return by_row(
                jnp.stack([jnp.where(half == 0, own, other), jnp.where(half == 0, other, own)])
            )

        gate_gradient = expert_gradient(own_terms[0], other_terms[0])
        up_gradient = expert_gradient(own_terms[1], other_terms[1])
        down_gradient = expert_gradient(own_terms[2], other_terms[2])
    else:
        slot_grad = slot_grad.reshape(own_count, batch, slots).transpose(1, 0, 2)
        weight_grad_tok = jnp.sum(jnp.where(match, slot_grad[:, None], 0.0), axis=3)
        route_part = jnp.sum(weight_grad_tok[:, :, None, :] * chosen, axis=-1)

        def send_routes(value):
            blocks = value.reshape(groups, tok_rows, TOP)
            total = lax.dynamic_index_in_dim(blocks, column, 0, False)
            for j in range(1, groups):
                sent = lax.dynamic_index_in_dim(blocks, column ^ j, 0, False)
                total = total + swap(sent, "seq", j, groups)
            return total

        route_grad = send_routes(route_part[0])
        gating = softmax_last(
            lax.dynamic_slice_in_dim(gate_logits[0], column * tok_rows, tok_rows, 0)
        )
        logits_rows = gating * (route_grad - jnp.sum(gating * route_grad, axis=-1, keepdims=True))

        def ring_sum(term):
            return lax.psum_scatter(term, "ring", scatter_dimension=0, tiled=False)

        normed_two_grad = scatter_seq(combine(0, slot_back[0]))
        gate_gradient, up_gradient, down_gradient = [
            by_row(ring_sum(term)) for term in (gate_term, up_term, down_term)
        ]
        moe_rows = scatter_seq(combine(0, slot_out[0]))
        layer_output = (hidden + moe_rows).astype(narrow)[None]
        back, gain_two_grad = norm_back(normed_two_grad, hidden, gains_float[1])
        hidden_grad = cotangent[0].astype(single) + back
        attn_grad_all = gather_seq(hidden_grad.astype(narrow))
        projected_grad, normed_part, gain_one_grad = attention_back_call(
            attn_grad_all, exit_own, mixing_own, queries, keys, values, logs, tokens_all,
            cos_table, sin_table,
        )
        mixing_term = dot(normed_low, projected_grad, 0, 0)
        output_term = dot(attn_grad_all, attended, 0, 0)
        gains_term = jnp.stack([gain_one_grad[0], gain_two_grad[0]], 1)
        gains_term = jnp.pad(gains_term, ((0, 0), (0, PAD - 2)))
        attn_term = jnp.concatenate([mixing_term, output_term, gains_term], 1).astype(narrow)
        attn_term = attn_term.reshape(groups, halves * rings, fsdp_rows, -1).transpose(1, 0, 2, 3)
        attn_total = lax.psum_scatter(attn_term, ("half", "ring"), scatter_dimension=0, tiled=False)
        attn_total = exchange_seq(attn_total).astype(single)
        back, _ = norm_back(scatter_seq(normed_part), inputs, gains_float[0])
        tokens_gradient = (hidden_grad + back)[None]

    def columns(first, width):
        return attn_total[:, :, first : first + width].transpose(1, 0, 2).reshape(fsdp_rows, -1)

    mixing_gradient = jnp.concatenate(
        [
            columns(0, q_width),
            columns(q_width, k_width),
            columns(q_width + k_width, k_width),
        ],
        1,
    )
    output_gradient = columns(mix_width, q_width)
    gains_gradient = jnp.sum(attn_total[:, :, mix_width + q_width :][:, :, :2], axis=0)

    return (
        layer_output,
        tokens_gradient,
        mixing_gradient,
        output_gradient,
        gains_gradient,
        gate_gradient,
        up_gradient,
        down_gradient,
        logits_rows[None],
    )


def solution(mesh):
    groups, shards = mesh.shape["seq"], mesh.shape["fsdp"]
    halves = 2 if (EXPERTS // groups) % 2 == 0 and (groups, shards) == (4, 8) else 1
    rings = shards // halves
    grid = Mesh(mesh.devices.reshape(groups, halves, rings), ("seq", "half", "ring"))
    fsdp = ("half", "ring")
    every = ("seq", "half", "ring")
    in_specs = (
        P(fsdp, "seq", None),
        P(every, None),
        P(every, None),
        P(every, None),
        P(fsdp, "seq", None),
        P(fsdp, "seq", None),
        P(fsdp, "seq", None),
        P(fsdp, None, None),
        P(fsdp, None, None),
        P(fsdp, None),
        P(fsdp, "seq", None),
    )
    out_specs = (
        P(fsdp, "seq", None),
        P(fsdp, "seq", None),
        P(every, None),
        P(every, None),
        P(every, None),
        P(fsdp, "seq", None),
        P(fsdp, "seq", None),
        P(fsdp, "seq", None),
        P(fsdp, "seq", None),
    )
    return jax.shard_map(
        functools.partial(local, halves, rings),
        mesh=grid,
        in_specs=in_specs,
        out_specs=out_specs,
        check_vma=False,
    )
```

```python
import functools
import math

import jax
import jax.numpy as jnp
import numpy as np
from jax import lax
from jax.experimental import pallas as pl
from jax.experimental.pallas import tpu as pltpu
from jax.sharding import Mesh
from jax.sharding import PartitionSpec as P

D = 1536
HEADS = 24
KV_HEADS = 8
HEAD_DIM = 64
FF = 512
EXPERTS = 40
TOP = 8
QROWS = 256
PAD = 128

epsilon = 1e-05
rope_base = 10000.0
single = jnp.float32
narrow = jnp.bfloat16
MESH = pl.DeviceIdType.MESH


def rotary_tables(positions):
    half_width = HEAD_DIM // 2
    frequency = rope_base ** (-2.0 * jnp.arange(half_width, dtype=single) / HEAD_DIM)
    angles = positions.astype(single)[:, None] * frequency[None, :]
    cos_table = jnp.cos(angles)
    sin_table = jnp.sin(angles)
    return (jnp.concatenate([cos_table, cos_table], 1), jnp.concatenate([sin_table, sin_table], 1))


def softmax_last(logit_rows):
    row_max = jnp.max(logit_rows, axis=-1, keepdims=True)
    exponent = jnp.exp(logit_rows - row_max)
    return exponent / jnp.sum(exponent, axis=-1, keepdims=True)


def swap(value, axis, step, size):
    return lax.ppermute(value, axis, [(i, i ^ step) for i in range(size)])


def dot(left, right, left_dim, right_dim):
    return lax.dot_general(
        left, right, (((left_dim,), (right_dim,)), ((), ())), preferred_element_type=single
    )


def rope(values, cos_row, sin_row):
    width = values.shape[-1]
    lane = lax.broadcasted_iota(jnp.int32, values.shape, 1) % HEAD_DIM
    turned = jnp.where(
        lane < HEAD_DIM // 2,
        -pltpu.roll(values, width - HEAD_DIM // 2, 1),
        pltpu.roll(values, HEAD_DIM // 2, 1),
    )
    return values * cos_row + turned * sin_row


def rope_back(values, cos_row, sin_row):
    width = values.shape[-1]
    lane = lax.broadcasted_iota(jnp.int32, values.shape, 1) % HEAD_DIM
    scaled = values * sin_row
    turned = jnp.where(
        lane < HEAD_DIM // 2,
        pltpu.roll(scaled, width - HEAD_DIM // 2, 1),
        -pltpu.roll(scaled, HEAD_DIM // 2, 1),
    )
    return values * cos_row + turned


def wide(table, width):
    return jnp.concatenate([table] * (width // table.shape[1]), axis=1)


def stacked(ref, at, kv, size):
    group_size = HEADS // KV_HEADS
    return jnp.concatenate(
        [
            ref[at : at + size, (kv * group_size + g) * HEAD_DIM : (kv * group_size + g + 1) * HEAD_DIM]
            for g in range(group_size)
        ],
        axis=0,
    )


def key_scores(keys, queries, at, size):
    scores = dot(keys, queries, 1, 1) * (1.0 / math.sqrt(HEAD_DIM))
    shape = scores.shape
    key_at = lax.broadcasted_iota(jnp.int32, shape, 0)
    query_at = lax.broadcasted_iota(jnp.int32, shape, 1) % size + at
    return jnp.where(key_at <= query_at, scores, -jnp.inf)


def attention_body(
    tok_ref, mix_ref, exit_ref, gain_ref, cos_ref, sin_ref,
    normed_ref, q_ref, k_ref, v_ref, att_ref, log_ref, part_ref,
):
    seq_len = tok_ref.shape[0]
    size = QROWS
    for at in range(0, seq_len, size):
        project_rows(
            at, size, tok_ref[at : at + size], mix_ref[...], gain_ref[0:1],
            cos_ref, sin_ref, normed_ref, q_ref, k_ref, v_ref,
        )
    attend_rows(q_ref, k_ref, v_ref, att_ref, log_ref)
    for at in range(0, seq_len, size):
        part_ref[at : at + size] = dot(att_ref[at : at + size], exit_ref[...], 1, 1).astype(narrow)


def attention_call(tokens_all, mixing_own, exit_own, gains, cos_table, sin_table):
    seq_len = tokens_all.shape[0]
    q_width = exit_own.shape[1]
    k_width = (mixing_own.shape[1] - q_width) // 2
    group_size = HEADS // KV_HEADS
    blocks = k_width // HEAD_DIM * (seq_len // QROWS)
    shape = jax.ShapeDtypeStruct
    return pl.pallas_call(
        attention_body,
        out_shape=[
            shape((seq_len, D), narrow),
            shape((seq_len, q_width), narrow),
            shape((seq_len, k_width), narrow),
            shape((seq_len, k_width), narrow),
            shape((seq_len, q_width), narrow),
            shape((blocks, 1, group_size * QROWS), single),
            shape((seq_len, D), narrow),
        ],
        cost_estimate=pl.CostEstimate(
            flops=2 * seq_len * D * (mixing_own.shape[1] + q_width) + 4 * seq_len**2 * q_width * 4,
            bytes_accessed=seq_len * D * 6, transcendentals=0,
        ),
        name="attention_forward",
    )(tokens_all, mixing_own, exit_own, gains, cos_table, sin_table)


def norm_back(grads, values, gain_row):
    inverse = lax.rsqrt(jnp.mean(values * values, axis=-1, keepdims=True) + epsilon)
    normal = values * inverse
    scaled = grads * gain_row
    back = inverse * (scaled - normal * jnp.mean(scaled * normal, axis=-1, keepdims=True))
    return back, jnp.sum(grads * normal, axis=0, keepdims=True)


def attend_back_rows(out_grad, q_ref, k_ref, v_ref, log_ref, pg_ref, keys_sum, values_sum):
    seq_len, k_width = k_ref.shape
    q_width = q_ref.shape[1]
    size = QROWS
    group_size = HEADS // KV_HEADS
    scale = 1.0 / math.sqrt(HEAD_DIM)
    for kv in range(k_width // HEAD_DIM):
        lanes = slice(kv * HEAD_DIM, (kv + 1) * HEAD_DIM)
        keys_sum[...] = jnp.zeros_like(keys_sum)
        values_sum[...] = jnp.zeros_like(values_sum)
        for block in range(seq_len // size):
            at = block * size
            end = at + size
            queries = stacked(q_ref, at, kv, size)
            grads = stacked(out_grad, at, kv, size)
            keys, values = k_ref[:end, lanes], v_ref[:end, lanes]
            scores = key_scores(keys, queries, at, size)
            soft = jnp.exp(scores - log_ref[kv * (seq_len // size) + block])
            values_sum[:end] += dot(soft.astype(narrow), grads, 1, 0)
            soft_grad = dot(values, grads, 1, 1)
            delta = jnp.sum(soft * soft_grad, axis=0, keepdims=True)
            scores_grad = (soft * (soft_grad - delta)).astype(narrow)
            keys_sum[:end] += dot(scores_grad, queries, 1, 0) * scale
            query_grad = dot(keys, scores_grad, 0, 0) * scale
            for g in range(group_size):
                head = kv * group_size + g
                pg_ref[at:end, head * HEAD_DIM : (head + 1) * HEAD_DIM] = (
                    query_grad[:, g * size : (g + 1) * size].T.astype(narrow)
                )
        first = q_width + kv * HEAD_DIM
        pg_ref[:, first : first + HEAD_DIM] = keys_sum[...].astype(narrow)
        first += k_width
        pg_ref[:, first : first + HEAD_DIM] = values_sum[...].astype(narrow)


def project_back_rows(pg_ref, mix_ref, tok_ref, cos_ref, sin_ref, part_ref, turned, size):
    gain = jnp.zeros((1, D), single)
    for at in range(0, tok_ref.shape[0], size):
        rows = slice(at, at + size)
        pg_ref[rows, :turned] = rope_back(
            pg_ref[rows, :turned].astype(single), wide(cos_ref[rows], turned),
            wide(sin_ref[rows], turned),
        ).astype(narrow)
        normed_part = dot(pg_ref[rows], mix_ref, 1, 1)
        if len(part_ref.shape) == 3:
            part_ref[at // size] = normed_part.astype(narrow)
        else:
            part_ref[rows] = normed_part.astype(narrow)
        values = tok_ref[rows].astype(single)
        inverse = lax.rsqrt(jnp.mean(values * values, axis=-1, keepdims=True) + epsilon)
        gain = gain + jnp.sum(normed_part * (values * inverse), axis=0, keepdims=True)
    return gain


def attention_back_body(
    grad_ref, exit_ref, mix_ref, q_ref, k_ref, v_ref, log_ref, tok_ref, cos_ref, sin_ref,
    pg_ref, part_ref, gain_ref,
    out_grad, keys_sum, values_sum,
):
    size = QROWS
    for at in range(0, tok_ref.shape[0], size):
        out_grad[at : at + size] = dot(grad_ref[at : at + size], exit_ref[...], 1, 0).astype(narrow)
    attend_back_rows(out_grad, q_ref, k_ref, v_ref, log_ref, pg_ref, keys_sum, values_sum)
    turned = q_ref.shape[1] + k_ref.shape[1]
    gain_ref[...] = project_back_rows(
        pg_ref, mix_ref[...], tok_ref, cos_ref, sin_ref, part_ref, turned, size
    )


def totals(wire, begin, first, third, zed, buffers, out_send, own_out, half_out):
    sources = (first, third, zed)
    for g in (1, 0):
        loads = [wire.near(ref.at[g], buffers.at[i]) for i, ref in enumerate(sources)]
        for load in loads:
            load.wait()
        total = buffers[0].astype(single) + buffers[1].astype(single) + buffers[2].astype(single)
        if g:
            out_send[...] = total.astype(narrow)
            key = wire.plan(out_send, half_out, wire.to_half)
            begin(key)
        else:
            buffers[0] = total.astype(narrow)
            wire.near(buffers.at[0], own_out).wait()


def backward_body(
    ba_ref, bo_ref, oa_ref, oo_ref, pickall_ref, tokall_ref, normed_ref, gg_ref, gu_ref, gd_ref,
    tok_ref, att_ref, hid_ref, gain_ref, cot_ref, wall_ref, q_ref, k_ref, v_ref, log_ref, cos_ref, sin_ref,
    slot_ref, table_ref, otab_ref,
    tgrad_ref, layer_ref, lgrad_ref, attn_ref,
    ra_ref, mo_ref, ma_ref, c1_ref, c3_ref, zb_ref, own_ref, hx_ref,
    pg_ref, free, gw, r1, r2, r3, fin, attn_in,
    ag, out_grad, keys_sum, values_sum, land_a, land_b, land_h, land_m, sums, own_rows, buffers, far,
    leave, passed, passing, values, pick, stage, route_own, route_send, land_r, quarters, land_q, logits,
    send, recv, local,
):
    wire = Wire(send, recv, local)
    s, groups = wire.s, wire.groups
    size = hid_ref.shape[0]
    q_width, k_width = q_ref.shape[1], k_ref.shape[1]
    mix_width = q_width + 2 * k_width
    terms = (gg_ref, gu_ref, gd_ref)
    wire.meet()

    middle = size // 2

    def scatter(source, landing):
        return wire.scatter(lambda j: source.at[s ^ j], landing)

    def scatter_on(keys, source, landing, which):
        loads = [
            wire.near(source.at[s ^ 2, pl.ds(0, middle)], passed.at[0]),
            wire.near(source.at[s ^ 1, pl.ds(middle, middle)], passed.at[1]),
        ]
        for load in loads:
            load.wait()
        wire.scatter_on(
            keys, landing, lambda j: passed[0 if j == 2 else 1].astype(single), passing.at[which]
        )

    def quarter_sends(source, landing):
        return [
            wire.go(source.at[s ^ j], landing.at[j - 1], wire.to_seq[j]) for j in range(1, groups)
        ]

    def fetch(source, b):
        loads = [wire.near(source, values)]
        if b is not None:
            loads.append(wire.near(pickall_ref.at[b], pick))
        for load in loads:
            load.wait()

    def combine(j):
        return dot(pick[:, j * size : (j + 1) * size], values[...], 0, 0).astype(narrow)

    def combine_out(target):
        for j in range(groups):
            stage[j] = combine(j)
        wire.near(stage, target).wait()

    def own_block(source):
        wire.near(source.at[s], own_rows).wait()
        return own_rows[...].astype(single)

    core_go = []
    for t in range(3):
        core_go.append(
            (
                wire.go(terms[t].at[3], c3_ref.at[t], wire.to_core),
                wire.go(terms[t].at[1], c1_ref.at[t], wire.to_core),
            )
        )
    fetch(bo_ref, 1)
    combine_out(mo_ref)
    other_go = scatter(mo_ref, land_a)
    z_go = []

    def send_far(t):
        wire.come(core_go[t][0])
        if t >= 2:
            for k in z_go[t - 2]:
                wire.leave(k)
        z_go.append([])
        for g in (1, 0):
            loads = [
                wire.near(terms[t].at[2, g], buffers.at[0]),
                wire.near(c3_ref.at[t, g], buffers.at[1]),
            ]
            for load in loads:
                load.wait()
            far[t % 2, g] = (buffers[0].astype(single) + buffers[1].astype(single)).astype(narrow)
            z_go[t].append(wire.go(far.at[t % 2, g], zb_ref.at[t, g], wire.to_z))

    send_far(0)
    fetch(ba_ref, 0)
    combine_out(ra_ref)
    own_go = scatter(ra_ref, land_b)
    scatter_on(other_go, mo_ref, land_a, 0)

    own_count = slot_ref.shape[0]
    slots = slot_ref.shape[1] // 2
    ids = own_ids(own_count, 2 * own_count)

    def route_rows(b, table):
        total = jnp.zeros((TOP, groups * size), single)
        for e in range(own_count):
            mine = pick[e * slots : (e + 1) * slots].astype(single)
            row = jnp.sum(mine * slot_ref[e, b * slots : (b + 1) * slots], axis=0, keepdims=True)
            total = total + jnp.where(table[0:TOP] == ids[e], row, 0.0)
        return total

    route_own[...] = route_rows(0, table_ref)
    total = wire.scatter_end(other_go, land_a, own_block(mo_ref))
    sums[...] = total.astype(narrow)
    half_go = wire.go(sums, land_h, wire.to_half)
    scatter_on(own_go, ra_ref, land_b, 1)
    send_far(1)
    fetch(oa_ref, None)
    combine_out(ma_ref)
    for k in other_go:
        wire.leave(k)
    fetch(oo_ref, 1)
    combine_out(mo_ref)
    route_send[...] = route_rows(1, otab_ref)
    route_go = wire.go(route_send, land_r, wire.to_half)
    total = wire.scatter_end(own_go, land_b, own_block(ra_ref))
    wire.come(half_go)
    total = total + land_h[...].astype(single)
    back, gain_two = norm_back(total, hid_ref[...], gain_ref[1:2])
    hidden_grad = cot_ref[...].astype(single) + back
    tgrad_ref[...] = hidden_grad
    ag[s] = hidden_grad.astype(narrow)
    grad_go = wire.gather(ag.at[s], ag)
    wire.come(route_go)
    total = route_own[...] + land_r[...]
    for j in range(groups):
        quarters[j] = total[:, j * size : (j + 1) * size]
        logits[j] = table_ref[TOP : 2 * TOP, j * size : (j + 1) * size]
    quarter_go = quarter_sends(quarters, land_q)

    leave_go = []

    def now(k):
        wire.remotes[k].start()

    def finish_term(t, begin):
        wire.come(core_go[t][1], *z_go[t])
        if t >= 2:
            wire.leave(leave_go[t - 2])
        leave_go.append(len(wire.remotes))
        totals(
            wire, begin, terms[t].at[0], c1_ref.at[t], zb_ref.at[t], buffers, leave.at[t % 2],
            own_ref.at[t], hx_ref.at[t],
        )

    finish_term(0, now)
    wire.gather_on(grad_go, ag)
    send_far(2)
    tok_rows = values.at[pl.ds(0, groups * size)]
    load_tok = wire.near(tokall_ref, tok_rows)
    wire.gather_end(grad_go)
    moe_go = scatter(mo_ref, land_a)
    exit_own = wall_ref[:, mix_width : mix_width + q_width]
    for j in range(groups):
        out_grad[j * size : (j + 1) * size] = dot(ag[j], exit_own, 1, 0).astype(narrow)
    attend_back_rows(out_grad, q_ref, k_ref, v_ref, log_ref, pg_ref, keys_sum, values_sum)
    load_tok.wait()
    gain_one = project_back_rows(
        pg_ref, wall_ref[:, :mix_width], tok_rows, cos_ref, sin_ref, stage, q_width + k_width, size
    )
    norm_go = scatter(stage, land_b)
    load_normed = wire.near(normed_ref, tok_rows)
    for k in other_go[4:] + own_go[4:]:
        wire.leave(k)
    scatter_on(moe_go, mo_ref, land_a, 0)
    finish_term(1, now)
    wire.scatter_on(
        norm_go, land_b,
        lambda j: stage[s ^ j, pl.ds(0 if j == 2 else middle, middle)].astype(single),
        passing.at[2],
    )
    total = wire.scatter_end(moe_go, land_a, own_block(mo_ref))
    for j in (1, 2):
        pl.semaphore_signal(free, inc=1, device_id=wire.to_seq[j], device_id_type=MESH)
    wire.leave(half_go)
    sums[...] = total.astype(narrow)
    moe_half_go = wire.go(sums, land_m, wire.to_half)

    pl.semaphore_wait(free, 2)
    moe_own_go = scatter(ma_ref, land_a)

    _, shards, few, width = gw.shape
    f, last = wire.f, mix_width + q_width
    shape = (groups, shards, few)
    load_normed.wait()
    gw[:, :, :, :mix_width] = (
        dot(tok_rows[...], pg_ref[...], 0, 0).astype(narrow).reshape(shape + (mix_width,))
    )
    grads = ag[...].reshape(groups * size, D)
    gw[:, :, :, mix_width:last] = (
        dot(grads, att_ref[...], 0, 0).astype(narrow).reshape(shape + (q_width,))
    )
    gains = jnp.concatenate([gain_one, gain_two, jnp.zeros((width - last - 2, D), single)], axis=0)
    gw[:, :, :, last:] = gains.T.astype(narrow).reshape(shape + (width - last,))
    pair_go = [wire.go(gw.at[:, f ^ (m + 1)], r1.at[m // 2], wire.to_core) for m in (2, 6, 0, 4)]
    scatter_on(moe_own_go, ma_ref, land_a, 1)
    total = wire.scatter_end(norm_go, land_b, stage[s].astype(single))
    back, _ = norm_back(total, tok_ref[...].astype(single), gain_ref[0:1])
    tgrad_ref[...] += back
    wire.come(*pair_go)

    def pair_sum(m):
        return gw[:, f ^ m].astype(single) + r1[m // 2].astype(single)

    gw[:, f ^ 2] = pair_sum(2).astype(narrow)
    go_2 = wire.go(gw.at[:, f ^ 2], r2.at[0], wire.to_z)
    gw[:, f ^ 6] = pair_sum(6).astype(narrow)
    go_6 = wire.go(gw.at[:, f ^ 6], r2.at[1], wire.to_z)
    wire.come(*quarter_go)
    route_grad = quarters[s]
    for j in range(groups - 1):
        route_grad = route_grad + land_q[j]
    top = logits[s]
    exponent = jnp.exp(top - jnp.max(top, axis=0, keepdims=True))
    gating = exponent / jnp.sum(exponent, axis=0, keepdims=True)
    lgrad_ref[...] = gating * (route_grad - jnp.sum(gating * route_grad, axis=0, keepdims=True))
    held = []
    finish_term(2, held.append)
    total = wire.scatter_end(moe_own_go, land_a, hid_ref[...] + own_block(ma_ref))
    wire.come(moe_half_go)
    layer_ref[...] = (total + land_m[...].astype(single)).astype(narrow)
    wire.come(go_6)
    gw[:, f ^ 4] = (pair_sum(4) + r2[1].astype(single)).astype(narrow)
    go_4 = wire.go(gw.at[:, f ^ 4], r3, wire.to_half)
    now(held[0])
    wire.come(go_2, go_4)
    fin[...] = pair_sum(0) + r2[0].astype(single) + r3[...].astype(single)
    attn_in[s] = fin[s]
    last_go = [wire.go(fin.at[s ^ j], attn_in.at[s], wire.to_seq[j]) for j in range(1, groups)]
    wire.come(*last_go)
    wire.near(attn_in, attn_ref).wait()
    wire.finish()


def backward_call(
    backs, outs, pick, terms, hidden, gains, cot, wall, q, k, v, logs, tokens_all,
    cos_table, sin_table, slot_grad, table, other_table, normed, tok, att, few,
):
    size = hidden.shape[0]
    seq_len = tokens_all.shape[0]
    groups = seq_len // size
    rings, halves, own, part, width = terms[0].shape
    slot_rows = pick.shape[1]
    shape = jax.ShapeDtypeStruct
    vmem = pl.BlockSpec(memory_space=pltpu.VMEM)
    hbm = pl.BlockSpec(memory_space=pl.ANY)
    block = (groups, size, D)
    slab = (groups, few, wall.shape[1])
    mix_width = q.shape[1] + 2 * k.shape[1]
    landing = pltpu.VMEM((6, size // 2, D), narrow)
    route = pltpu.VMEM((TOP, seq_len), single)
    count = 96
    return pl.pallas_call(
        backward_body,
        in_specs=[hbm] * 10 + [vmem] * 15,
        out_specs=[vmem] * 3 + [hbm] * 9,
        out_shape=[
            shape((size, D), single),
            shape((size, D), narrow),
            shape((TOP, size), single),
            shape(slab, single),
            shape(block, narrow),
            shape(block, narrow),
            shape(block, narrow),
            shape((3, halves, own, part, width), narrow),
            shape((3, halves, own, part, width), narrow),
            shape((3, halves, own, part, width), narrow),
            shape((3, own, part, width), narrow),
            shape((3, own, part, width), narrow),
        ],
        scratch_shapes=[
            pltpu.VMEM((seq_len, mix_width), narrow),
            pltpu.SemaphoreType.REGULAR,
            pltpu.VMEM((groups, 8) + slab[1:], narrow),
            pltpu.VMEM((4,) + slab, narrow),
            pltpu.VMEM((2,) + slab, narrow),
            pltpu.VMEM(slab, narrow),
            pltpu.VMEM(slab, single),
            pltpu.VMEM(slab, single),
            pltpu.VMEM(block, narrow),
            pltpu.VMEM(q.shape, narrow),
            pltpu.VMEM((seq_len, HEAD_DIM), single),
            pltpu.VMEM((seq_len, HEAD_DIM), single),
            landing,
            landing,
            pltpu.VMEM((size, D), narrow),
            pltpu.VMEM((size, D), narrow),
            pltpu.VMEM((size, D), narrow),
            pltpu.VMEM((size, D), narrow),
            pltpu.VMEM((3, own, part, width), narrow),
            pltpu.VMEM((2, halves, own, part, width), narrow),
            pltpu.VMEM((2, own, part, width), narrow),
            pltpu.VMEM((2, size // 2, D), narrow),
            pltpu.VMEM((3, 2, size // 2, D), narrow),
            pltpu.VMEM((slot_rows, D), narrow),
            pltpu.VMEM((slot_rows, seq_len), narrow),
            pltpu.VMEM(block, narrow),
            route,
            route,
            route,
            pltpu.VMEM((groups, TOP, size), single),
            pltpu.VMEM((groups - 1, TOP, size), single),
            pltpu.VMEM((groups, TOP, size), single),
            pltpu.SemaphoreType.DMA((count,)),
            pltpu.SemaphoreType.DMA((count,)),
            pltpu.SemaphoreType.DMA((count,)),
        ],
        compiler_params=pltpu.CompilerParams(
            collective_id=1, has_side_effects=True, vmem_limit_bytes=67_000_000
        ),
        cost_estimate=pl.CostEstimate(
            flops=150_000_000_000, bytes_accessed=100_000_000, transcendentals=0
        ),
        name="backward_exchange",
    )(
        *backs, *outs, pick, tokens_all, normed, *terms, tok, att, hidden, gains, cot, wall,
        q, k, v, logs, cos_table, sin_table, slot_grad, table, other_table,
    )


def attention_back_call(grads, exit_own, mixing_own, q, k, v, logs, tokens_all, cos_table, sin_table):
    seq_len = tokens_all.shape[0]
    shape = jax.ShapeDtypeStruct
    return pl.pallas_call(
        attention_back_body,
        out_shape=[
            shape((seq_len, mixing_own.shape[1]), narrow),
            shape((seq_len, D), narrow),
            shape((1, D), single),
        ],
        scratch_shapes=[
            pltpu.VMEM(q.shape, narrow),
            pltpu.VMEM((seq_len, HEAD_DIM), single),
            pltpu.VMEM((seq_len, HEAD_DIM), single),
        ],
        cost_estimate=pl.CostEstimate(
            flops=2 * seq_len * D * (mixing_own.shape[1] + q.shape[1])
            + 10 * seq_len**2 * q.shape[1] * 4,
            bytes_accessed=seq_len * D * 8, transcendentals=0,
        ),
        name="attention_backward",
    )(grads, exit_own, mixing_own, q, k, v, logs, tokens_all, cos_table, sin_table)


def project_rows(at, size, tok_rows, mix, gain_row, cos_ref, sin_ref, normed_ref, q_ref, k_ref, v_ref):
    rows = slice(at, at + size)
    q_width, k_width = q_ref.shape[1], k_ref.shape[1]
    values = tok_rows.astype(single)
    inverse = lax.rsqrt(jnp.mean(values * values, axis=-1, keepdims=True) + epsilon)
    normed = (values * inverse * gain_row).astype(narrow)
    normed_ref[rows] = normed
    projected = dot(normed, mix, 1, 0)
    width = q_width + k_width
    turned = rope(
        projected[:, :width], wide(cos_ref[rows], width), wide(sin_ref[rows], width)
    ).astype(narrow)
    q_ref[rows] = turned[:, :q_width]
    k_ref[rows] = turned[:, q_width:]
    v_ref[rows] = projected[:, width:].astype(narrow)


def attend_rows(q_ref, k_ref, v_ref, att_ref, log_ref):
    seq_len, k_width = k_ref.shape
    size = QROWS
    group_size = HEADS // KV_HEADS
    for kv in range(k_width // HEAD_DIM):
        lanes = slice(kv * HEAD_DIM, (kv + 1) * HEAD_DIM)
        for block in range(seq_len // size):
            at = block * size
            end = at + size
            queries = stacked(q_ref, at, kv, size)
            scores = key_scores(k_ref[:end, lanes], queries, at, size)
            top = jnp.max(scores, axis=0, keepdims=True)
            exponent = jnp.exp(scores - top)
            total = jnp.sum(exponent, axis=0, keepdims=True)
            soft = (exponent * (1.0 / total)).astype(narrow)
            log_ref[kv * (seq_len // size) + block] = top + jnp.log(total)
            out = dot(v_ref[:end, lanes], soft, 0, 0)
            for g in range(group_size):
                head = kv * group_size + g
                att_ref[at:end, head * HEAD_DIM : (head + 1) * HEAD_DIM] = (
                    out[:, g * size : (g + 1) * size].T.astype(narrow)
                )


class Wire:
    def __init__(self, send, recv, local):
        self.send, self.recv, self.local = send, recv, local
        self.remotes, self.landed, self.left, self.locals = [], [], [], 0
        s, h, r = lax.axis_index("seq"), lax.axis_index("half"), lax.axis_index("ring")
        groups = lax.axis_size("seq")
        self.s, self.h, self.r, self.f, self.groups = s, h, r, h * 4 + r, groups
        self.to_half, self.to_z, self.to_core = {"half": h ^ 1}, {"ring": r ^ 2}, {"ring": r ^ 1}
        self.to_seq = [{"seq": s ^ j} for j in range(groups)]

    def meet(self):
        barrier = pltpu.get_barrier_semaphore()
        peers = self.to_seq[1:] + [self.to_half, self.to_z, self.to_core]
        for peer in peers:
            pl.semaphore_signal(barrier, inc=1, device_id=peer, device_id_type=MESH)
        pl.semaphore_wait(barrier, len(peers))

    def go(self, source, target, peer):
        k = self.plan(source, target, peer)
        self.remotes[k].start()
        return k

    def plan(self, source, target, peer):
        k = len(self.remotes)
        self.remotes.append(
            pltpu.make_async_remote_copy(
                src_ref=source, dst_ref=target, send_sem=self.send.at[k],
                recv_sem=self.recv.at[k], device_id=peer, device_id_type=MESH,
            )
        )
        self.landed.append(False)
        self.left.append(False)
        return k

    def by_core(self, *sends):
        keys = [self.plan(*send) for send in sends]

        @pl.when(self.r % 2 == 0)
        def _():
            for k in keys:
                self.remotes[k].start()

        @pl.when(self.r % 2 == 1)
        def _():
            for k in reversed(keys):
                self.remotes[k].start()

        return keys

    def come(self, *which):
        for k in which:
            self.remotes[k].wait_recv()
            self.landed[k] = True

    def leave(self, k):
        if not self.left[k]:
            self.remotes[k].wait_send()
        self.left[k] = True

    def near(self, source, target):
        copy = pltpu.make_async_copy(source, target, self.local.at[self.locals])
        self.locals += 1
        copy.start()
        return copy

    def gather(self, source, target):
        s = self.s
        return [self.go(source, target.at[s], self.to_seq[j]) for j in (1, 2)]

    def gather_on(self, keys, target):
        s, middle = self.s, target.shape[1] // 2
        first, second = pl.ds(0, middle), pl.ds(middle, middle)
        self.come(keys[0])
        block = target.at[s ^ 1, first]
        keys.append(self.go(block, block, self.to_seq[2]))
        self.come(keys[1])
        block = target.at[s ^ 2, second]
        keys.append(self.go(block, block, self.to_seq[1]))

    def gather_end(self, keys):
        self.come(*keys[2:])

    def scatter(self, source, landing):
        middle = landing.shape[1]
        first, second = pl.ds(0, middle), pl.ds(middle, middle)
        return [
            self.go(source(3).at[first], landing.at[1], self.to_seq[1]),
            self.go(source(3).at[second], landing.at[3], self.to_seq[2]),
            self.go(source(1).at[first], landing.at[0], self.to_seq[1]),
            self.go(source(2).at[second], landing.at[2], self.to_seq[2]),
        ]

    def scatter_on(self, keys, landing, kept, passing):
        self.come(keys[0])
        passing[0] = (kept(2) + landing[1].astype(single)).astype(narrow)
        keys.append(self.go(passing.at[0], landing.at[4], self.to_seq[2]))
        self.come(keys[1])
        passing[1] = (kept(1) + landing[3].astype(single)).astype(narrow)
        keys.append(self.go(passing.at[1], landing.at[5], self.to_seq[1]))

    def scatter_end(self, keys, landing, own):
        self.come(*keys[2:])
        first = landing[0].astype(single) + landing[4].astype(single)
        second = landing[2].astype(single) + landing[5].astype(single)
        return own + jnp.concatenate([first, second], axis=0)

    def finish(self):
        for k, copy in enumerate(self.remotes):
            if not self.left[k]:
                copy.wait_send()
            if not self.landed[k]:
                copy.wait_recv()


def place_rows(table, ids, capacity, slots, pick_ref, share_ref, b):
    length = table.shape[1]
    picked, logits, order = table[0:TOP], table[TOP : 2 * TOP], table[2 * TOP : 2 * TOP + 1]
    exponent = jnp.exp(logits - jnp.max(logits, axis=0, keepdims=True))
    gating = exponent / jnp.sum(exponent, axis=0, keepdims=True)
    down = lax.broadcasted_iota(jnp.int32, (length, length), 0).astype(single)
    along = lax.broadcasted_iota(jnp.int32, (length, length), 1).astype(single)
    place_col = jnp.sum(jnp.where(order == down, along, 0.0), axis=1, keepdims=True)
    place_row = jnp.broadcast_to(place_col, (length, 128)).T[0:1]
    earlier = (place_col < place_row).astype(single).astype(narrow)
    hits = [jnp.sum((picked == i).astype(single), axis=0, keepdims=True) for i in ids]
    share = [
        jnp.sum(jnp.where(picked == i, gating, 0.0), axis=0, keepdims=True) for i in ids
    ]
    spare = jnp.zeros((8 - len(ids), length), single)
    rank = dot(jnp.concatenate(hits + [spare], axis=0).astype(narrow), earlier, 1, 0)
    slot_at = lax.broadcasted_iota(jnp.int32, (slots, length), 0).astype(single)
    for e in range(len(ids)):
        kept = (hits[e] > 0.0) & (rank[e : e + 1] < capacity)
        filled = jnp.where(kept, rank[e : e + 1], -1.0) == slot_at
        pick_ref[b, e * slots : (e + 1) * slots] = filled.astype(single).astype(narrow)
        share_ref[e, b * slots : (b + 1) * slots] = jnp.sum(
            jnp.where(filled, share[e], 0.0), axis=1, keepdims=True
        )


def own_ids(own, local_count):
    first = lax.axis_index("seq") * local_count + lax.axis_index("half") * own
    return [(first + e).astype(single) for e in range(own)]


def forward_body(
    tok_ref, pack_ref, cot_ref, wg_ref, wu_ref, wd_ref, cos_ref, sin_ref, table_ref,
    normed_ref, q_ref, k_ref, v_ref, att_ref, log_ref, hid_ref, gain_ref, share_ref, otab_ref,
    tokall_ref, wall_ref, pickall_ref, xa_ref, xo_ref, ya_ref, yo_ref, wout_ref,
    xown_ref, xother_ref, yown_ref, yother_ref,
    tokv, wv, part, landed, passing, xv, other_table, pick, picked_rows, send, recv, local,
):
    wire = Wire(send, recv, local)
    s, h, r, f, groups = wire.s, wire.h, wire.r, wire.f, wire.groups
    _, fsdp, few, width = wv.shape
    q_width, k_width = q_ref.shape[1], k_ref.shape[1]
    mix_width = q_width + 2 * k_width
    size = tok_ref.shape[0]
    middle = size // 2
    wire.meet()

    pack_go = [wire.go(pack_ref.at[s ^ j], wv.at[s, f], wire.to_seq[j]) for j in range(1, groups)]
    tok_go = wire.gather(tok_ref, tokv)
    table_go = wire.go(table_ref, other_table, wire.to_half)
    own_cot = wire.near(cot_ref, ya_ref.at[s])
    wv[s, f] = pack_ref[s]
    tokv[s] = tok_ref[...]

    sources = (wg_ref, wu_ref, wd_ref)

    def weights_first(t):
        own, other = sources[t].at[h], sources[t].at[1 - h]
        target = wout_ref.at[t, h, r]
        keys = wire.by_core((other, target, wire.to_half), (own, target, wire.to_z))
        wire.go(own, target, wire.to_core)
        return keys

    def weights_next(t, keys):
        wire.come(keys[0])
        came = wout_ref.at[t, 1 - h, r]
        on_z = wire.go(came, came, wire.to_z)
        wire.go(came, came, wire.to_core)
        wire.come(keys[1])
        beside = wout_ref.at[t, h, r ^ 2]
        wire.go(beside, beside, wire.to_core)
        return on_z

    def weights_last(t, key):
        wire.come(key)
        beyond = wout_ref.at[t, 1 - h, r ^ 2]
        wire.go(beyond, beyond, wire.to_core)

    wire.come(*pack_go)
    mine = wv.at[:, f]
    a_half = wire.go(mine, mine, wire.to_half)
    a_z = wire.go(mine, mine, wire.to_z)
    parts_go = [wire.go(mine, mine, wire.to_core)]
    wire.come(a_half)
    block = wv.at[:, f ^ 4]
    b_z = wire.go(block, block, wire.to_z)
    parts_go.append(wire.go(block, block, wire.to_core))
    wire.come(a_z)
    block = wv.at[:, f ^ 2]
    parts_go.append(wire.go(block, block, wire.to_core))
    cot_half = wire.go(cot_ref, yo_ref.at[s], wire.to_half)
    gate_first = weights_first(0)
    wire.gather_on(tok_go, tokv)
    cot_go = wire.gather(cot_ref, ya_ref)
    wire.come(b_z)
    block = wv.at[:, f ^ 6]
    parts_go.append(wire.go(block, block, wire.to_core))
    up_first = weights_first(1)

    own, slots = wout_ref.shape[3], share_ref.shape[1] // 2
    capacity = (groups * size * TOP + EXPERTS - 1) // EXPERTS
    ids = own_ids(own, 2 * own)
    place_rows(table_ref[...], ids, capacity, slots, pick, share_ref, 0)
    wire.gather_end(tok_go)
    wire.come(*parts_go)
    wire.gather_on(cot_go, ya_ref)
    keep_tok = wire.near(tokv, tokall_ref)
    keep_wall = wire.near(wv, wall_ref)
    depth = groups * fsdp * few
    gains = wv[:, :, :, mix_width + q_width :].reshape(depth, width - mix_width - q_width)
    gains = gains.astype(single).T[0:8]
    gain_ref[...] = gains
    for j in range(groups):
        project_rows(
            j * size, size, tokv[j], wv[:, :, :, :mix_width].reshape(depth, mix_width),
            gains[0:1], cos_ref, sin_ref, normed_ref, q_ref, k_ref, v_ref,
        )
    attend_rows(q_ref, k_ref, v_ref, att_ref, log_ref)
    exit_own = wv[:, :, :, mix_width : mix_width + q_width].reshape(depth, q_width)
    for j in (3, 1, 2, 0):
        rows = pl.ds(pl.multiple_of((s ^ j) * size, size), size)
        partial = dot(att_ref[rows], exit_own, 1, 1)
        if j:
            part[j - 1] = partial.astype(narrow)
        else:
            part_go = wire.scatter(lambda j: part.at[j - 1], landed)
            hid_ref[...] = tok_ref[...].astype(single) + partial

    def dispatch(b, source, target):
        wire.near(source, tokv).wait()
        whole = tokv[...].reshape(groups * size, D)
        for at in range(0, D, 512):
            picked_rows[:, at : at + 512] = dot(pick[b], whole[:, at : at + 512], 1, 0).astype(narrow)
        wire.near(picked_rows, target).wait()

    def kept(j):
        return part[j - 1, (0 if j == 2 else middle) : (middle if j == 2 else size)].astype(single)

    for k in tok_go[2:]:
        wire.leave(k)
    gate_next = weights_next(0, gate_first)
    wire.scatter_on(part_go, landed, kept, passing)
    keep_tok.wait()
    own_cot.wait()
    wire.gather_end(cot_go)
    dispatch(0, ya_ref, yown_ref)
    hidden = wire.scatter_end(part_go, landed, hid_ref[...])
    hid_ref[...] = hidden
    inverse = lax.rsqrt(jnp.mean(hidden * hidden, axis=-1, keepdims=True) + epsilon)
    xv[...] = (hidden * inverse * gains[1:2]).astype(narrow)
    row_half = wire.go(xv, xo_ref.at[s], wire.to_half)
    row_go = wire.gather(xv, xa_ref)
    own_row = wire.near(xv, xa_ref.at[s])
    down_first = weights_first(2)
    wire.come(table_go)
    otab_ref[...] = other_table[...]
    place_rows(other_table[...], ids, capacity, slots, pick, share_ref, 1)
    keep_pick = wire.near(pick, pickall_ref)
    wire.gather_on(row_go, xa_ref)
    wire.come(cot_half)
    up_next = weights_next(1, up_first)
    wire.come(row_half)
    other_go = wire.gather(xo_ref.at[s], xo_ref)
    cot_other = wire.gather(yo_ref.at[s], yo_ref)
    weights_last(0, gate_next)
    own_row.wait()
    wire.gather_end(row_go)
    dispatch(0, xa_ref, xown_ref)
    wire.gather_on(other_go, xo_ref)
    wire.gather_on(cot_other, yo_ref)
    down_next = weights_next(2, down_first)
    weights_last(1, up_next)
    wire.gather_end(other_go)
    dispatch(1, xo_ref, xother_ref)
    wire.gather_end(cot_other)
    dispatch(1, yo_ref, yother_ref)
    weights_last(2, down_next)
    keep_wall.wait()
    keep_pick.wait()
    wire.finish()


def forward_call(tokens, packed, cotangent, weights, cos_table, sin_table, table, q_width, k_width, slots):
    groups, few, width = packed.shape
    _, own, part, hidden_units = weights[0].shape
    size = tokens.shape[0]
    seq_len = size * groups
    blocks = k_width // HEAD_DIM * (seq_len // QROWS)
    shape = jax.ShapeDtypeStruct
    vmem = pl.BlockSpec(memory_space=pltpu.VMEM)
    hbm = pl.BlockSpec(memory_space=pl.ANY)
    rows = shape((groups, size, D), narrow)
    count = 80
    picked = shape((own * slots, D), narrow)
    return pl.pallas_call(
        forward_body,
        in_specs=[vmem] * 3 + [hbm] * 3 + [vmem] * 3,
        out_specs=[vmem] * 10 + [hbm] * 12,
        out_shape=[
            shape((seq_len, D), narrow),
            shape((seq_len, q_width), narrow),
            shape((seq_len, k_width), narrow),
            shape((seq_len, k_width), narrow),
            shape((seq_len, q_width), narrow),
            shape((blocks, 1, HEADS // KV_HEADS * QROWS), single),
            shape((size, D), single),
            shape((8, D), single),
            shape((own, 2 * slots, 1), single),
            shape(table.shape, single),
            rows,
            shape((groups, 8, few, width), narrow),
            shape((2, own * slots, seq_len), narrow),
            rows, rows, rows, rows,
            shape((3, 2, 4, own, part, hidden_units), narrow),
            picked, picked, picked, picked,
        ],
        scratch_shapes=[
            pltpu.VMEM((groups, size, D), narrow),
            pltpu.VMEM((groups, 8, few, width), narrow),
            pltpu.VMEM((groups - 1, size, D), narrow),
            pltpu.VMEM((6, size // 2, D), narrow),
            pltpu.VMEM((2, size // 2, D), narrow),
            pltpu.VMEM((size, D), narrow),
            pltpu.VMEM(table.shape, single),
            pltpu.VMEM((2, own * slots, seq_len), narrow),
            pltpu.VMEM((own * slots, D), narrow),
            pltpu.SemaphoreType.DMA((count,)),
            pltpu.SemaphoreType.DMA((count,)),
            pltpu.SemaphoreType.DMA((24,)),
        ],
        compiler_params=pltpu.CompilerParams(collective_id=0, has_side_effects=True),
        cost_estimate=pl.CostEstimate(
            flops=200_000_000_000, bytes_accessed=100_000_000, transcendentals=0
        ),
        name="forward_exchange",
    )(tokens, packed, cotangent, *weights, cos_table, sin_table, table)


def expert_body(
    batch, own_apart, where_ref, all_ref, g_ref, u_ref, d_ref, *refs,
):
    _, halves, rings, _, part, width = all_ref.shape
    pieces = halves * rings
    x_refs, y_refs, w_ref = refs[:batch], refs[batch : 2 * batch], refs[2 * batch]
    refs = refs[2 * batch + 1 :]
    out_refs, row_refs, slot_ref = refs[:batch], refs[batch : 2 * batch], refs[2 * batch]
    gg_ref, gu_ref, gd_ref, held, sems = refs[2 * batch + 1 :]
    half, ring = where_ref[0], where_ref[1]
    e = pl.program_id(0)
    slot = lax.rem(e, 2)

    def each(expert, slot, act):
        for t, own_ref in enumerate((g_ref, u_ref, d_ref)):
            for g in range(halves):
                for r in range(rings):
                    at = g * rings + r
                    target, sem = held.at[slot, t, at], sems.at[slot, t, at]
                    if not own_apart:
                        act(pltpu.make_async_copy(all_ref.at[t, g, r, expert], target, sem))
                        continue
                    own = (half == g) & (ring == r)

                    @pl.when(own)
                    def _():
                        act(pltpu.make_async_copy(own_ref.at[g, expert], target, sem))

                    @pl.when(jnp.logical_not(own))
                    def _():
                        act(pltpu.make_async_copy(all_ref.at[t, g, r, expert], target, sem))

    @pl.when(e == 0)
    def _():
        each(e, slot, lambda copy: copy.start())

    @pl.when(e + 1 < pl.num_programs(0))
    def _():
        each(e + 1, 1 - slot, lambda copy: copy.start())

    for t in range(3):
        for at in range(pieces):
            pltpu.make_async_copy(
                all_ref.at[t, at // rings, at % rings, e], held.at[slot, t, at], sems.at[slot, t, at]
            ).wait()

    def weight(t):
        return held[slot, t].reshape(pieces * part, width)

    def write(ref, value):
        for g in range(halves):
            for r in range(rings):
                at = (g * rings + r) * part
                ref[r ^ ring if own_apart else r, g ^ half, 0] = value[at : at + part].astype(ref.dtype)

    slots = x_refs[0].shape[1]

    def split(outs, value):
        for b, ref in enumerate(outs):
            ref[0] = value[b * slots : (b + 1) * slots].astype(ref.dtype)

    rows = jnp.concatenate([ref[0] for ref in x_refs], axis=0)
    cots = jnp.concatenate([ref[0] for ref in y_refs], axis=0)
    share = w_ref[0]
    gate, up, down = weight(0), weight(1), weight(2)
    gate_pre = dot(rows, gate, 1, 0)
    up_pre = dot(rows, up, 1, 0)
    sig = jax.nn.sigmoid(gate_pre)
    mid = (gate_pre * sig * up_pre).astype(narrow)
    expert_out = dot(mid, down, 1, 1)
    cot_float = cots.astype(single)
    slot_ref[0] = jnp.sum(cot_float * expert_out, axis=-1, keepdims=True)
    split(out_refs, expert_out * share)
    out_low = (cot_float * share).astype(narrow)
    mid_grad = dot(out_low, down, 1, 0)
    write(gd_ref, dot(out_low, mid, 0, 0))
    gate_grad = (mid_grad * up_pre * sig * (1.0 + gate_pre * (1.0 - sig))).astype(narrow)
    up_grad = (mid_grad * gate_pre * sig).astype(narrow)
    split(row_refs, dot(gate_grad, gate, 1, 1) + dot(up_grad, up, 1, 1))
    both = dot(rows, jnp.concatenate([gate_grad, up_grad], axis=1), 0, 0)
    write(gg_ref, both[:, :width])
    write(gu_ref, both[:, width:])


def expert_call(where, gathered, weights, own_apart, rows, cots, share):
    _, halves, rings, own, part, width = gathered.shape
    batch = len(rows)
    _, slots, depth = rows[0].shape
    pieces = halves * rings
    weight_spec = pl.BlockSpec((rings, halves, 1, part, width), lambda e, h: (0, 0, e, 0, 0))
    row_spec = pl.BlockSpec((1, slots, depth), lambda e, h: (e, 0, 0))
    share_spec = pl.BlockSpec((1, batch * slots, 1), lambda e, h: (e, 0, 0))
    shape = jax.ShapeDtypeStruct
    row_shape = shape((own, slots, depth), narrow)
    outs = pl.pallas_call(
        functools.partial(expert_body, batch, own_apart),
        grid_spec=pltpu.PrefetchScalarGridSpec(
            num_scalar_prefetch=1,
            grid=(own,),
            in_specs=[pl.BlockSpec(memory_space=pl.ANY)] * 4
            + [row_spec] * (2 * batch)
            + [share_spec],
            out_specs=[row_spec] * (2 * batch) + [share_spec] + [weight_spec] * 3,
            scratch_shapes=[
                pltpu.VMEM((2, 3, pieces, part, width), narrow),
                pltpu.SemaphoreType.DMA((2, 3, pieces)),
            ],
        ),
        out_shape=[row_shape] * (2 * batch)
        + [shape((own, batch * slots, 1), single)]
        + [shape((rings, halves, own, part, width), narrow)] * 3,
        cost_estimate=pl.CostEstimate(
            flops=9 * 2 * own * batch * slots * depth * width,
            bytes_accessed=12 * own * depth * width + 8 * batch * own * slots * depth,
            transcendentals=0,
        ),
        name="expert_ffn",
    )(where, gathered, *weights, *rows, *cots, share)
    return outs[:batch], outs[batch : 2 * batch], outs[2 * batch], outs[2 * batch + 1 :]


def local(
    halves, rings,
    tokens, mixing_weight, output_weight, norm_gains, expert_gate, expert_up, expert_down,
    gate_logits, routes, fill_order, cotangent,
):
    groups = lax.axis_size("seq")
    column = lax.axis_index("seq")
    half = lax.axis_index("half")
    ring = lax.axis_index("ring")
    paired = halves == 2
    tok_rows = tokens.shape[1]
    seq_len = tok_rows * groups
    capacity = (seq_len * TOP + EXPERTS - 1) // EXPERTS
    local_count = expert_gate.shape[1]
    own_count = local_count // halves
    part = expert_gate.shape[0]
    fsdp_rows = mixing_weight.shape[0]
    q_width = HEADS * HEAD_DIM // groups
    k_width = KV_HEADS * HEAD_DIM // groups
    mix_width = q_width + 2 * k_width
    own_kv = KV_HEADS // groups
    own_heads = HEADS // groups
    group_size = HEADS // KV_HEADS
    score_scale = 1.0 / math.sqrt(HEAD_DIM)
    query_all = HEADS * HEAD_DIM
    key_all = KV_HEADS * HEAD_DIM

    def gather_seq(value):
        parts = [value] + [swap(value, "seq", j, groups) for j in range(1, groups)]
        whole = jnp.zeros((groups,) + value.shape, value.dtype)
        for j, item in enumerate(parts):
            whole = lax.dynamic_update_index_in_dim(whole, item, column ^ j, 0)
        return whole.reshape((seq_len,) + value.shape[1:])

    def scatter_seq(value):
        blocks = value.reshape((groups, tok_rows) + value.shape[1:])
        total = lax.dynamic_index_in_dim(blocks, column, 0, False).astype(single)
        for j in range(1, groups):
            sent = lax.dynamic_index_in_dim(blocks, column ^ j, 0, False).astype(narrow)
            total = total + swap(sent, "seq", j, groups).astype(single)
        return total

    def exchange_seq(blocks):
        whole = lax.dynamic_update_index_in_dim(
            jnp.zeros_like(blocks), lax.dynamic_index_in_dim(blocks, column, 0, False), column, 0
        )
        for j in range(1, groups):
            sent = lax.dynamic_index_in_dim(blocks, column ^ j, 0, False)
            whole = lax.dynamic_update_index_in_dim(
                whole, swap(sent, "seq", j, groups), column ^ j, 0
            )
        return whole

    packed = jnp.concatenate(
        [
            mixing_weight[:, :query_all].reshape(fsdp_rows, groups, q_width),
            mixing_weight[:, query_all : query_all + key_all].reshape(fsdp_rows, groups, k_width),
            mixing_weight[:, query_all + key_all :].reshape(fsdp_rows, groups, k_width),
            output_weight.reshape(fsdp_rows, groups, q_width),
            jnp.broadcast_to(
                jnp.pad(norm_gains, ((0, 0), (0, PAD - 2)))[:, None], (fsdp_rows, groups, PAD)
            ),
        ],
        2,
    ).transpose(1, 0, 2)
    cos_table, sin_table = rotary_tables(jnp.arange(seq_len, dtype=jnp.int32))
    cos_table, sin_table = jnp.tile(cos_table, (1, 2)), jnp.tile(sin_table, (1, 2))
    own_weights = [
        item.transpose(1, 0, 2).reshape(halves, own_count, part, FF)
        for item in (expert_gate, expert_up, expert_down)
    ]
    inputs = tokens[0].astype(single)
    slots = (capacity + 15) // 16 * 16
    if paired:
        table = jnp.concatenate(
            [
                routes[0].astype(single).T,
                gate_logits[0].T,
                jnp.broadcast_to(fill_order[0].astype(single), (8, seq_len)),
            ],
            0,
        )
        (
            normed_low, queries, keys, values, attended, logs, hidden, gains_float, share,
            other_table, tokens_all, packed, pick, _, _, _, _, gathered,
            own_x, other_x, own_y, other_y,
        ) = forward_call(
            tokens[0], packed, cotangent[0], own_weights, cos_table, sin_table, table,
            q_width, k_width, slots,
        )
        tokens_all = tokens_all.reshape(seq_len, D)
        packed = packed.reshape(D, -1)
        mixing_own = packed[:, :mix_width]
        exit_own = packed[:, mix_width : mix_width + q_width]
        seq_rows = [item.reshape(own_count, slots, D) for item in (own_x, other_x)]
        cot_rows = [item.reshape(own_count, slots, D) for item in (own_y, other_y)]
    else:
        packed = exchange_seq(packed)
        packed = lax.all_gather(packed, ("half", "ring"), axis=0, tiled=False)
        packed = packed.transpose(1, 0, 2, 3).reshape(D, -1)
        mixing_own = packed[:, :mix_width]
        exit_own = packed[:, mix_width : mix_width + q_width]
        gains_float = packed[:, mix_width + q_width : mix_width + q_width + 2].astype(single).T
        tokens_all = gather_seq(tokens[0])
        gathered = jnp.stack(
            [lax.all_gather(item[0], "ring", axis=0, tiled=False)[None] for item in own_weights]
        )
        normed_low, queries, keys, values, attended, logs, attn_part = attention_call(
            tokens_all, mixing_own, exit_own, gains_float, cos_table, sin_table
        )
        hidden = inputs + scatter_seq(attn_part)
        scale_two = lax.rsqrt(jnp.mean(hidden * hidden, axis=-1, keepdims=True) + epsilon)
        seq_rows = [gather_seq((hidden * scale_two * gains_float[1]).astype(narrow))]
        cot_rows = [gather_seq(cotangent[0])]

    if not paired:
        pair_routes = routes
        pair_order = fill_order
        pair_gating = softmax_last(gate_logits)
        expert_ids = column * local_count + half * own_count + jnp.arange(own_count, dtype=jnp.int32)
        places = jnp.arange(seq_len, dtype=jnp.int32)
        chosen = (pair_routes[..., None] == expert_ids).astype(single)
        hits = jnp.sum(chosen, axis=2)
        token_weight = jnp.sum(pair_gating[..., None] * chosen, axis=2)
        place_of = jnp.sum(
            jnp.where(pair_order[:, :, None] == places, places[None, :, None], 0), axis=1
        )
        earlier = (place_of[:, None, :] < place_of[:, :, None]).astype(narrow)
        rank = jnp.einsum(
            "btu,bue->bte", earlier, hits.astype(narrow), preferred_element_type=single
        ).astype(jnp.int32)
        kept = (hits > 0) & (rank < capacity)
        flat_place = jnp.where(kept, rank + jnp.arange(own_count, dtype=jnp.int32) * slots, -1)
        flat_ids = jnp.arange(own_count * slots, dtype=jnp.int32)
        filled = flat_place[:, :, 0:1] == flat_ids
        for e in range(1, own_count):
            filled = filled | (flat_place[:, :, e : e + 1] == flat_ids)
        select = filled.astype(narrow)
        batch = select.shape[0]
        match = flat_place[:, :, :, None] == (
            jnp.arange(own_count, dtype=jnp.int32)[:, None] * slots
            + jnp.arange(slots, dtype=jnp.int32)[None, :]
        )
        slot_weight = jnp.sum(jnp.where(match, token_weight[..., None], 0.0), axis=1)
        share = slot_weight.transpose(1, 0, 2).reshape(own_count, batch * slots, 1)

        def dispatch(rows):
            return [
                lax.dot_general(
                    select[b], item, (((0,), (0,)), ((), ())), preferred_element_type=narrow
                ).reshape(own_count, slots, D)
                for b, item in enumerate(rows)
            ]

        def combine(b, values):
            return lax.dot_general(
                select[b],
                values.reshape(own_count * slots, D),
                (((1,), (0,)), ((), ())),
                preferred_element_type=narrow,
            )

        seq_rows, cot_rows = dispatch(seq_rows), dispatch(cot_rows)

    slot_out, slot_back, slot_grad, (gate_term, up_term, down_term) = expert_call(
        jnp.stack([half, ring]), gathered, own_weights, paired,
        seq_rows, cot_rows, share,
    )
    def by_row(total):
        return total.reshape(local_count, part, FF).transpose(1, 0, 2).astype(single)

    if paired:
        flat = (own_count * slots, D)
        (
            tokens_gradient, layer_output, logits_rows, attn_total,
            _, _, _, _, _, _, own_terms, other_terms,
        ) = backward_call(
            [item.reshape(flat) for item in slot_back], [item.reshape(flat) for item in slot_out],
            pick, (gate_term, up_term, down_term), hidden, gains_float, cotangent[0], packed,
            queries, keys, values, logs, tokens_all, cos_table, sin_table, slot_grad, table,
            other_table, normed_low, tokens[0], attended, fsdp_rows,
        )
        logits_rows = logits_rows.T
        tokens_gradient, layer_output = tokens_gradient[None], layer_output[None]

        def expert_gradient(own, other):
            return by_row(
                jnp.stack([jnp.where(half == 0, own, other), jnp.where(half == 0, other, own)])
            )

        gate_gradient = expert_gradient(own_terms[0], other_terms[0])
        up_gradient = expert_gradient(own_terms[1], other_terms[1])
        down_gradient = expert_gradient(own_terms[2], other_terms[2])
    else:
        slot_grad = slot_grad.reshape(own_count, batch, slots).transpose(1, 0, 2)
        weight_grad_tok = jnp.sum(jnp.where(match, slot_grad[:, None], 0.0), axis=3)
        route_part = jnp.sum(weight_grad_tok[:, :, None, :] * chosen, axis=-1)

        def send_routes(value):
            blocks = value.reshape(groups, tok_rows, TOP)
            total = lax.dynamic_index_in_dim(blocks, column, 0, False)
            for j in range(1, groups):
                sent = lax.dynamic_index_in_dim(blocks, column ^ j, 0, False)
                total = total + swap(sent, "seq", j, groups)
            return total

        route_grad = send_routes(route_part[0])
        gating = softmax_last(
            lax.dynamic_slice_in_dim(gate_logits[0], column * tok_rows, tok_rows, 0)
        )
        logits_rows = gating * (route_grad - jnp.sum(gating * route_grad, axis=-1, keepdims=True))

        def ring_sum(term):
            return lax.psum_scatter(term, "ring", scatter_dimension=0, tiled=False)

        normed_two_grad = scatter_seq(combine(0, slot_back[0]))
        gate_gradient, up_gradient, down_gradient = [
            by_row(ring_sum(term)) for term in (gate_term, up_term, down_term)
        ]
        moe_rows = scatter_seq(combine(0, slot_out[0]))
        layer_output = (hidden + moe_rows).astype(narrow)[None]
        back, gain_two_grad = norm_back(normed_two_grad, hidden, gains_float[1])
        hidden_grad = cotangent[0].astype(single) + back
        attn_grad_all = gather_seq(hidden_grad.astype(narrow))
        projected_grad, normed_part, gain_one_grad = attention_back_call(
            attn_grad_all, exit_own, mixing_own, queries, keys, values, logs, tokens_all,
            cos_table, sin_table,
        )
        mixing_term = dot(normed_low, projected_grad, 0, 0)
        output_term = dot(attn_grad_all, attended, 0, 0)
        gains_term = jnp.stack([gain_one_grad[0], gain_two_grad[0]], 1)
        gains_term = jnp.pad(gains_term, ((0, 0), (0, PAD - 2)))
        attn_term = jnp.concatenate([mixing_term, output_term, gains_term], 1).astype(narrow)
        attn_term = attn_term.reshape(groups, halves * rings, fsdp_rows, -1).transpose(1, 0, 2, 3)
        attn_total = lax.psum_scatter(attn_term, ("half", "ring"), scatter_dimension=0, tiled=False)
        attn_total = exchange_seq(attn_total).astype(single)
        back, _ = norm_back(scatter_seq(normed_part), inputs, gains_float[0])
        tokens_gradient = (hidden_grad + back)[None]

    def columns(first, width):
        return attn_total[:, :, first : first + width].transpose(1, 0, 2).reshape(fsdp_rows, -1)

    mixing_gradient = jnp.concatenate(
        [
            columns(0, q_width),
            columns(q_width, k_width),
            columns(q_width + k_width, k_width),
        ],
        1,
    )
    output_gradient = columns(mix_width, q_width)
    gains_gradient = jnp.sum(attn_total[:, :, mix_width + q_width :][:, :, :2], axis=0)

    return (
        layer_output,
        tokens_gradient,
        mixing_gradient,
        output_gradient,
        gains_gradient,
        gate_gradient,
        up_gradient,
        down_gradient,
        logits_rows[None],
    )


def solution(mesh):
    groups, shards = mesh.shape["seq"], mesh.shape["fsdp"]
    halves = 2 if (EXPERTS // groups) % 2 == 0 and (groups, shards) == (4, 8) else 1
    rings = shards // halves
    grid = Mesh(mesh.devices.reshape(groups, halves, rings), ("seq", "half", "ring"))
    fsdp = ("half", "ring")
    every = ("seq", "half", "ring")
    in_specs = (
        P(fsdp, "seq", None),
        P(every, None),
        P(every, None),
        P(every, None),
        P(fsdp, "seq", None),
        P(fsdp, "seq", None),
        P(fsdp, "seq", None),
        P(fsdp, None, None),
        P(fsdp, None, None),
        P(fsdp, None),
        P(fsdp, "seq", None),
    )
    out_specs = (
        P(fsdp, "seq", None),
        P(fsdp, "seq", None),
        P(every, None),
        P(every, None),
        P(every, None),
        P(fsdp, "seq", None),
        P(fsdp, "seq", None),
        P(fsdp, "seq", None),
        P(fsdp, "seq", None),
    )
    return jax.shard_map(
        functools.partial(local, halves, rings),
        mesh=grid,
        in_specs=in_specs,
        out_specs=out_specs,
        check_vma=False,
    )
```
